32 devices in a mesh: row: 8 (over z, y), col: 4 (over x, core).
Axes of the slice: x: 2, y: 2, z: 4, core: 2. Of those that a mesh axis runs over, the one named last changes fastest.
Arguments:
- front: float32 [8, 8, 128, 16, 4, 128], P(None, 'row', None, None, 'col'), as said below
- updates: float32 [2, 8, 8, 128, 12, 4, 128], P(None, None, 'row', None, None, 'col'), as said below
- maps: int32 [2, 48], replicated, may hold values from 0 to 63, as said below
Outputs:
- factor: float32 [8, 8, 128, 16, 4, 128], P(None, 'row', None, None, 'col')
The draws below stay inside these ranges and needn't reach their ends.
Inputs may be any that keep to these rules, and one draw needn't show every extreme that they name: maps[k, j] is strictly increasing in j, and maps[k, j] - j is the same within each aligned group of 4 blocks. For each child and each c, of the blocks j with j % 4 == c at most 6 have maps[k, j] % 4 equal to any one value, and exactly 6 do for some value. updates[k] is child k's symmetric update matrix with its row block i placed at parent row block maps[k, i]; parent row blocks that no block of child k maps to are zero. front is symmetric, and with the updates added every block that is factored is positive definite.
All inputs are finite; a program needn't handle non-finite values.
Results may differ from the reference program's by a relative error of at most 0.0003.
Values sent between devices are 32-bit elements; how exact they have to be, the bound alone decides.
A program may use at most 192 MiB of HBM per device.

```python
import jax
import jax.numpy as jnp
from jax import lax

BLK = 128
NF = 8192
NC = 6144
NP = 2
NBP = 64
NBC = 48
PR = 8
PC = 16
CC = 12
W = 512
N_ROW = 8
N_COL = 4


def symmetric(key, length):
    base_draw = jax.random.normal(key, (length, length), jnp.float32)
    return (base_draw + base_draw.T) * 0.70710678


def gram_part(key):
    columns = NP * W // 4
    factors = jax.random.randint(key, (NF, columns), -3, 4).astype(jnp.float32)
    spread = 4.0
    gram = jnp.dot(factors, factors.T, precision=lax.Precision.HIGHEST, preferred_element_type=jnp.float32)
    return gram * (16.0 * NF ** 0.5 / (spread * columns))


def child_map(key):
    groups = NBC // N_COL
    capacity = groups // 2
    subkeys = jax.random.split(key, 4)
    first_count = jax.random.randint(subkeys[0], (), 0, groups - capacity + 1)
    second = jax.random.randint(subkeys[1], (), 0, groups - capacity - first_count + 1)
    counts = jnp.stack([jnp.int32(capacity), first_count, second, groups - capacity - first_count - second])
    bounds = jnp.cumsum(counts)
    positions = jnp.arange(groups, dtype=jnp.int32)
    run_index = jnp.sum((positions[:, None] >= bounds[None, :3]).astype(jnp.int32), axis=1)
    residue_order = jax.random.permutation(subkeys[2], N_COL).astype(jnp.int32)
    residue = jnp.sum(jnp.where(run_index[:, None] == jnp.arange(N_COL, dtype=jnp.int32)[None, :], residue_order[None, :], 0), axis=1)
    previous = jnp.concatenate([jnp.zeros((1,), jnp.int32), residue[:-1]])
    increment = (residue - previous) % N_COL
    spare_groups = min(groups - 1, (NBP - NBC - N_COL * (N_COL - 1)) // N_COL)
    extras = jax.random.randint(subkeys[3], (groups,), 0, 2)
    extras = jnp.where((positions >= 1) & (positions <= spare_groups), extras, 0)
    offsets = jnp.cumsum(increment + N_COL * extras)
    blocks = jnp.arange(NBC, dtype=jnp.int32)
    return (blocks + jnp.repeat(offsets, N_COL)).astype(jnp.int32)


def make_maps(key):
    base_key = jax.random.fold_in(key, 7)
    return jnp.stack([child_map(jax.random.fold_in(base_key, 0)), child_map(jax.random.fold_in(base_key, 1))])


def draw_maps(key, part):
    return make_maps(key)


def draw_front(key, part):
    matrix = symmetric(jax.random.fold_in(key, 3), NF)
    diagonal = jax.random.uniform(jax.random.fold_in(key, 4), (NF,), jnp.float32, 4.0, 8.0) * NF ** 0.5
    diagonal_index = jnp.arange(NF)
    matrix = matrix.at[diagonal_index, diagonal_index].set(diagonal)
    matrix = matrix + gram_part(jax.random.fold_in(key, 5))
    return matrix.reshape(PR, N_ROW, BLK, PC, N_COL, BLK)


def draw_updates(key, part):
    parents = make_maps(key)
    stacked = []
    for member in range(2):
        values = symmetric(jax.random.fold_in(key, 20 + member), NC) * 0.7
        matches = parents[member][None, :] == jnp.arange(NBP, dtype=jnp.int32)[:, None]
        source = jnp.sum(jnp.where(matches, jnp.arange(NBC, dtype=jnp.int32)[None, :], 0), axis=1)
        present = jnp.any(matches, axis=1).astype(jnp.float32)
        placed = values.reshape(NBC, BLK, NC)[source] * present[:, None, None]
        stacked.append(placed.reshape(PR, N_ROW, BLK, CC, N_COL, BLK))
    return jnp.stack(stacked)


def setup_inputs(seed: int = 0) -> dict:
    splits = jax.random.split(jax.random.key(seed), 4)
    front = draw_front(jax.random.fold_in(splits[3], 71), 0)
    updates = draw_updates(jax.random.fold_in(splits[3], 71), 0)
    maps = draw_maps(jax.random.fold_in(splits[3], 71), 0)
    return dict(front=front, updates=updates, maps=maps)


highest = lax.Precision.HIGHEST

def extend(matrix, update, parent_of):
    row_total = matrix.shape[0]
    blocks = matrix.reshape(row_total, NBP, BLK)
    blocks = blocks.at[:, parent_of].add(update.reshape(row_total, NBC, BLK))
    return blocks.reshape(row_total, NF)

def reference(front, updates, maps):
    matrix = front.reshape(NF, NF)
    children = updates.reshape(2, NF, NC)
    for member in range(2):
        matrix = extend(matrix, children[member], maps[member])
    position = jnp.arange(NF, dtype=jnp.int32)
    for panel_index in range(NP):
        begin_at = panel_index * W
        finish = begin_at + W
        square = matrix[begin_at:finish, begin_at:finish]
        lower_factor = jnp.linalg.cholesky(square)
        inverse = lax.linalg.triangular_solve(lower_factor, jnp.eye(W, dtype=jnp.float32), left_side=True, lower=True)
        left_factor = jnp.dot(matrix[:, begin_at:finish].astype(jnp.float32), inverse.T.astype(jnp.float32), precision=highest, preferred_element_type=jnp.float32)
        right_factor = jnp.dot(inverse.astype(jnp.float32), matrix[begin_at:finish, :].astype(jnp.float32), precision=highest, preferred_element_type=jnp.float32)
        beyond = position >= finish
        trailing = jnp.dot(jnp.where(beyond[:, None], left_factor, 0.0).astype(jnp.float32), jnp.where(beyond[None, :], right_factor, 0.0).astype(jnp.float32), precision=highest, preferred_element_type=jnp.float32)
        matrix = matrix - trailing
        inside = (position >= begin_at) & (position < finish)
        diag_rows = lower_factor[jnp.clip(position - begin_at, 0, W - 1)]
        column_vals = jnp.where(beyond[:, None], left_factor, jnp.where(inside[:, None], diag_rows, 0.0))
        matrix = matrix.at[:, begin_at:finish].set(column_vals)
        matrix = jnp.where(inside[:, None] & beyond[None, :], 0.0, matrix)
    return matrix.reshape(front.shape)
```

```python
import functools

import jax
import jax.numpy as jnp
from jax import lax
from jax.experimental import pallas as pl
from jax.experimental.pallas import tpu as pltpu
from jax.sharding import PartitionSpec as P

NP = 2
highest = lax.Precision.HIGHEST
VMEM_LIMIT = 56 * 1024 * 1024
MESH = pl.DeviceIdType.MESH
FIRST = 4
LEVELS = ((12, 12, 12),)


def split(value):
    high = value.astype(jnp.bfloat16)
    low = (value - high.astype(jnp.float32)).astype(jnp.bfloat16)
    return high, low


def dims(transposed):
    return (((1,), (1 if transposed else 0,)), ((), ()))


def product3(left_pair, right_pair, transposed=False):
    def one(a, b):
        return lax.dot_general(a, b, dims(transposed), preferred_element_type=jnp.float32)

    return (
        one(left_pair[0], right_pair[0])
        + one(left_pair[0], right_pair[1])
        + one(left_pair[1], right_pair[0])
    )


def product(a, b, transposed=False):
    return lax.dot_general(
        a, b, dims(transposed), precision=highest, preferred_element_type=jnp.float32
    )


def pack_kernel(child_cols, cap, blk, table, updates_ref, one_ref, two_ref, three_ref):
    for turn, out_ref in enumerate((one_ref, two_ref, three_ref)):
        for member in range(2):
            for slot in range(cap):
                source = table[(turn + 1) * 2 * cap + member * cap + slot]
                out_ref[member * cap + slot] = updates_ref[
                    member, 0, pl.ds(source, blk, stride=child_cols), :
                ]


def pack(table, updates, cap, begin, count):
    part_rows, blk, child_cols = updates.shape[1], updates.shape[3], updates.shape[4]
    flat = updates.reshape(2, part_rows, blk * child_cols, blk)
    return pl.pallas_call(
        functools.partial(pack_kernel, child_cols, cap, blk),
        grid_spec=pltpu.PrefetchScalarGridSpec(
            num_scalar_prefetch=1,
            grid=(count,),
            in_specs=[
                pl.BlockSpec((2, 1, blk * child_cols, blk), lambda a, t: (0, a + begin, 0, 0))
            ],
            out_specs=[pl.BlockSpec((2 * cap, blk, blk), lambda a, t: (0, a, 0))] * 3,
        ),
        out_shape=[jax.ShapeDtypeStruct((2 * cap, count * blk, blk), jnp.float32)] * 3,
        compiler_params=pltpu.CompilerParams(vmem_limit_bytes=VMEM_LIMIT),
        name="pack",
    )(table, flat)


def add_children(out_ref, table, front_ref, updates_ref, received, slots, part_cols, child_cols, blk):
    for slot in slots:
        cols = slice(slot * blk, (slot + 1) * blk)
        out_ref[:, cols] = front_ref[0, pl.ds(slot, blk, stride=part_cols), :]
        for member in range(2):
            turn = table[(member * part_cols + slot) * 2]
            index = table[(member * part_cols + slot) * 2 + 1]

            @pl.when(turn == 0)
            def _():
                out_ref[:, cols] += updates_ref[member, 0, pl.ds(index, blk, stride=child_cols), :]

            for step in range(3):

                @pl.when(turn == step + 1)
                def _():
                    out_ref[:, cols] += received[step][index]


def assemble(table, front, updates, received, begin, count, width):
    part_rows, blk, part_cols = front.shape[0], front.shape[2], front.shape[3]
    child_cols = updates.shape[4]
    slots = received[0].shape[0]

    def kernel(table, front_ref, updates_ref, one, two, three, out_ref):
        add_children(
            out_ref, table, front_ref, updates_ref, (one, two, three),
            range(width), part_cols, child_cols, blk,
        )

    return pl.pallas_call(
        kernel,
        grid_spec=pltpu.PrefetchScalarGridSpec(
            num_scalar_prefetch=1,
            grid=(count,),
            in_specs=[
                pl.BlockSpec((1, blk * part_cols, blk), lambda a, t: (a + begin, 0, 0)),
                pl.BlockSpec((2, 1, blk * child_cols, blk), lambda a, t: (0, a + begin, 0, 0)),
            ]
            + [pl.BlockSpec((slots, blk, blk), lambda a, t: (0, a, 0))] * 3,
            out_specs=pl.BlockSpec((blk, width * blk), lambda a, t: (a, 0)),
        ),
        out_shape=jax.ShapeDtypeStruct((count * blk, width * blk), jnp.float32),
        compiler_params=pltpu.CompilerParams(vmem_limit_bytes=VMEM_LIMIT),
        name="assemble",
    )(
        table,
        front.reshape(part_rows, blk * part_cols, blk),
        updates.reshape(2, part_rows, blk * child_cols, blk),
        *received,
    )


def eliminate(block):
    size = block.shape[0]
    group = 8
    tiles = size // group
    shape = (group, size)
    row_ids = lax.broadcasted_iota(jnp.int32, (size, size), 0)
    col_ids = lax.broadcasted_iota(jnp.int32, (size, size), 1)
    local = lax.broadcasted_iota(jnp.int32, shape, 0)
    start = (row_ids == col_ids).astype(jnp.float32)
    upper = [block[group * t : group * (t + 1), :] for t in range(tiles)]
    solved = [start[group * t : group * (t + 1), :] for t in range(tiles)]
    for h in range(tiles):
        def column(t, j):
            return jnp.broadcast_to(upper[t][:, group * h + j : group * h + j + 1], shape)
        home = [column(h, j) for j in range(group)]
        pivot = {
            (i, j): jnp.broadcast_to(home[j][i : i + 1, :], shape)
            for j in range(group) for i in range(j, group)
        }
        scale, ratio = [], {}
        for j in range(group):
            scale.append(1.0 / pivot[j, j])
            for i in range(j + 1, group):
                ratio[i, j] = pivot[i, j] * scale[j]
            for k in range(j + 1, group):
                for i in range(k, group):
                    pivot[i, k] = pivot[i, k] - ratio[i, j] * pivot[k, j]
        upper_rows, solved_rows = [], []
        for j in range(group):
            u = jnp.broadcast_to(upper[h][j : j + 1, :], shape)
            s = jnp.broadcast_to(solved[h][j : j + 1, :], shape)
            for i in range(j):
                u = u - ratio[j, i] * upper_rows[i]
                s = s - ratio[j, i] * solved_rows[i]
            upper_rows.append(u)
            solved_rows.append(s)
        for t in range(h, tiles):
            if t == h:
                u, s = upper_rows[0], solved_rows[0]
                for j in range(1, group):
                    u = jnp.where(local == j, upper_rows[j], u)
                    s = jnp.where(local == j, solved_rows[j], s)
                upper[t], solved[t] = u, s
                continue
            factors = []
            for j in range(group):
                c = column(t, j)
                for i in range(j):
                    c = c - factors[i] * pivot[j, i]
                factors.append(c * scale[j])
            for j in range(group):
                upper[t] = upper[t] - factors[j] * upper_rows[j]
                solved[t] = solved[t] - factors[j] * solved_rows[j]
    upper = jnp.concatenate(upper, axis=0)
    solved = jnp.concatenate(solved, axis=0)
    diagonal = jnp.sum(jnp.where(row_ids == col_ids, upper, 0.0), axis=1, keepdims=True)
    scale = 1.0 / jnp.sqrt(diagonal)
    lower = jnp.where(col_ids >= row_ids, upper * scale, 0.0).T
    return lower, solved * scale

def factor_kernel(blk, square_ref, lower_ref, inverse_ref, work):
    size = square_ref.shape[0]
    count = size // blk
    work[...] = square_ref[...]
    lower_ref[...] = jnp.zeros_like(lower_ref)
    inverse_ref[...] = jnp.zeros_like(inverse_ref)

    def spread(k, diag_inverse):
        begin, end = k * blk, (k + 1) * blk
        here = slice(begin, end)
        inverse_pair = split(diag_inverse)
        if k:
            done = product3(inverse_pair, split(inverse_ref[here, :begin]))
            inverse_ref[here, :begin] = done
        inverse_ref[here, here] = diag_inverse
        if end == size:
            return
        row_high, row_low = split(inverse_ref[here, :end])
        left_high, left_low = [], []
        for q in range(end, size, 256):
            top = min(q + 256, size)
            left = product3(split(work[q:top, here]), inverse_pair, True)
            lower_ref[q:top, here] = left
            high, low = split(left)
            left_high.append(high)
            left_low.append(low)
        high = jnp.concatenate(left_high, axis=0)
        low = jnp.concatenate(left_low, axis=0)
        for q in range(end, size, 256):
            top = min(q + 256, size)
            pair = high[q - end : top - end], low[q - end : top - end]
            below = high[: top - end], low[: top - end]
            work[q:top, end:top] -= product3(pair, below, True)
            inverse_ref[q:top, :end] -= product3(pair, (row_high, row_low))

    def step(k, carry):
        begin = pl.multiple_of(k * blk, blk)
        here = pl.ds(begin, blk)
        diag_lower, diag_inverse = eliminate(work[here, here])
        lower_ref[here, here] = diag_lower
        for t in range(count):
            pl.when(k == t)(functools.partial(spread, t, diag_inverse))
        return carry

    lax.fori_loop(0, count, step, 0)


def factorize(square, blk):
    size = square.shape[0]
    shape = jax.ShapeDtypeStruct((size, size), jnp.float32)
    return pl.pallas_call(
        functools.partial(factor_kernel, blk),
        out_shape=[shape, shape],
        scratch_shapes=[pltpu.VMEM((size, size), jnp.float32)],
        compiler_params=pltpu.CompilerParams(vmem_limit_bytes=VMEM_LIMIT),
        cost_estimate=pl.CostEstimate(flops=size, bytes_accessed=size, transcendentals=0),
        name="factorize",
    )(square)


def right_kernel(inverse_ref, top_ref, high_ref, low_ref, inv_high, inv_low):
    @pl.when(pl.program_id(0) == 0)
    def _():
        inv_high[...], inv_low[...] = split(inverse_ref[...])

    result = product3((inv_high[...], inv_low[...]), split(top_ref[...]))
    high_ref[...], low_ref[...] = split(result)


def right_side(inverse, top, tile):
    size, cols = top.shape
    out = jax.ShapeDtypeStruct((size, cols), jnp.bfloat16)
    return pl.pallas_call(
        right_kernel,
        grid=(cols // tile,),
        in_specs=[
            pl.BlockSpec((size, size), lambda n: (0, 0)),
            pl.BlockSpec((size, tile), lambda n: (0, n)),
        ],
        out_specs=[pl.BlockSpec((size, tile), lambda n: (0, n))] * 2,
        out_shape=[out, out],
        scratch_shapes=[pltpu.VMEM((size, size), jnp.bfloat16)] * 2,
        compiler_params=pltpu.CompilerParams(vmem_limit_bytes=VMEM_LIMIT),
        name="right",
    )(inverse, top)


def finish_kernel(
    part_cols, child_cols, blk, row_count, col_count, first, table, place,
    panel_ref, front_ref, updates_ref, one, two, three, inverse_ref, lower_ref, high_ref, low_ref,
    out_ref, inv_high, inv_low, left_ref, sum_ref,
):
    step = pl.program_id(0)
    block_row = step * row_count + place[0]
    panel_blocks = NP * col_count
    inside = block_row < panel_blocks
    columns = [pl.multiple_of((s * col_count + place[1]) * blk, blk) for s in range(NP)]

    @pl.when(step == 0)
    def _():
        inv_high[...], inv_low[...] = split(inverse_ref[...])

    @pl.when(jnp.logical_not(inside))
    def _():
        add_children(
            sum_ref, table, front_ref, updates_ref, (one, two, three),
            range(NP, part_cols), part_cols, child_cols, blk,
        )
        panel = jnp.concatenate(
            [
                panel_ref[c, :, s * blk : (s + 1) * blk]
                for s in range(NP)
                for c in range(col_count)
            ],
            axis=1,
        )
        left_ref[...] = product3(split(panel), (inv_high[...], inv_low[...]), True)
        left_pair = split(left_ref[...])
        for pair in range(NP, part_cols, 2):
            cols = slice((pair - NP) * blk, (pair - NP + 2) * blk)
            trailing = product3(left_pair, (high_ref[:, cols], low_ref[:, cols]))
            updated = sum_ref[:, pair * blk : (pair + 2) * blk] - trailing
            for half in range(2):
                out_ref[0, pl.ds(pair + half, blk, stride=part_cols), :] = updated[
                    :, half * blk : (half + 1) * blk
                ]
        for s in range(NP):
            out_ref[0, pl.ds(s, blk, stride=part_cols), :] = left_ref[:, pl.ds(columns[s], blk)]

    @pl.when(inside)
    def _():
        out_ref[...] = jnp.zeros_like(out_ref)
        begin = pl.multiple_of(block_row * blk, blk)
        for s in range(NP):
            out_ref[0, pl.ds(s, blk, stride=part_cols), :] = lower_ref[
                pl.ds(begin, blk), pl.ds(columns[s], blk)
            ]


def finish(table, place, panel, front, updates, received, inverse, lower, high, low, row_count, first):
    part_rows, blk, part_cols = front.shape[0], front.shape[2], front.shape[3]
    child_cols = updates.shape[4]
    size = inverse.shape[0]
    slots = received[0].shape[0]
    col_count = panel.shape[0]

    def resident(shape):
        return pl.BlockSpec(shape, lambda a, t, p: (0, 0), pipeline_mode=pl.Buffered(1))

    def late(a, t, p):
        return (0, jnp.maximum(a - first, 0), 0)

    return pl.pallas_call(
        functools.partial(finish_kernel, part_cols, child_cols, blk, row_count, col_count, first),
        grid_spec=pltpu.PrefetchScalarGridSpec(
            num_scalar_prefetch=2,
            grid=(part_rows,),
            in_specs=[
                pl.BlockSpec((col_count, blk, NP * blk), late),
                pl.BlockSpec((1, blk * part_cols, blk), lambda a, t, p: (a, 0, 0)),
                pl.BlockSpec((2, 1, blk * child_cols, blk), lambda a, t, p: (0, a, 0, 0)),
            ]
            + [pl.BlockSpec((slots, blk, blk), late)] * 3
            + [
                resident((size, size)),
                resident((size, size)),
                resident(high.shape),
                resident(low.shape),
            ],
            out_specs=pl.BlockSpec((1, blk * part_cols, blk), lambda a, t, p: (a, 0, 0)),
            scratch_shapes=[
                pltpu.VMEM((size, size), jnp.bfloat16),
                pltpu.VMEM((size, size), jnp.bfloat16),
                pltpu.VMEM((blk, size), jnp.float32),
                pltpu.VMEM((blk, part_cols * blk), jnp.float32),
            ],
        ),
        out_shape=jax.ShapeDtypeStruct((part_rows, blk * part_cols, blk), jnp.float32),
        compiler_params=pltpu.CompilerParams(vmem_limit_bytes=VMEM_LIMIT),
        name="finish",
    )(
        table, place, panel,
        front.reshape(part_rows, blk * part_cols, blk),
        updates.reshape(2, part_rows, blk * child_cols, blk),
        *received, inverse, lower, high, low,
    )


def tables(maps, col_index, col_count, child_cols, part_cols, cap):
    offsets = maps[:, ::col_count] - col_count * jnp.arange(child_cols, dtype=jnp.int32)[None, :]
    turn = offsets % col_count
    groups = jnp.arange(child_cols, dtype=jnp.int32)
    same = (turn[:, :, None] == turn[:, None, :]) & (groups[None, None, :] < groups[None, :, None])
    rank = jnp.sum(same.astype(jnp.int32), axis=2)
    turns = jnp.arange(col_count, dtype=jnp.int32)
    slots = jnp.arange(cap, dtype=jnp.int32)
    hot = (turn[None, :, None, :] == turns[:, None, None, None]) & (
        rank[None, :, None, :] == slots[None, None, :, None]
    )
    send = jnp.sum(jnp.where(hot, groups[None, None, None, :], 0), axis=3).reshape(-1)
    parents = jnp.arange(part_cols, dtype=jnp.int32) * col_count + col_index
    match = maps[:, None, :] == parents[None, :, None]
    spread = jnp.repeat(groups, col_count)
    group = jnp.sum(jnp.where(match, spread[None, None, :], 0), axis=2)
    present = jnp.any(match, axis=2)
    pick = group[:, :, None] == groups[None, None, :]
    kind = jnp.sum(jnp.where(pick, turn[:, None, :], 0), axis=2)
    order = jnp.sum(jnp.where(pick, rank[:, None, :], 0), axis=2)
    order = jnp.where(kind == 0, group, order + cap * jnp.arange(2, dtype=jnp.int32)[:, None])
    kind = jnp.where(present, kind, col_count)
    place = jnp.stack([kind, order], axis=2).reshape(-1)
    return send, place


def gather_top(piece, row_count, row_index, panel_blocks):
    if row_count == panel_blocks:
        return lax.all_gather(piece, "row", axis=0, tiled=True)
    ids = jnp.arange(panel_blocks, dtype=jnp.int32)
    kept = jnp.where((ids == row_index)[:, None, None], piece[None], 0.0)
    return lax.psum(kept, "row").reshape(panel_blocks * piece.shape[0], piece.shape[1])


def simple_body(front, updates, maps):
    row_count = lax.axis_size("row")
    col_count = lax.axis_size("col")
    row_index = lax.axis_index("row")
    col_index = lax.axis_index("col")
    front = front.reshape(front.shape[0], 1, *front.shape[2:4], front.shape[5])
    blk, part_cols = front.shape[2], front.shape[3]
    child_cols = updates.shape[4]
    cap = child_cols // 2
    panel_blocks = NP * col_count
    send, place = tables(maps, col_index, col_count, child_cols, part_cols, cap)
    part_rows = front.shape[0]
    first = 1 if part_rows > 1 and row_count == panel_blocks else part_rows

    def exchange(outgoing):
        return [
            lax.ppermute(
                outgoing[turn - 1], "col", [(c, (c + turn) % col_count) for c in range(col_count)]
            )
            for turn in range(1, col_count)
        ]

    early = exchange(pack(send, updates, cap, 0, first))
    if first < part_rows:
        outgoing = pack(send, updates, cap, first, part_rows - first)
        early, outgoing = lax.optimization_barrier((early, outgoing))
        received = exchange(outgoing)
    else:
        received = early
    head = assemble(place, front, updates, early, 0, 1, part_cols)
    square = jnp.concatenate(
        [
            lax.all_gather(head[:, s * blk : (s + 1) * blk], "col", axis=1, tiled=True)
            for s in range(NP)
        ],
        axis=1,
    )
    square = gather_top(square, row_count, row_index, panel_blocks)
    rest, square = lax.optimization_barrier((head[:, NP * blk :], square))
    top = gather_top(rest, row_count, row_index, panel_blocks)
    lower, inverse = factorize(square, blk)
    high, low = right_side(inverse, top, 2 * blk)
    received, high, low = lax.optimization_barrier((received, high, low))
    late = first if first < part_rows else 0
    panel = assemble(place, front, updates, received, late, part_rows - late, NP)
    panel = lax.all_gather(panel, "col", axis=0)
    where = jnp.stack([row_index, col_index]).astype(jnp.int32)
    result = finish(
        place, where, panel, front, updates, received, inverse, lower, high, low, row_count, late
    )
    return result.reshape(front.shape[0], 1, blk, part_cols, 1, blk)


def square_kernel(
    blk, row_count, table, front_ref, updates_ref, square_ref,
    work, front_part, updates_part, units, local, line_send, line_recv,
    col_send, col_recv, core_send, core_recv,
):
    row, col = lax.axis_index("row"), lax.axis_index("col")
    part_cols = front_part.shape[0] // blk
    child_cols = updates_part.shape[1] // blk
    width = units.shape[0] // 4
    half = row_count // 2
    core = lax.rem(col, 2)
    other_core = col + 1 - 2 * core
    other_chip = lax.rem(col + 2, 4)
    loads = [pltpu.make_async_copy(front_ref.at[0], front_part, local.at[0])]
    for member in range(2):
        loads.append(
            pltpu.make_async_copy(
                updates_ref.at[member, 0], updates_part.at[member], local.at[1 + member]
            )
        )
    for load in loads:
        load.start()

    def ring_row(position):
        position = lax.rem(position + row_count, row_count)
        return jnp.where(position < half, 2 * position, 2 * (row_count - position) - 1)

    place = jnp.where(lax.rem(row, 2) == 0, row // 2, row_count - 1 - row // 2)
    right, left = ring_row(place + 1), ring_row(place - 1)
    barrier = pltpu.get_barrier_semaphore()
    for device in ((row, other_core), (row, other_chip), (right, col), (left, col)):
        pl.semaphore_signal(barrier, inc=1, device_id=device, device_id_type=MESH)
    for load in loads:
        load.wait()
    mine = col * width
    for member in range(2):
        for g in range(2):
            units[mine + member * 2 + g] = updates_part[member, pl.ds(g, blk, stride=child_cols), :]
    for s in range(NP):
        units[mine + 4 + s] = front_part[pl.ds(s, blk, stride=part_cols), :]
    pl.semaphore_wait(barrier, 4)

    def share(owner, device, index):
        part = units.at[pl.ds(owner * width, width)]
        return pltpu.make_async_remote_copy(
            src_ref=part, dst_ref=part, send_sem=col_send.at[index], recv_sem=col_recv.at[index],
            device_id=(row, device), device_id_type=MESH,
        )

    across = share(col, other_chip, 0)
    beside = share(col, other_core, 1)
    across.start()
    beside.start()
    share(other_chip, other_chip, 0).wait_recv()
    passed = share(other_chip, other_core, 2)
    passed.start()
    share(other_core, other_core, 1).wait_recv()
    share(lax.rem(other_core + 2, 4), other_core, 2).wait_recv()
    here = pl.multiple_of(row * blk, blk)
    for q in range(row_count):
        s, owner = q // 4, q % 4
        total = units[owner * width + 4 + s]
        for member in range(2):
            entry = 2 * (member * row_count + q)
            total = total + units[table[entry]] * table[entry + 1].astype(jnp.float32)
        work[pl.ds(here, blk), q * blk : (q + 1) * blk] = total

    cols = work.shape[1] // 2

    def part(position, side):
        begin = pl.multiple_of(ring_row(position) * blk, blk)
        return work.at[pl.ds(begin, blk), pl.ds(pl.multiple_of(side * cols, cols), cols)]

    def copy(ref, device, send, recv):
        return pltpu.make_async_remote_copy(
            src_ref=ref, dst_ref=ref, send_sem=send, recv_sem=recv,
            device_id=device, device_id_type=MESH,
        )

    pending = []
    for step in range(half):
        ways = range(2 if step < half - 1 else 1)
        for way in ways:
            position = place - step if way == 0 else place + step
            target = right if way == 0 else left
            move = copy(
                part(position, core), (target, col), line_send.at[way, step], line_recv.at[way, step]
            )
            move.start()
            pending.append(move)
        for way in ways:
            origin = place - step - 1 if way == 0 else place + step + 1
            landed = part(origin, core)
            copy(
                landed, (right, col), line_send.at[way, step], line_recv.at[way, step]
            ).wait_recv()
            forward = copy(
                landed, (row, other_core), core_send.at[way, step], core_recv.at[way, step]
            )
            forward.start()
            pending.append(forward)
    for way in range(2):
        for step in range(half - way):
            origin = place - step - 1 if way == 0 else place + step + 1
            copy(
                part(origin, 1 - core), (row, other_core),
                core_send.at[way, step], core_recv.at[way, step],
            ).wait_recv()
    store = pltpu.make_async_copy(work, square_ref, local.at[0])
    store.start()
    for move in [across, beside, passed] + pending:
        move.wait_send()
    store.wait()


def gather_square(table, front, updates, row_count):
    part_rows, blk, part_cols = front.shape[0], front.shape[2], front.shape[3]
    child_cols = updates.shape[4]
    size = row_count * blk
    half = row_count // 2
    anywhere = pl.BlockSpec(memory_space=pl.ANY)
    return pl.pallas_call(
        functools.partial(square_kernel, blk, row_count),
        in_specs=[pl.BlockSpec(memory_space=pltpu.SMEM), anywhere, anywhere],
        out_specs=anywhere,
        out_shape=jax.ShapeDtypeStruct((size, size), jnp.float32),
        scratch_shapes=[
            pltpu.VMEM((size, size), jnp.float32),
            pltpu.VMEM((blk * part_cols, blk), jnp.float32),
            pltpu.VMEM((2, blk * child_cols, blk), jnp.float32),
            pltpu.VMEM((4 * (4 + NP), blk, blk), jnp.float32),
            pltpu.SemaphoreType.DMA((3,)),
            pltpu.SemaphoreType.DMA((2, half)),
            pltpu.SemaphoreType.DMA((2, half)),
            pltpu.SemaphoreType.DMA((3,)),
            pltpu.SemaphoreType.DMA((3,)),
            pltpu.SemaphoreType.DMA((2, half)),
            pltpu.SemaphoreType.DMA((2, half)),
        ],
        compiler_params=pltpu.CompilerParams(
            vmem_limit_bytes=VMEM_LIMIT, collective_id=0, has_side_effects=True
        ),
        cost_estimate=pl.CostEstimate(flops=20_000_000_000, bytes_accessed=size, transcendentals=0),
        name="square",
    )(
        table,
        front.reshape(part_rows, blk * part_cols, blk),
        updates.reshape(2, part_rows, blk * child_cols, blk),
    )


def pack_turns_kernel(caps, most, child_cols, blk, table, updates_ref, *outs):
    step = pl.program_id(0)

    def unit(turn, slot):
        entry = (turn * most + slot) * 2
        return updates_ref[table[entry], 0, pl.ds(table[entry + 1], blk, stride=child_cols), :]

    @pl.when(step == 0)
    def _():
        for turn, cap in enumerate(caps):
            for slot in range(cap):
                outs[turn][slot] = unit(turn, slot)

    @pl.when(step > 0)
    def _():
        for turn, cap in enumerate(caps):
            for slot in range(cap):
                if slot < FIRST:
                    outs[3 + turn][slot] = unit(turn, slot)
                else:
                    outs[6 + turn][slot - FIRST] = unit(turn, slot)


def pack_turns(table, updates, caps, most):
    part_rows, blk, child_cols = updates.shape[1], updates.shape[3], updates.shape[4]
    flat = updates.reshape(2, part_rows, blk * child_cols, blk)
    sizes = [(cap, 1) for cap in caps]
    sizes += [(FIRST, part_rows - 1)] * 3 + [(cap - FIRST, part_rows - 1) for cap in caps]

    def late(a, t):
        return (0, jnp.maximum(a - 1, 0), 0)

    outs = pl.pallas_call(
        functools.partial(pack_turns_kernel, caps, most, child_cols, blk),
        grid_spec=pltpu.PrefetchScalarGridSpec(
            num_scalar_prefetch=1,
            grid=(part_rows,),
            in_specs=[pl.BlockSpec((2, 1, blk * child_cols, blk), lambda a, t: (0, a, 0, 0))],
            out_specs=[
                pl.BlockSpec((count, blk, blk), late if rows > 1 else lambda a, t: (0, 0, 0))
                for count, rows in sizes
            ],
        ),
        out_shape=[
            jax.ShapeDtypeStruct((count, rows * blk, blk), jnp.float32) for count, rows in sizes
        ],
        compiler_params=pltpu.CompilerParams(vmem_limit_bytes=VMEM_LIMIT),
        name="pack",
    )(table, flat)
    return outs[:3], outs[3:6], outs[6:]


def add_units(out_ref, table, front_ref, updates_ref, received, slots, base, part_cols, child_cols, blk):
    for slot in slots:
        cols = slice((slot - base) * blk, (slot - base + 1) * blk)
        out_ref[:, cols] = front_ref[0, pl.ds(slot, blk, stride=part_cols), :]
        for member in range(2):
            turn = table[(member * part_cols + slot) * 2]
            index = table[(member * part_cols + slot) * 2 + 1]

            @pl.when(turn == 0)
            def _():
                out_ref[:, cols] += updates_ref[member, 0, pl.ds(index, blk, stride=child_cols), :]

            for step, ref in enumerate(received):

                @pl.when((turn == step + 1) & (index < ref.shape[0]))
                def _():
                    out_ref[:, cols] += ref[index]


def assemble_part(table, front, updates, received, begin, count, slots):
    part_rows, blk, part_cols = front.shape[0], front.shape[2], front.shape[3]
    child_cols = updates.shape[4]
    width = len(slots)

    def kernel(table, front_ref, updates_ref, one, two, three, out_ref):
        add_units(
            out_ref, table, front_ref, updates_ref, (one, two, three),
            slots, slots[0], part_cols, child_cols, blk,
        )

    return pl.pallas_call(
        kernel,
        grid_spec=pltpu.PrefetchScalarGridSpec(
            num_scalar_prefetch=1,
            grid=(count,),
            in_specs=[
                pl.BlockSpec((1, blk * part_cols, blk), lambda a, t: (a + begin, 0, 0)),
                pl.BlockSpec((2, 1, blk * child_cols, blk), lambda a, t: (0, a + begin, 0, 0)),
            ]
            + [pl.BlockSpec((r.shape[0], blk, blk), lambda a, t: (0, a, 0)) for r in received],
            out_specs=pl.BlockSpec((blk, width * blk), lambda a, t: (a, 0)),
        ),
        out_shape=jax.ShapeDtypeStruct((count * blk, width * blk), jnp.float32),
        compiler_params=pltpu.CompilerParams(vmem_limit_bytes=VMEM_LIMIT),
        name="assemble",
    )(
        table,
        front.reshape(part_rows, blk * part_cols, blk),
        updates.reshape(2, part_rows, blk * child_cols, blk),
        *received,
    )


def update_kernel(
    part_cols, child_cols, blk, row_count, col_count, table, place,
    panel_ref, front_ref, updates_ref, one, two, three, inverse_ref, lower_ref, high_ref, low_ref,
    out_ref, inv_high, inv_low, left_ref, sum_ref,
):
    step = pl.program_id(0)
    columns = [pl.multiple_of((s * col_count + place[1]) * blk, blk) for s in range(NP)]

    @pl.when(step == 0)
    def _():
        inv_high[...], inv_low[...] = split(inverse_ref[...])
        out_ref[...] = jnp.zeros_like(out_ref)
        begin = pl.multiple_of(place[0] * blk, blk)
        for s in range(NP):
            out_ref[0, pl.ds(s, blk, stride=part_cols), :] = lower_ref[
                pl.ds(begin, blk), pl.ds(columns[s], blk)
            ]

    @pl.when(step > 0)
    def _():
        add_units(
            sum_ref, table, front_ref, updates_ref, (one, two, three),
            range(NP, part_cols), 0, part_cols, child_cols, blk,
        )
        panel = jnp.concatenate(
            [
                panel_ref[c, :, s * blk : (s + 1) * blk]
                for s in range(NP)
                for c in range(col_count)
            ],
            axis=1,
        )
        left_ref[...] = product3(split(panel), (inv_high[...], inv_low[...]), True)
        left_pair = split(left_ref[...])
        for pair in range(NP, part_cols, 2):
            cols = slice((pair - NP) * blk, (pair - NP + 2) * blk)
            trailing = product3(left_pair, (high_ref[:, cols], low_ref[:, cols]))
            updated = sum_ref[:, pair * blk : (pair + 2) * blk] - trailing
            for half in range(2):
                out_ref[0, pl.ds(pair + half, blk, stride=part_cols), :] = updated[
                    :, half * blk : (half + 1) * blk
                ]
        for s in range(NP):
            out_ref[0, pl.ds(s, blk, stride=part_cols), :] = left_ref[:, pl.ds(columns[s], blk)]


def update(table, place, panel, front, updates, received, inverse, lower, high, low, row_count):
    part_rows, blk, part_cols = front.shape[0], front.shape[2], front.shape[3]
    child_cols = updates.shape[4]
    size = inverse.shape[0]
    col_count = panel.shape[0]

    def resident(shape):
        return pl.BlockSpec(shape, lambda a, t, p: (0, 0), pipeline_mode=pl.Buffered(1))

    def late(a, t, p):
        return (0, jnp.maximum(a - 1, 0), 0)

    return pl.pallas_call(
        functools.partial(update_kernel, part_cols, child_cols, blk, row_count, col_count),
        grid_spec=pltpu.PrefetchScalarGridSpec(
            num_scalar_prefetch=2,
            grid=(part_rows,),
            in_specs=[
                pl.BlockSpec((col_count, blk, NP * blk), late),
                pl.BlockSpec((1, blk * part_cols, blk), lambda a, t, p: (a, 0, 0)),
                pl.BlockSpec((2, 1, blk * child_cols, blk), lambda a, t, p: (0, a, 0, 0)),
            ]
            + [pl.BlockSpec((r.shape[0], blk, blk), late) for r in received]
            + [
                resident((size, size)),
                resident((size, size)),
                resident(high.shape),
                resident(low.shape),
            ],
            out_specs=pl.BlockSpec((1, blk * part_cols, blk), lambda a, t, p: (a, 0, 0)),
            scratch_shapes=[
                pltpu.VMEM((size, size), jnp.bfloat16),
                pltpu.VMEM((size, size), jnp.bfloat16),
                pltpu.VMEM((blk, size), jnp.float32),
                pltpu.VMEM((blk, part_cols * blk), jnp.float32),
            ],
        ),
        out_shape=jax.ShapeDtypeStruct((part_rows, blk * part_cols, blk), jnp.float32),
        compiler_params=pltpu.CompilerParams(vmem_limit_bytes=VMEM_LIMIT),
        name="update",
    )(
        table, place, panel,
        front.reshape(part_rows, blk * part_cols, blk),
        updates.reshape(2, part_rows, blk * child_cols, blk),
        *received, inverse, lower, high, low,
    )


def add_last_kernel(part_cols, blk, table, given_ref, one, two, three, out_ref):
    out_ref[...] = given_ref[...]
    for slot in range(NP, part_cols):
        for member in range(2):
            turn = table[(member * part_cols + slot) * 2]
            index = table[(member * part_cols + slot) * 2 + 1] - FIRST
            for step, ref in enumerate((one, two, three)):

                @pl.when((turn == step + 1) & (index >= 0))
                def _():
                    out_ref[0, pl.ds(slot, blk, stride=part_cols), :] += ref[index]


def add_last(table, given, received, part_cols, blk):
    part_rows = given.shape[0]
    block = pl.BlockSpec((1, blk * part_cols, blk), lambda a, t: (a + 1, 0, 0))
    return pl.pallas_call(
        functools.partial(add_last_kernel, part_cols, blk),
        grid_spec=pltpu.PrefetchScalarGridSpec(
            num_scalar_prefetch=1,
            grid=(part_rows - 1,),
            in_specs=[block]
            + [pl.BlockSpec((r.shape[0], blk, blk), lambda a, t: (0, a, 0)) for r in received],
            out_specs=block,
        ),
        out_shape=jax.ShapeDtypeStruct(given.shape, given.dtype),
        input_output_aliases={1: 0},
        compiler_params=pltpu.CompilerParams(vmem_limit_bytes=VMEM_LIMIT),
        name="add_last",
    )(table, given, *received)


def turn_tables(maps, col_index, col_count, child_cols, part_cols, most, panel_blocks):
    groups = jnp.arange(child_cols, dtype=jnp.int32)
    turn = (maps[:, ::col_count] - col_count * groups[None, :]) % col_count
    flat = turn.T.reshape(-1)
    order = jnp.arange(2 * child_cols, dtype=jnp.int32)
    same = (flat[:, None] == flat[None, :]) & (order[None, :] < order[:, None])
    rank = jnp.sum(same.astype(jnp.int32), axis=1)
    turns = jnp.arange(1, col_count, dtype=jnp.int32)
    counts = jnp.sum((flat[None, :] == turns[:, None]).astype(jnp.int32), axis=1)
    slots = jnp.arange(most, dtype=jnp.int32)
    hot = (flat[None, None, :] == turns[:, None, None]) & (
        rank[None, None, :] == slots[None, :, None]
    )
    chosen = jnp.sum(jnp.where(hot, order[None, None, :], 0), axis=2)
    send = jnp.stack([chosen % 2, chosen // 2], axis=2).reshape(-1)
    rank = rank.reshape(child_cols, 2).T
    spread = jnp.repeat(groups, col_count)

    def look(parents):
        match = maps[:, None, :] == parents[None, :, None]
        group = jnp.sum(jnp.where(match, spread[None, None, :], 0), axis=2)
        source = jnp.sum(
            jnp.where(match, jnp.arange(maps.shape[1], dtype=jnp.int32)[None, None, :], 0), axis=2
        )
        return jnp.any(match, axis=2), group, source

    present, group, _ = look(jnp.arange(part_cols, dtype=jnp.int32) * col_count + col_index)
    pick = group[:, :, None] == groups[None, None, :]
    kind = jnp.sum(jnp.where(pick, turn[:, None, :], 0), axis=2)
    index = jnp.sum(jnp.where(pick, rank[:, None, :], 0), axis=2)
    index = jnp.where(kind == 0, group, index)
    kind = jnp.where(present, kind, col_count)
    place = jnp.stack([kind, index], axis=2).reshape(-1)
    present, group, source = look(jnp.arange(panel_blocks, dtype=jnp.int32))
    group = jnp.minimum(group, 1)
    unit = (source % col_count) * (4 + NP) + 2 * jnp.arange(2, dtype=jnp.int32)[:, None] + group
    square = jnp.stack([unit, present.astype(jnp.int32)], axis=2).reshape(-1)
    return send, place, square, counts


def main_branch(caps, most, row_count, front, updates, send, place, square_table, where):
    blk, part_cols = front.shape[2], front.shape[3]
    part_rows = front.shape[0]
    col_count = 4

    def exchange(outgoing):
        return [
            lax.ppermute(
                outgoing[turn - 1], "col", [(c, (c + turn) % col_count) for c in range(col_count)]
            )
            for turn in range(1, col_count)
        ]

    early, first, last = pack_turns(send, updates, caps, most)
    early, first, last = exchange(early), exchange(first), exchange(last)
    square = gather_square(square_table, front, updates, row_count)
    top = assemble_part(place, front, updates, early, 0, 1, range(NP, part_cols))
    top = lax.all_gather(top, "row", axis=0, tiled=True)
    lower, inverse = factorize(square, blk)
    panel = assemble_part(place, front, updates, first, 1, part_rows - 1, range(NP))
    panel = lax.all_gather(panel, "col", axis=0)
    high, low = right_side(inverse, top, 2 * blk)
    result = update(
        place, where, panel, front, updates, first, inverse, lower, high, low, row_count
    )
    return add_last(place, result, last, part_cols, blk)


def body(row_count, col_count, front, updates, maps):
    part_rows = front.shape[0]
    if part_rows == 1 or row_count != NP * col_count or col_count != 4:
        return simple_body(front, updates, maps)
    row_index = lax.axis_index("row")
    col_index = lax.axis_index("col")
    front = front.reshape(front.shape[0], 1, *front.shape[2:4], front.shape[5])
    blk, part_cols = front.shape[2], front.shape[3]
    child_cols = updates.shape[4]
    most = child_cols
    send, place, square_table, counts = turn_tables(
        maps, col_index, col_count, child_cols, part_cols, most, row_count
    )
    where = jnp.stack([row_index, col_index]).astype(jnp.int32)
    branches = [functools.partial(main_branch, caps, most, row_count) for caps in LEVELS]
    fits = jnp.all(counts[None, :] <= jnp.asarray(LEVELS, jnp.int32), axis=1)
    level = jnp.argmax(fits).astype(jnp.int32)
    operands = (front, updates, send, place, square_table, where)
    if len(branches) == 1:
        result = branches[0](*operands)
    else:
        result = lax.switch(level, branches, *operands)
    return result.reshape(part_rows, 1, blk, part_cols, 1, blk)


def solution(mesh):
    return jax.shard_map(
        functools.partial(body, mesh.shape["row"], mesh.shape["col"]),
        mesh=mesh,
        in_specs=(
            P(None, "row", None, None, "col", None),
            P(None, None, "row", None, None, "col", None),
            P(),
        ),
        out_specs=P(None, "row", None, None, "col", None),
        check_vma=False,
    )
```

```python
import functools

import jax
import jax.numpy as jnp
from jax import lax
from jax.experimental import pallas as pl
from jax.experimental.pallas import tpu as pltpu
from jax.sharding import PartitionSpec as P

NP = 2
highest = lax.Precision.HIGHEST
VMEM_LIMIT = 56 * 1024 * 1024
MESH = pl.DeviceIdType.MESH
SHARED = 5
LEVELS = ((12, 12, 12),)


def split(value):
    high = value.astype(jnp.bfloat16)
    low = (value - high.astype(jnp.float32)).astype(jnp.bfloat16)
    return high, low


def dims(transposed):
    return (((1,), (1 if transposed else 0,)), ((), ()))


def product3(left_pair, right_pair, transposed=False):
    def one(a, b):
        return lax.dot_general(a, b, dims(transposed), preferred_element_type=jnp.float32)

    return (
        one(left_pair[0], right_pair[0])
        + one(left_pair[0], right_pair[1])
        + one(left_pair[1], right_pair[0])
    )


def product(a, b, transposed=False):
    return lax.dot_general(
        a, b, dims(transposed), precision=highest, preferred_element_type=jnp.float32
    )


def pack_kernel(child_cols, cap, blk, table, updates_ref, one_ref, two_ref, three_ref):
    for turn, out_ref in enumerate((one_ref, two_ref, three_ref)):
        for member in range(2):
            for slot in range(cap):
                source = table[(turn + 1) * 2 * cap + member * cap + slot]
                out_ref[member * cap + slot] = updates_ref[
                    member, 0, pl.ds(source, blk, stride=child_cols), :
                ]


def pack(table, updates, cap, begin, count):
    part_rows, blk, child_cols = updates.shape[1], updates.shape[3], updates.shape[4]
    flat = updates.reshape(2, part_rows, blk * child_cols, blk)
    return pl.pallas_call(
        functools.partial(pack_kernel, child_cols, cap, blk),
        grid_spec=pltpu.PrefetchScalarGridSpec(
            num_scalar_prefetch=1,
            grid=(count,),
            in_specs=[
                pl.BlockSpec((2, 1, blk * child_cols, blk), lambda a, t: (0, a + begin, 0, 0))
            ],
            out_specs=[pl.BlockSpec((2 * cap, blk, blk), lambda a, t: (0, a, 0))] * 3,
        ),
        out_shape=[jax.ShapeDtypeStruct((2 * cap, count * blk, blk), jnp.float32)] * 3,
        compiler_params=pltpu.CompilerParams(vmem_limit_bytes=VMEM_LIMIT),
        name="pack",
    )(table, flat)


def add_children(out_ref, table, front_ref, updates_ref, received, slots, part_cols, child_cols, blk):
    for slot in slots:
        cols = slice(slot * blk, (slot + 1) * blk)
        out_ref[:, cols] = front_ref[0, pl.ds(slot, blk, stride=part_cols), :]
        for member in range(2):
            turn = table[(member * part_cols + slot) * 2]
            index = table[(member * part_cols + slot) * 2 + 1]

            @pl.when(turn == 0)
            def _():
                out_ref[:, cols] += updates_ref[member, 0, pl.ds(index, blk, stride=child_cols), :]

            for step in range(3):

                @pl.when(turn == step + 1)
                def _():
                    out_ref[:, cols] += received[step][index]


def assemble(table, front, updates, received, begin, count, width):
    part_rows, blk, part_cols = front.shape[0], front.shape[2], front.shape[3]
    child_cols = updates.shape[4]
    slots = received[0].shape[0]

    def kernel(table, front_ref, updates_ref, one, two, three, out_ref):
        add_children(
            out_ref, table, front_ref, updates_ref, (one, two, three),
            range(width), part_cols, child_cols, blk,
        )

    return pl.pallas_call(
        kernel,
        grid_spec=pltpu.PrefetchScalarGridSpec(
            num_scalar_prefetch=1,
            grid=(count,),
            in_specs=[
                pl.BlockSpec((1, blk * part_cols, blk), lambda a, t: (a + begin, 0, 0)),
                pl.BlockSpec((2, 1, blk * child_cols, blk), lambda a, t: (0, a + begin, 0, 0)),
            ]
            + [pl.BlockSpec((slots, blk, blk), lambda a, t: (0, a, 0))] * 3,
            out_specs=pl.BlockSpec((blk, width * blk), lambda a, t: (a, 0)),
        ),
        out_shape=jax.ShapeDtypeStruct((count * blk, width * blk), jnp.float32),
        compiler_params=pltpu.CompilerParams(vmem_limit_bytes=VMEM_LIMIT),
        name="assemble",
    )(
        table,
        front.reshape(part_rows, blk * part_cols, blk),
        updates.reshape(2, part_rows, blk * child_cols, blk),
        *received,
    )


def eliminate(block):
    size = block.shape[0]
    group = 8
    tiles = size // group
    shape = (group, size)
    row_ids = lax.broadcasted_iota(jnp.int32, (size, size), 0)
    col_ids = lax.broadcasted_iota(jnp.int32, (size, size), 1)
    local = lax.broadcasted_iota(jnp.int32, shape, 0)
    start = (row_ids == col_ids).astype(jnp.float32)
    upper = [block[group * t : group * (t + 1), :] for t in range(tiles)]
    solved = [start[group * t : group * (t + 1), :] for t in range(tiles)]
    for h in range(tiles):
        def column(t, j):
            return jnp.broadcast_to(upper[t][:, group * h + j : group * h + j + 1], shape)
        home = [column(h, j) for j in range(group)]
        pivot = {
            (i, j): jnp.broadcast_to(home[j][i : i + 1, :], shape)
            for j in range(group) for i in range(j, group)
        }
        scale, ratio = [], {}
        for j in range(group):
            scale.append(1.0 / pivot[j, j])
            for i in range(j + 1, group):
                ratio[i, j] = pivot[i, j] * scale[j]
            for k in range(j + 1, group):
                for i in range(k, group):
                    pivot[i, k] = pivot[i, k] - ratio[i, j] * pivot[k, j]
        upper_rows, solved_rows = [], []
        for j in range(group):
            u = jnp.broadcast_to(upper[h][j : j + 1, :], shape)
            s = jnp.broadcast_to(solved[h][j : j + 1, :], shape)
            for i in range(j):
                u = u - ratio[j, i] * upper_rows[i]
                s = s - ratio[j, i] * solved_rows[i]
            upper_rows.append(u)
            solved_rows.append(s)
        for t in range(h, tiles):
            if t == h:
                u, s = upper_rows[0], solved_rows[0]
                for j in range(1, group):
                    u = jnp.where(local == j, upper_rows[j], u)
                    s = jnp.where(local == j, solved_rows[j], s)
                upper[t], solved[t] = u, s
                continue
            factors = []
            for j in range(group):
                c = column(t, j)
                for i in range(j):
                    c = c - factors[i] * pivot[j, i]
                factors.append(c * scale[j])
            for j in range(group):
                upper[t] = upper[t] - factors[j] * upper_rows[j]
                solved[t] = solved[t] - factors[j] * solved_rows[j]
    upper = jnp.concatenate(upper, axis=0)
    solved = jnp.concatenate(solved, axis=0)
    diagonal = jnp.sum(jnp.where(row_ids == col_ids, upper, 0.0), axis=1, keepdims=True)
    scale = 1.0 / jnp.sqrt(diagonal)
    lower = jnp.where(col_ids >= row_ids, upper * scale, 0.0).T
    return lower, solved * scale

def factor_kernel(blk, square_ref, lower_ref, inverse_ref, work):
    size = square_ref.shape[0]
    count = size // blk
    work[...] = square_ref[...]
    lower_ref[...] = jnp.zeros_like(lower_ref)
    inverse_ref[...] = jnp.zeros_like(inverse_ref)

    def spread(k, diag_inverse):
        begin, end = k * blk, (k + 1) * blk
        here = slice(begin, end)
        inverse_pair = split(diag_inverse)
        if k:
            done = product3(inverse_pair, split(inverse_ref[here, :begin]))
            inverse_ref[here, :begin] = done
        inverse_ref[here, here] = diag_inverse
        if end == size:
            return
        row_high, row_low = split(inverse_ref[here, :end])
        left_high, left_low = [], []
        for q in range(end, size, 256):
            top = min(q + 256, size)
            left = product3(split(work[q:top, here]), inverse_pair, True)
            lower_ref[q:top, here] = left
            high, low = split(left)
            left_high.append(high)
            left_low.append(low)
        high = jnp.concatenate(left_high, axis=0)
        low = jnp.concatenate(left_low, axis=0)
        for q in range(end, size, 256):
            top = min(q + 256, size)
            pair = high[q - end : top - end], low[q - end : top - end]
            below = high[: top - end], low[: top - end]
            work[q:top, end:top] -= product3(pair, below, True)
            inverse_ref[q:top, :end] -= product3(pair, (row_high, row_low))

    def step(k, carry):
        begin = pl.multiple_of(k * blk, blk)
        here = pl.ds(begin, blk)
        diag_lower, diag_inverse = eliminate(work[here, here])
        lower_ref[here, here] = diag_lower
        for t in range(count):
            pl.when(k == t)(functools.partial(spread, t, diag_inverse))
        return carry

    lax.fori_loop(0, count, step, 0)


def factorize(square, blk):
    size = square.shape[0]
    shape = jax.ShapeDtypeStruct((size, size), jnp.float32)
    return pl.pallas_call(
        functools.partial(factor_kernel, blk),
        out_shape=[shape, shape],
        scratch_shapes=[pltpu.VMEM((size, size), jnp.float32)],
        compiler_params=pltpu.CompilerParams(vmem_limit_bytes=VMEM_LIMIT),
        cost_estimate=pl.CostEstimate(flops=size, bytes_accessed=size, transcendentals=0),
        name="factorize",
    )(square)


def right_kernel(inverse_ref, top_ref, high_ref, low_ref, inv_high, inv_low):
    @pl.when(pl.program_id(0) == 0)
    def _():
        inv_high[...], inv_low[...] = split(inverse_ref[...])

    result = product3((inv_high[...], inv_low[...]), split(top_ref[...]))
    high_ref[...], low_ref[...] = split(result)


def right_side(inverse, top, tile):
    size, cols = top.shape
    out = jax.ShapeDtypeStruct((size, cols), jnp.bfloat16)
    return pl.pallas_call(
        right_kernel,
        grid=(cols // tile,),
        in_specs=[
            pl.BlockSpec((size, size), lambda n: (0, 0)),
            pl.BlockSpec((size, tile), lambda n: (0, n)),
        ],
        out_specs=[pl.BlockSpec((size, tile), lambda n: (0, n))] * 2,
        out_shape=[out, out],
        scratch_shapes=[pltpu.VMEM((size, size), jnp.bfloat16)] * 2,
        compiler_params=pltpu.CompilerParams(vmem_limit_bytes=VMEM_LIMIT),
        cost_estimate=pl.CostEstimate(flops=size, bytes_accessed=size, transcendentals=0),
        name="right",
    )(inverse, top)


def finish_kernel(
    part_cols, child_cols, blk, row_count, col_count, first, table, place,
    panel_ref, front_ref, updates_ref, one, two, three, inverse_ref, lower_ref, high_ref, low_ref,
    out_ref, inv_high, inv_low, left_ref, sum_ref,
):
    step = pl.program_id(0)
    block_row = step * row_count + place[0]
    panel_blocks = NP * col_count
    inside = block_row < panel_blocks
    columns = [pl.multiple_of((s * col_count + place[1]) * blk, blk) for s in range(NP)]

    @pl.when(step == 0)
    def _():
        inv_high[...], inv_low[...] = split(inverse_ref[...])

    @pl.when(jnp.logical_not(inside))
    def _():
        add_children(
            sum_ref, table, front_ref, updates_ref, (one, two, three),
            range(NP, part_cols), part_cols, child_cols, blk,
        )
        panel = jnp.concatenate(
            [
                panel_ref[c, :, s * blk : (s + 1) * blk]
                for s in range(NP)
                for c in range(col_count)
            ],
            axis=1,
        )
        left_ref[...] = product3(split(panel), (inv_high[...], inv_low[...]), True)
        left_pair = split(left_ref[...])
        for pair in range(NP, part_cols, 2):
            cols = slice((pair - NP) * blk, (pair - NP + 2) * blk)
            trailing = product3(left_pair, (high_ref[:, cols], low_ref[:, cols]))
            updated = sum_ref[:, pair * blk : (pair + 2) * blk] - trailing
            for half in range(2):
                out_ref[0, pl.ds(pair + half, blk, stride=part_cols), :] = updated[
                    :, half * blk : (half + 1) * blk
                ]
        for s in range(NP):
            out_ref[0, pl.ds(s, blk, stride=part_cols), :] = left_ref[:, pl.ds(columns[s], blk)]

    @pl.when(inside)
    def _():
        out_ref[...] = jnp.zeros_like(out_ref)
        begin = pl.multiple_of(block_row * blk, blk)
        for s in range(NP):
            out_ref[0, pl.ds(s, blk, stride=part_cols), :] = lower_ref[
                pl.ds(begin, blk), pl.ds(columns[s], blk)
            ]


def finish(table, place, panel, front, updates, received, inverse, lower, high, low, row_count, first):
    part_rows, blk, part_cols = front.shape[0], front.shape[2], front.shape[3]
    child_cols = updates.shape[4]
    size = inverse.shape[0]
    slots = received[0].shape[0]
    col_count = panel.shape[0]

    def resident(shape):
        return pl.BlockSpec(shape, lambda a, t, p: (0, 0), pipeline_mode=pl.Buffered(1))

    def late(a, t, p):
        return (0, jnp.maximum(a - first, 0), 0)

    return pl.pallas_call(
        functools.partial(finish_kernel, part_cols, child_cols, blk, row_count, col_count, first),
        grid_spec=pltpu.PrefetchScalarGridSpec(
            num_scalar_prefetch=2,
            grid=(part_rows,),
            in_specs=[
                pl.BlockSpec((col_count, blk, NP * blk), late),
                pl.BlockSpec((1, blk * part_cols, blk), lambda a, t, p: (a, 0, 0)),
                pl.BlockSpec((2, 1, blk * child_cols, blk), lambda a, t, p: (0, a, 0, 0)),
            ]
            + [pl.BlockSpec((slots, blk, blk), late)] * 3
            + [
                resident((size, size)),
                resident((size, size)),
                resident(high.shape),
                resident(low.shape),
            ],
            out_specs=pl.BlockSpec((1, blk * part_cols, blk), lambda a, t, p: (a, 0, 0)),
            scratch_shapes=[
                pltpu.VMEM((size, size), jnp.bfloat16),
                pltpu.VMEM((size, size), jnp.bfloat16),
                pltpu.VMEM((blk, size), jnp.float32),
                pltpu.VMEM((blk, part_cols * blk), jnp.float32),
            ],
        ),
        out_shape=jax.ShapeDtypeStruct((part_rows, blk * part_cols, blk), jnp.float32),
        compiler_params=pltpu.CompilerParams(vmem_limit_bytes=VMEM_LIMIT),
        name="finish",
    )(
        table, place, panel,
        front.reshape(part_rows, blk * part_cols, blk),
        updates.reshape(2, part_rows, blk * child_cols, blk),
        *received, inverse, lower, high, low,
    )


def tables(maps, col_index, col_count, child_cols, part_cols, cap):
    offsets = maps[:, ::col_count] - col_count * jnp.arange(child_cols, dtype=jnp.int32)[None, :]
    turn = offsets % col_count
    groups = jnp.arange(child_cols, dtype=jnp.int32)
    same = (turn[:, :, None] == turn[:, None, :]) & (groups[None, None, :] < groups[None, :, None])
    rank = jnp.sum(same.astype(jnp.int32), axis=2)
    turns = jnp.arange(col_count, dtype=jnp.int32)
    slots = jnp.arange(cap, dtype=jnp.int32)
    hot = (turn[None, :, None, :] == turns[:, None, None, None]) & (
        rank[None, :, None, :] == slots[None, None, :, None]
    )
    send = jnp.sum(jnp.where(hot, groups[None, None, None, :], 0), axis=3).reshape(-1)
    parents = jnp.arange(part_cols, dtype=jnp.int32) * col_count + col_index
    match = maps[:, None, :] == parents[None, :, None]
    spread = jnp.repeat(groups, col_count)
    group = jnp.sum(jnp.where(match, spread[None, None, :], 0), axis=2)
    present = jnp.any(match, axis=2)
    pick = group[:, :, None] == groups[None, None, :]
    kind = jnp.sum(jnp.where(pick, turn[:, None, :], 0), axis=2)
    order = jnp.sum(jnp.where(pick, rank[:, None, :], 0), axis=2)
    order = jnp.where(kind == 0, group, order + cap * jnp.arange(2, dtype=jnp.int32)[:, None])
    kind = jnp.where(present, kind, col_count)
    place = jnp.stack([kind, order], axis=2).reshape(-1)
    return send, place


def gather_top(piece, row_count, row_index, panel_blocks):
    if row_count == panel_blocks:
        return lax.all_gather(piece, "row", axis=0, tiled=True)
    ids = jnp.arange(panel_blocks, dtype=jnp.int32)
    kept = jnp.where((ids == row_index)[:, None, None], piece[None], 0.0)
    return lax.psum(kept, "row").reshape(panel_blocks * piece.shape[0], piece.shape[1])


def simple_body(front, updates, maps):
    row_count = lax.axis_size("row")
    col_count = lax.axis_size("col")
    row_index = lax.axis_index("row")
    col_index = lax.axis_index("col")
    front = front.reshape(front.shape[0], 1, *front.shape[2:4], front.shape[5])
    blk, part_cols = front.shape[2], front.shape[3]
    child_cols = updates.shape[4]
    cap = child_cols // 2
    panel_blocks = NP * col_count
    send, place = tables(maps, col_index, col_count, child_cols, part_cols, cap)
    part_rows = front.shape[0]
    first = 1 if part_rows > 1 and row_count == panel_blocks else part_rows

    def exchange(outgoing):
        return [
            lax.ppermute(
                outgoing[turn - 1], "col", [(c, (c + turn) % col_count) for c in range(col_count)]
            )
            for turn in range(1, col_count)
        ]

    early = exchange(pack(send, updates, cap, 0, first))
    if first < part_rows:
        outgoing = pack(send, updates, cap, first, part_rows - first)
        early, outgoing = lax.optimization_barrier((early, outgoing))
        received = exchange(outgoing)
    else:
        received = early
    head = assemble(place, front, updates, early, 0, 1, part_cols)
    square = jnp.concatenate(
        [
            lax.all_gather(head[:, s * blk : (s + 1) * blk], "col", axis=1, tiled=True)
            for s in range(NP)
        ],
        axis=1,
    )
    square = gather_top(square, row_count, row_index, panel_blocks)
    rest, square = lax.optimization_barrier((head[:, NP * blk :], square))
    top = gather_top(rest, row_count, row_index, panel_blocks)
    lower, inverse = factorize(square, blk)
    high, low = right_side(inverse, top, 2 * blk)
    received, high, low = lax.optimization_barrier((received, high, low))
    late = first if first < part_rows else 0
    panel = assemble(place, front, updates, received, late, part_rows - late, NP)
    panel = lax.all_gather(panel, "col", axis=0)
    where = jnp.stack([row_index, col_index]).astype(jnp.int32)
    result = finish(
        place, where, panel, front, updates, received, inverse, lower, high, low, row_count, late
    )
    return result.reshape(front.shape[0], 1, blk, part_cols, 1, blk)


def square_kernel(
    blk, row_count, table, front_ref, updates_ref, one, two, three,
    square_ref, units_ref, got_one, got_two, got_three,
    work, front_part, updates_part, units, local, line_send, line_recv,
    col_send, col_recv, core_send, core_recv, turn_send, turn_recv,
):
    row, col = lax.axis_index("row"), lax.axis_index("col")
    part_cols = front_part.shape[0] // blk
    child_cols = updates_part.shape[1] // blk
    width = units.shape[0] // 4
    half = row_count // 2
    core = lax.rem(col, 2)
    other_core = col + 1 - 2 * core
    other_chip = lax.rem(col + 2, 4)
    diagonal = lax.rem(other_core + 2, 4)
    loads = [pltpu.make_async_copy(front_ref.at[0], front_part, local.at[0])]
    for member in range(2):
        loads.append(
            pltpu.make_async_copy(
                updates_ref.at[member, 0], updates_part.at[member], local.at[1 + member]
            )
        )
    for load in loads:
        load.start()

    def ring_row(position):
        position = lax.rem(position + row_count, row_count)
        return jnp.where(position < half, 2 * position, 2 * (row_count - position) - 1)

    place = jnp.where(lax.rem(row, 2) == 0, row // 2, row_count - 1 - row // 2)
    right, left = ring_row(place + 1), ring_row(place - 1)
    barrier = pltpu.get_barrier_semaphore()
    for device in (
        (row, other_core), (row, other_chip), (row, diagonal), (right, col), (left, col)
    ):
        pl.semaphore_signal(barrier, inc=1, device_id=device, device_id_type=MESH)
    for load in loads:
        load.wait()
    mine = col * width
    for member in range(2):
        for g in range(2):
            units[mine + member * 2 + g] = updates_part[member, pl.ds(g, blk, stride=child_cols), :]
    for s in range(NP):
        units[mine + 4 + s] = front_part[pl.ds(s, blk, stride=part_cols), :]
    pl.semaphore_wait(barrier, 5)

    def share(owner, device, index):
        part = units.at[pl.ds(owner * width, width)]
        return pltpu.make_async_remote_copy(
            src_ref=part, dst_ref=part, send_sem=col_send.at[index], recv_sem=col_recv.at[index],
            device_id=(row, device), device_id_type=MESH,
        )

    across = share(col, other_chip, 0)
    beside = share(col, other_core, 1)
    across.start()
    beside.start()
    turns = []
    for index, (source, target) in enumerate(((one, got_one), (two, got_two), (three, got_three))):
        turns.append(
            pltpu.make_async_remote_copy(
                src_ref=source, dst_ref=target,
                send_sem=turn_send.at[index], recv_sem=turn_recv.at[index],
                device_id=(row, lax.rem(col + index + 1, 4)), device_id_type=MESH,
            )
        )
        turns[-1].start()
    share(other_chip, other_chip, 0).wait_recv()
    passed = share(other_chip, other_core, 2)
    passed.start()
    share(other_core, other_core, 1).wait_recv()
    share(diagonal, other_core, 2).wait_recv()
    here = pl.multiple_of(row * blk, blk)
    for q in range(row_count):
        s, owner = q // 4, q % 4
        total = units[owner * width + 4 + s]
        for member in range(2):
            entry = 2 * (member * row_count + q)
            total = total + units[table[entry]] * table[entry + 1].astype(jnp.float32)
        work[pl.ds(here, blk), q * blk : (q + 1) * blk] = total

    cols = work.shape[1] // 2

    def part(position, side):
        begin = pl.multiple_of(ring_row(position) * blk, blk)
        return work.at[pl.ds(begin, blk), pl.ds(pl.multiple_of(side * cols, cols), cols)]

    def copy(ref, device, send, recv):
        return pltpu.make_async_remote_copy(
            src_ref=ref, dst_ref=ref, send_sem=send, recv_sem=recv,
            device_id=device, device_id_type=MESH,
        )

    pending = []
    for step in range(half):
        ways = range(2 if step < half - 1 else 1)
        for way in ways:
            position = place - step if way == 0 else place + step
            target = right if way == 0 else left
            move = copy(
                part(position, core), (target, col), line_send.at[way, step], line_recv.at[way, step]
            )
            move.start()
            pending.append(move)
        for way in ways:
            origin = place - step - 1 if way == 0 else place + step + 1
            landed = part(origin, core)
            copy(
                landed, (right, col), line_send.at[way, step], line_recv.at[way, step]
            ).wait_recv()
            forward = copy(
                landed, (row, other_core), core_send.at[way, step], core_recv.at[way, step]
            )
            forward.start()
            pending.append(forward)
    for way in range(2):
        for step in range(half - way):
            origin = place - step - 1 if way == 0 else place + step + 1
            copy(
                part(origin, 1 - core), (row, other_core),
                core_send.at[way, step], core_recv.at[way, step],
            ).wait_recv()
    stores = [
        pltpu.make_async_copy(work, square_ref, local.at[0]),
        pltpu.make_async_copy(units, units_ref, local.at[1]),
    ]
    for store in stores:
        store.start()
    for move in [across, beside, passed] + pending:
        move.wait_send()
    for store in stores:
        store.wait()
    for move in turns:
        move.wait()


def gather_square(table, front, updates, early, row_count):
    part_rows, blk, part_cols = front.shape[0], front.shape[2], front.shape[3]
    child_cols = updates.shape[4]
    size = row_count * blk
    half = row_count // 2
    anywhere = pl.BlockSpec(memory_space=pl.ANY)
    return pl.pallas_call(
        functools.partial(square_kernel, blk, row_count),
        in_specs=[pl.BlockSpec(memory_space=pltpu.SMEM)] + [anywhere] * 5,
        out_specs=[anywhere] * 5,
        out_shape=[
            jax.ShapeDtypeStruct((size, size), jnp.float32),
            jax.ShapeDtypeStruct((4 * (4 + NP), blk, blk), jnp.float32),
        ]
        + [jax.ShapeDtypeStruct(e.shape, e.dtype) for e in early],
        scratch_shapes=[
            pltpu.VMEM((size, size), jnp.float32),
            pltpu.VMEM((blk * part_cols, blk), jnp.float32),
            pltpu.VMEM((2, blk * child_cols, blk), jnp.float32),
            pltpu.VMEM((4 * (4 + NP), blk, blk), jnp.float32),
            pltpu.SemaphoreType.DMA((3,)),
            pltpu.SemaphoreType.DMA((2, half)),
            pltpu.SemaphoreType.DMA((2, half)),
            pltpu.SemaphoreType.DMA((3,)),
            pltpu.SemaphoreType.DMA((3,)),
            pltpu.SemaphoreType.DMA((2, half)),
            pltpu.SemaphoreType.DMA((2, half)),
            pltpu.SemaphoreType.DMA((3,)),
            pltpu.SemaphoreType.DMA((3,)),
        ],
        compiler_params=pltpu.CompilerParams(
            vmem_limit_bytes=VMEM_LIMIT, collective_id=0, has_side_effects=True
        ),
        cost_estimate=pl.CostEstimate(flops=size, bytes_accessed=size, transcendentals=0),
        name="square",
    )(
        table,
        front.reshape(part_rows, blk * part_cols, blk),
        updates.reshape(2, part_rows, blk * child_cols, blk),
        *early,
    )


def pack_turns_kernel(caps, most, part_cols, child_cols, blk, table, front_ref, updates_ref, *outs):
    step = pl.program_id(0)
    turns = len(caps)

    def send(refs):
        for turn, cap in enumerate(caps):
            for slot in range(cap):
                entry = (turn * most + slot) * 2
                refs[turn][slot] = updates_ref[
                    table[entry], 0, pl.ds(table[entry + 1], blk, stride=child_cols), :
                ]

    @pl.when(step == 0)
    def _():
        send(outs[1 : 1 + turns])

    @pl.when(step > 0)
    def _():
        for member in range(2):
            for g in range(2):
                outs[0][member * 2 + g] = updates_ref[member, 0, pl.ds(g, blk, stride=child_cols), :]
        for s in range(NP):
            outs[0][4 + s] = front_ref[0, pl.ds(s, blk, stride=part_cols), :]
        send(outs[1 + turns :])


def pack_turns(table, front, updates, caps, most):
    part_rows, blk, part_cols = front.shape[0], front.shape[2], front.shape[3]
    child_cols = updates.shape[4]
    turns = len(caps)
    sizes = [(4 + NP, part_rows - 1)] + [(cap, 1) for cap in caps]
    sizes += [(cap, part_rows - 1) for cap in caps]

    def late(a, t):
        return (0, jnp.maximum(a - 1, 0), 0)

    outs = pl.pallas_call(
        functools.partial(pack_turns_kernel, caps, most, part_cols, child_cols, blk),
        grid_spec=pltpu.PrefetchScalarGridSpec(
            num_scalar_prefetch=1,
            grid=(part_rows,),
            in_specs=[
                pl.BlockSpec((1, blk * part_cols, blk), lambda a, t: (a, 0, 0)),
                pl.BlockSpec((2, 1, blk * child_cols, blk), lambda a, t: (0, a, 0, 0)),
            ],
            out_specs=[
                pl.BlockSpec((count, blk, blk), late if rows > 1 else lambda a, t: (0, 0, 0))
                for count, rows in sizes
            ],
        ),
        out_shape=[
            jax.ShapeDtypeStruct((count, rows * blk, blk), jnp.float32) for count, rows in sizes
        ],
        compiler_params=pltpu.CompilerParams(vmem_limit_bytes=VMEM_LIMIT),
        cost_estimate=pl.CostEstimate(flops=blk, bytes_accessed=blk, transcendentals=0),
        name="pack",
    )(
        table,
        front.reshape(part_rows, blk * part_cols, blk),
        updates.reshape(2, part_rows, blk * child_cols, blk),
    )
    return outs[0], outs[1 : 1 + turns], outs[1 + turns :]


def add_units(out_ref, table, front_ref, updates_ref, received, shared, slots, base, part_cols, child_cols, blk):
    for slot in slots:
        cols = slice((slot - base) * blk, (slot - base + 1) * blk)
        out_ref[:, cols] = front_ref[0, pl.ds(slot, blk, stride=part_cols), :]
        for member in range(2):
            turn = table[(member * part_cols + slot) * 2]
            index = table[(member * part_cols + slot) * 2 + 1]

            @pl.when(turn == 0)
            def _():
                out_ref[:, cols] += updates_ref[member, 0, pl.ds(index, blk, stride=child_cols), :]

            @pl.when(turn == SHARED)
            def _():
                out_ref[:, cols] += shared[index]

            for step, ref in enumerate(received):

                @pl.when(turn == step + 1)
                def _():
                    out_ref[:, cols] += ref[index]


def assemble_top(table, front, updates, received, shared):
    part_rows, blk, part_cols = front.shape[0], front.shape[2], front.shape[3]
    child_cols = updates.shape[4]
    slots = range(NP, part_cols)

    def kernel(table, front_ref, updates_ref, one, two, three, shared_ref, out_ref):
        add_units(
            out_ref, table, front_ref, updates_ref, (one, two, three), shared_ref,
            slots, NP, part_cols, child_cols, blk,
        )

    return pl.pallas_call(
        kernel,
        grid_spec=pltpu.PrefetchScalarGridSpec(
            num_scalar_prefetch=1,
            grid=(1,),
            in_specs=[
                pl.BlockSpec((1, blk * part_cols, blk), lambda a, t: (0, 0, 0)),
                pl.BlockSpec((2, 1, blk * child_cols, blk), lambda a, t: (0, 0, 0, 0)),
            ]
            + [pl.BlockSpec(r.shape, lambda a, t: (0, 0, 0)) for r in received]
            + [pl.BlockSpec(shared.shape, lambda a, t: (0, 0, 0))],
            out_specs=pl.BlockSpec((blk, len(slots) * blk), lambda a, t: (0, 0)),
        ),
        out_shape=jax.ShapeDtypeStruct((blk, len(slots) * blk), jnp.float32),
        compiler_params=pltpu.CompilerParams(vmem_limit_bytes=VMEM_LIMIT),
        cost_estimate=pl.CostEstimate(flops=blk, bytes_accessed=blk, transcendentals=0),
        name="assemble",
    )(
        table,
        front.reshape(part_rows, blk * part_cols, blk),
        updates.reshape(2, part_rows, blk * child_cols, blk),
        *received, shared,
    )


def prepare_kernel(
    part_cols, child_cols, blk, row_count, col_count, table, square_table, place,
    front_ref, updates_ref, own, chip, core, both, inverse_ref, lower_ref,
    out_ref, left_ref, inv_high, inv_low, units, sum_ref, panel_ref,
):
    step = pl.program_id(0)
    columns = [pl.multiple_of((s * col_count + place[1]) * blk, blk) for s in range(NP)]
    size = inverse_ref.shape[0]

    @pl.when(step == 0)
    def _():
        inv_high[...], inv_low[...] = split(inverse_ref[...])
        out_ref[...] = jnp.zeros_like(out_ref)
        begin = pl.multiple_of(place[0] * blk, blk)
        for s in range(NP):
            out_ref[0, pl.ds(s, blk, stride=part_cols), :] = lower_ref[
                pl.ds(begin, blk), pl.ds(columns[s], blk)
            ]

    @pl.when(step > 0)
    def _():
        width = own.shape[0]
        for ref, owner in ((own, place[1]), (chip, place[2]), (core, place[3]), (both, place[4])):
            for i in range(width):
                units[owner * width + i] = ref[i]
        for q in range(row_count):
            total = units[(q % col_count) * width + 4 + q // col_count]
            for member in range(2):
                entry = 2 * (member * row_count + q)
                total = total + units[square_table[entry]] * square_table[entry + 1].astype(
                    jnp.float32
                )
            panel_ref[:, q * blk : (q + 1) * blk] = total
        add_units(
            sum_ref, table, front_ref, updates_ref, (), units,
            range(NP, part_cols), 0, part_cols, child_cols, blk,
        )
        panel_pair = split(panel_ref[...])
        for begin in range(0, size, 2 * blk):
            end = begin + 2 * blk
            left_ref[:, begin:end] = product3(
                tuple(p[:, :end] for p in panel_pair),
                (inv_high[begin:end, :end], inv_low[begin:end, :end]),
                True,
            )
        for slot in range(NP, part_cols):
            out_ref[0, pl.ds(slot, blk, stride=part_cols), :] = sum_ref[
                :, slot * blk : (slot + 1) * blk
            ]
        for s in range(NP):
            out_ref[0, pl.ds(s, blk, stride=part_cols), :] = left_ref[:, pl.ds(columns[s], blk)]


def prepare(table, square_table, place, front, updates, gathered, inverse, lower, row_count, col_count):
    part_rows, blk, part_cols = front.shape[0], front.shape[2], front.shape[3]
    child_cols = updates.shape[4]
    size = inverse.shape[0]

    def resident(shape):
        return pl.BlockSpec(shape, lambda a, t, q, p: (0, 0), pipeline_mode=pl.Buffered(1))

    return pl.pallas_call(
        functools.partial(prepare_kernel, part_cols, child_cols, blk, row_count, col_count),
        grid_spec=pltpu.PrefetchScalarGridSpec(
            num_scalar_prefetch=3,
            grid=(part_rows,),
            in_specs=[
                pl.BlockSpec((1, blk * part_cols, blk), lambda a, t, q, p: (a, 0, 0)),
                pl.BlockSpec((2, 1, blk * child_cols, blk), lambda a, t, q, p: (0, a, 0, 0)),
            ]
            + [
                pl.BlockSpec((g.shape[0], blk, blk), lambda a, t, q, p: (0, jnp.maximum(a - 1, 0), 0))
                for g in gathered
            ]
            + [resident((size, size))] * 2,
            out_specs=[
                pl.BlockSpec((1, blk * part_cols, blk), lambda a, t, q, p: (a, 0, 0)),
                pl.BlockSpec((blk, size), lambda a, t, q, p: (jnp.maximum(a - 1, 0), 0)),
            ],
            scratch_shapes=[
                pltpu.VMEM((size, size), jnp.bfloat16),
                pltpu.VMEM((size, size), jnp.bfloat16),
                pltpu.VMEM((4 * (4 + NP), blk, blk), jnp.float32),
                pltpu.VMEM((blk, part_cols * blk), jnp.float32),
                pltpu.VMEM((blk, size), jnp.float32),
            ],
        ),
        out_shape=[
            jax.ShapeDtypeStruct((part_rows, blk * part_cols, blk), jnp.float32),
            jax.ShapeDtypeStruct(((part_rows - 1) * blk, size), jnp.float32),
        ],
        compiler_params=pltpu.CompilerParams(vmem_limit_bytes=VMEM_LIMIT),
        cost_estimate=pl.CostEstimate(flops=blk, bytes_accessed=blk, transcendentals=0),
        name="prepare",
    )(
        table, square_table, place,
        front.reshape(part_rows, blk * part_cols, blk),
        updates.reshape(2, part_rows, blk * child_cols, blk),
        *gathered, inverse, lower,
    )


def trail_kernel(part_cols, blk, given_ref, left_ref, high_ref, low_ref, out_ref):
    left_pair = split(left_ref[...])
    for s in range(NP):
        out_ref[0, pl.ds(s, blk, stride=part_cols), :] = given_ref[
            0, pl.ds(s, blk, stride=part_cols), :
        ]
    for pair in range(NP, part_cols, 2):
        cols = slice((pair - NP) * blk, (pair - NP + 2) * blk)
        trailing = product3(left_pair, (high_ref[:, cols], low_ref[:, cols]))
        for half in range(2):
            slot = pl.ds(pair + half, blk, stride=part_cols)
            out_ref[0, slot, :] = given_ref[0, slot, :] - trailing[:, half * blk : (half + 1) * blk]


def trail(given, left, high, low, part_cols, blk):
    block = pl.BlockSpec((1, blk * part_cols, blk), lambda a: (a + 1, 0, 0))

    def resident(shape):
        return pl.BlockSpec(shape, lambda a: (0, 0), pipeline_mode=pl.Buffered(1))

    return pl.pallas_call(
        functools.partial(trail_kernel, part_cols, blk),
        grid=(given.shape[0] - 1,),
        in_specs=[
            block,
            pl.BlockSpec((blk, left.shape[1]), lambda a: (a, 0)),
            resident(high.shape),
            resident(low.shape),
        ],
        out_specs=block,
        out_shape=jax.ShapeDtypeStruct(given.shape, given.dtype),
        input_output_aliases={0: 0},
        compiler_params=pltpu.CompilerParams(vmem_limit_bytes=VMEM_LIMIT),
        cost_estimate=pl.CostEstimate(flops=blk, bytes_accessed=blk, transcendentals=0),
        name="trail",
    )(given, left, high, low)


def right_rows_kernel(inverse_ref, top_ref, high_ref, low_ref, inv_high, inv_low):
    @pl.when(pl.program_id(0) == 0)
    def _():
        inv_high[...], inv_low[...] = split(inverse_ref[...])

    size = inverse_ref.shape[0]
    top_high, top_low = split(top_ref[...])
    for begin in range(0, size, 256):
        end = begin + 256
        result = product3(
            (inv_high[begin:end, :end], inv_low[begin:end, :end]), (top_high[:end], top_low[:end])
        )
        high_ref[begin:end, :], low_ref[begin:end, :] = split(result)


def right_rows(inverse, top, tile):
    size, cols = top.shape
    out = jax.ShapeDtypeStruct((size, cols), jnp.bfloat16)
    return pl.pallas_call(
        right_rows_kernel,
        grid=(cols // tile,),
        in_specs=[
            pl.BlockSpec((size, size), lambda n: (0, 0)),
            pl.BlockSpec((size, tile), lambda n: (0, n)),
        ],
        out_specs=[pl.BlockSpec((size, tile), lambda n: (0, n))] * 2,
        out_shape=[out, out],
        scratch_shapes=[pltpu.VMEM((size, size), jnp.bfloat16)] * 2,
        compiler_params=pltpu.CompilerParams(vmem_limit_bytes=VMEM_LIMIT),
        cost_estimate=pl.CostEstimate(flops=size, bytes_accessed=size, transcendentals=0),
        name="right",
    )(inverse, top)


def add_last_kernel(part_cols, blk, table, given_ref, one, two, three, out_ref):
    out_ref[...] = given_ref[...]
    for slot in range(NP, part_cols):
        for member in range(2):
            turn = table[(member * part_cols + slot) * 2]
            index = table[(member * part_cols + slot) * 2 + 1]
            for step, ref in enumerate((one, two, three)):

                @pl.when(turn == step + 1)
                def _():
                    out_ref[0, pl.ds(slot, blk, stride=part_cols), :] += ref[index]


def add_last(table, given, received, part_cols, blk):
    part_rows = given.shape[0]
    block = pl.BlockSpec((1, blk * part_cols, blk), lambda a, t: (a + 1, 0, 0))
    return pl.pallas_call(
        functools.partial(add_last_kernel, part_cols, blk),
        grid_spec=pltpu.PrefetchScalarGridSpec(
            num_scalar_prefetch=1,
            grid=(part_rows - 1,),
            in_specs=[block]
            + [pl.BlockSpec((r.shape[0], blk, blk), lambda a, t: (0, a, 0)) for r in received],
            out_specs=block,
        ),
        out_shape=jax.ShapeDtypeStruct(given.shape, given.dtype),
        input_output_aliases={1: 0},
        compiler_params=pltpu.CompilerParams(vmem_limit_bytes=VMEM_LIMIT),
        cost_estimate=pl.CostEstimate(flops=blk, bytes_accessed=blk, transcendentals=0),
        name="add_last",
    )(table, given, *received)


def turn_tables(maps, col_index, col_count, child_cols, part_cols, most, panel_blocks):
    groups = jnp.arange(child_cols, dtype=jnp.int32)
    turn = (maps[:, ::col_count] - col_count * groups[None, :]) % col_count
    flat = jnp.where(groups[None, :] < 2, col_count, turn).T.reshape(-1)
    order = jnp.arange(2 * child_cols, dtype=jnp.int32)
    same = (flat[:, None] == flat[None, :]) & (order[None, :] < order[:, None])
    rank = jnp.sum(same.astype(jnp.int32), axis=1)
    turns = jnp.arange(1, col_count, dtype=jnp.int32)
    counts = jnp.sum((flat[None, :] == turns[:, None]).astype(jnp.int32), axis=1)
    slots = jnp.arange(most, dtype=jnp.int32)
    hot = (flat[None, None, :] == turns[:, None, None]) & (
        rank[None, None, :] == slots[None, :, None]
    )
    chosen = jnp.sum(jnp.where(hot, order[None, None, :], 0), axis=2)
    send = jnp.stack([chosen % 2, chosen // 2], axis=2).reshape(-1)
    rank = rank.reshape(child_cols, 2).T
    spread = jnp.repeat(groups, col_count)

    def look(parents):
        match = maps[:, None, :] == parents[None, :, None]
        group = jnp.sum(jnp.where(match, spread[None, None, :], 0), axis=2)
        source = jnp.sum(
            jnp.where(match, jnp.arange(maps.shape[1], dtype=jnp.int32)[None, None, :], 0), axis=2
        )
        return jnp.any(match, axis=2), group, source

    present, group, source = look(jnp.arange(part_cols, dtype=jnp.int32) * col_count + col_index)
    pick = group[:, :, None] == groups[None, None, :]
    kind = jnp.sum(jnp.where(pick, turn[:, None, :], 0), axis=2)
    index = jnp.sum(jnp.where(pick, rank[:, None, :], 0), axis=2)
    members = jnp.arange(2, dtype=jnp.int32)[:, None]
    index = jnp.where(kind == 0, group, index)
    shared = (group < 2) & (kind > 0)
    index = jnp.where(shared, (source % col_count) * (4 + NP) + 2 * members + group, index)
    kind = jnp.where(shared, SHARED, kind)
    kind = jnp.where(present, kind, col_count)
    place = jnp.stack([kind, index], axis=2).reshape(-1)
    present, group, source = look(jnp.arange(panel_blocks, dtype=jnp.int32))
    group = jnp.minimum(group, 1)
    unit = (source % col_count) * (4 + NP) + 2 * members + group
    square = jnp.stack([unit, present.astype(jnp.int32)], axis=2).reshape(-1)
    return send, place, square, counts


def main_branch(caps, most, row_count, front, updates, send, place, square_table, where):
    blk, part_cols = front.shape[2], front.shape[3]
    col_count = 4
    columns = range(col_count)

    def swap(value, mask):
        return lax.ppermute(value, "col", [(c, c ^ mask) for c in columns])

    units, early, late = pack_turns(send, front, updates, caps, most)
    square, shared, *early = gather_square(square_table, front, updates, early, row_count)
    units, square = lax.optimization_barrier((units, square))
    chip, core = swap(units, 2), swap(units, 1)
    top = assemble_top(place, front, updates, early, shared)
    top, square = lax.optimization_barrier((top, square))
    top = lax.all_gather(top, "row", axis=0, tiled=True)
    lower, inverse = factorize(square, blk)
    chip, core, inverse = lax.optimization_barrier((chip, core, inverse))
    late, chip = lax.optimization_barrier((late, chip))
    both = swap(chip, 1)
    late = [
        lax.ppermute(late[turn - 1], "col", [(c, (c + turn) % col_count) for c in columns])
        for turn in range(1, col_count)
    ]
    result, left = prepare(
        place, square_table, where, front, updates, (units, chip, core, both), inverse, lower,
        row_count, col_count,
    )
    left, top = lax.optimization_barrier((left, top))
    high, low = right_rows(inverse, top, 2 * blk)
    result = trail(result, left, high, low, part_cols, blk)
    result, late = lax.optimization_barrier((result, late))
    return add_last(place, result, late, part_cols, blk)


def body(row_count, col_count, front, updates, maps):
    part_rows = front.shape[0]
    if part_rows == 1 or row_count != NP * col_count or col_count != 4:
        return simple_body(front, updates, maps)
    row_index = lax.axis_index("row")
    col_index = lax.axis_index("col")
    front = front.reshape(front.shape[0], 1, *front.shape[2:4], front.shape[5])
    blk, part_cols = front.shape[2], front.shape[3]
    child_cols = updates.shape[4]
    most = child_cols
    send, place, square_table, counts = turn_tables(
        maps, col_index, col_count, child_cols, part_cols, most, row_count
    )
    where = jnp.stack([row_index] + [col_index ^ mask for mask in (0, 2, 1, 3)]).astype(jnp.int32)
    branches = [functools.partial(main_branch, caps, most, row_count) for caps in LEVELS]
    fits = jnp.all(counts[None, :] <= jnp.asarray(LEVELS, jnp.int32), axis=1)
    level = jnp.argmax(fits).astype(jnp.int32)
    operands = (front, updates, send, place, square_table, where)
    if len(branches) == 1:
        result = branches[0](*operands)
    else:
        result = lax.switch(level, branches, *operands)
    return result.reshape(part_rows, 1, blk, part_cols, 1, blk)


def solution(mesh):
    return jax.shard_map(
        functools.partial(body, mesh.shape["row"], mesh.shape["col"]),
        mesh=mesh,
        in_specs=(
            P(None, "row", None, None, "col", None),
            P(None, None, "row", None, None, "col", None),
            P(),
        ),
        out_specs=P(None, "row", None, None, "col", None),
        check_vma=False,
    )
```

```python
import functools

import jax
import jax.numpy as jnp
from jax import lax
from jax.experimental import pallas as pl
from jax.experimental.pallas import tpu as pltpu
from jax.sharding import PartitionSpec as P

NP = 2
highest = lax.Precision.HIGHEST
VMEM_LIMIT = 56 * 1024 * 1024
MESH = pl.DeviceIdType.MESH
SHARED = 5
LEVELS = (
    (5, 4, 7), (9, 2, 8), (8, 5, 6), (5, 6, 9), (8, 8, 4), (10, 4, 10), (6, 10, 5), (9, 8, 8),
    (12, 12, 12),
)


def split(value):
    high = value.astype(jnp.bfloat16)
    low = (value - high.astype(jnp.float32)).astype(jnp.bfloat16)
    return high, low


def dims(transposed):
    return (((1,), (1 if transposed else 0,)), ((), ()))


def product3(left_pair, right_pair, transposed=False):
    def one(a, b):
        return lax.dot_general(a, b, dims(transposed), preferred_element_type=jnp.float32)

    return (
        one(left_pair[0], right_pair[0])
        + one(left_pair[0], right_pair[1])
        + one(left_pair[1], right_pair[0])
    )


def product(a, b, transposed=False):
    return lax.dot_general(
        a, b, dims(transposed), precision=highest, preferred_element_type=jnp.float32
    )


def pack_kernel(child_cols, cap, blk, table, updates_ref, one_ref, two_ref, three_ref):
    for turn, out_ref in enumerate((one_ref, two_ref, three_ref)):
        for member in range(2):
            for slot in range(cap):
                source = table[(turn + 1) * 2 * cap + member * cap + slot]
                out_ref[member * cap + slot] = updates_ref[
                    member, 0, pl.ds(source, blk, stride=child_cols), :
                ]


def pack(table, updates, cap, begin, count):
    part_rows, blk, child_cols = updates.shape[1], updates.shape[3], updates.shape[4]
    flat = updates.reshape(2, part_rows, blk * child_cols, blk)
    return pl.pallas_call(
        functools.partial(pack_kernel, child_cols, cap, blk),
        grid_spec=pltpu.PrefetchScalarGridSpec(
            num_scalar_prefetch=1,
            grid=(count,),
            in_specs=[
                pl.BlockSpec((2, 1, blk * child_cols, blk), lambda a, t: (0, a + begin, 0, 0))
            ],
            out_specs=[pl.BlockSpec((2 * cap, blk, blk), lambda a, t: (0, a, 0))] * 3,
        ),
        out_shape=[jax.ShapeDtypeStruct((2 * cap, count * blk, blk), jnp.float32)] * 3,
        compiler_params=pltpu.CompilerParams(vmem_limit_bytes=VMEM_LIMIT),
        name="pack",
    )(table, flat)


def add_children(out_ref, table, front_ref, updates_ref, received, slots, part_cols, child_cols, blk):
    for slot in slots:
        cols = slice(slot * blk, (slot + 1) * blk)
        out_ref[:, cols] = front_ref[0, pl.ds(slot, blk, stride=part_cols), :]
        for member in range(2):
            turn = table[(member * part_cols + slot) * 2]
            index = table[(member * part_cols + slot) * 2 + 1]

            @pl.when(turn == 0)
            def _():
                out_ref[:, cols] += updates_ref[member, 0, pl.ds(index, blk, stride=child_cols), :]

            for step in range(3):

                @pl.when(turn == step + 1)
                def _():
                    out_ref[:, cols] += received[step][index]


def assemble(table, front, updates, received, begin, count, width):
    part_rows, blk, part_cols = front.shape[0], front.shape[2], front.shape[3]
    child_cols = updates.shape[4]
    slots = received[0].shape[0]

    def kernel(table, front_ref, updates_ref, one, two, three, out_ref):
        add_children(
            out_ref, table, front_ref, updates_ref, (one, two, three),
            range(width), part_cols, child_cols, blk,
        )

    return pl.pallas_call(
        kernel,
        grid_spec=pltpu.PrefetchScalarGridSpec(
            num_scalar_prefetch=1,
            grid=(count,),
            in_specs=[
                pl.BlockSpec((1, blk * part_cols, blk), lambda a, t: (a + begin, 0, 0)),
                pl.BlockSpec((2, 1, blk * child_cols, blk), lambda a, t: (0, a + begin, 0, 0)),
            ]
            + [pl.BlockSpec((slots, blk, blk), lambda a, t: (0, a, 0))] * 3,
            out_specs=pl.BlockSpec((blk, width * blk), lambda a, t: (a, 0)),
        ),
        out_shape=jax.ShapeDtypeStruct((count * blk, width * blk), jnp.float32),
        compiler_params=pltpu.CompilerParams(vmem_limit_bytes=VMEM_LIMIT),
        name="assemble",
    )(
        table,
        front.reshape(part_rows, blk * part_cols, blk),
        updates.reshape(2, part_rows, blk * child_cols, blk),
        *received,
    )


def eliminate(block):
    size = block.shape[0]
    group = 8
    tiles = size // group
    shape = (group, size)
    row_ids = lax.broadcasted_iota(jnp.int32, (size, size), 0)
    col_ids = lax.broadcasted_iota(jnp.int32, (size, size), 1)
    local = lax.broadcasted_iota(jnp.int32, shape, 0)
    start = (row_ids == col_ids).astype(jnp.float32)
    upper = [block[group * t : group * (t + 1), :] for t in range(tiles)]
    solved = [start[group * t : group * (t + 1), :] for t in range(tiles)]
    for h in range(tiles):
        def column(t, j):
            return jnp.broadcast_to(upper[t][:, group * h + j : group * h + j + 1], shape)
        home = [column(h, j) for j in range(group)]
        pivot = {
            (i, j): jnp.broadcast_to(home[j][i : i + 1, :], shape)
            for j in range(group) for i in range(j, group)
        }
        scale, ratio = [], {}
        for j in range(group):
            scale.append(1.0 / pivot[j, j])
            for i in range(j + 1, group):
                ratio[i, j] = pivot[i, j] * scale[j]
            for k in range(j + 1, group):
                for i in range(k, group):
                    pivot[i, k] = pivot[i, k] - ratio[i, j] * pivot[k, j]
        upper_rows, solved_rows = [], []
        for j in range(group):
            u = jnp.broadcast_to(upper[h][j : j + 1, :], shape)
            s = jnp.broadcast_to(solved[h][j : j + 1, :], shape)
            for i in range(j):
                u = u - ratio[j, i] * upper_rows[i]
                s = s - ratio[j, i] * solved_rows[i]
            upper_rows.append(u)
            solved_rows.append(s)
        for t in range(h, tiles):
            if t == h:
                u, s = upper_rows[0], solved_rows[0]
                for j in range(1, group):
                    u = jnp.where(local == j, upper_rows[j], u)
                    s = jnp.where(local == j, solved_rows[j], s)
                upper[t], solved[t] = u, s
                continue
            factors = []
            for j in range(group):
                c = column(t, j)
                for i in range(j):
                    c = c - factors[i] * pivot[j, i]
                factors.append(c * scale[j])
            for j in range(group):
                upper[t] = upper[t] - factors[j] * upper_rows[j]
                solved[t] = solved[t] - factors[j] * solved_rows[j]
    upper = jnp.concatenate(upper, axis=0)
    solved = jnp.concatenate(solved, axis=0)
    diagonal = jnp.sum(jnp.where(row_ids == col_ids, upper, 0.0), axis=1, keepdims=True)
    scale = 1.0 / jnp.sqrt(diagonal)
    lower = jnp.where(col_ids >= row_ids, upper * scale, 0.0).T
    return lower, solved * scale

def factor_kernel(blk, square_ref, lower_ref, inverse_ref, work):
    size = square_ref.shape[0]
    count = size // blk
    work[...] = square_ref[...]
    lower_ref[...] = jnp.zeros_like(lower_ref)
    inverse_ref[...] = jnp.zeros_like(inverse_ref)

    def spread(k, diag_inverse):
        begin, end = k * blk, (k + 1) * blk
        here = slice(begin, end)
        inverse_pair = split(diag_inverse)
        if k:
            done = product3(inverse_pair, split(inverse_ref[here, :begin]))
            inverse_ref[here, :begin] = done
        inverse_ref[here, here] = diag_inverse
        if end == size:
            return
        row_high, row_low = split(inverse_ref[here, :end])
        left_high, left_low = [], []
        for q in range(end, size, 256):
            top = min(q + 256, size)
            left = product3(split(work[q:top, here]), inverse_pair, True)
            lower_ref[q:top, here] = left
            high, low = split(left)
            left_high.append(high)
            left_low.append(low)
        high = jnp.concatenate(left_high, axis=0)
        low = jnp.concatenate(left_low, axis=0)
        for q in range(end, size, 256):
            top = min(q + 256, size)
            pair = high[q - end : top - end], low[q - end : top - end]
            below = high[: top - end], low[: top - end]
            work[q:top, end:top] -= product3(pair, below, True)
            inverse_ref[q:top, :end] -= product3(pair, (row_high, row_low))

    def step(k, carry):
        begin = pl.multiple_of(k * blk, blk)
        here = pl.ds(begin, blk)
        diag_lower, diag_inverse = eliminate(work[here, here])
        lower_ref[here, here] = diag_lower
        for t in range(count):
            pl.when(k == t)(functools.partial(spread, t, diag_inverse))
        return carry

    lax.fori_loop(0, count, step, 0)


def factorize(square, blk):
    size = square.shape[0]
    shape = jax.ShapeDtypeStruct((size, size), jnp.float32)
    return pl.pallas_call(
        functools.partial(factor_kernel, blk),
        out_shape=[shape, shape],
        scratch_shapes=[pltpu.VMEM((size, size), jnp.float32)],
        compiler_params=pltpu.CompilerParams(vmem_limit_bytes=VMEM_LIMIT),
        cost_estimate=pl.CostEstimate(flops=size, bytes_accessed=size, transcendentals=0),
        name="factorize",
    )(square)


def right_kernel(inverse_ref, top_ref, high_ref, low_ref, inv_high, inv_low):
    @pl.when(pl.program_id(0) == 0)
    def _():
        inv_high[...], inv_low[...] = split(inverse_ref[...])

    result = product3((inv_high[...], inv_low[...]), split(top_ref[...]))
    high_ref[...], low_ref[...] = split(result)


def right_side(inverse, top, tile):
    size, cols = top.shape
    out = jax.ShapeDtypeStruct((size, cols), jnp.bfloat16)
    return pl.pallas_call(
        right_kernel,
        grid=(cols // tile,),
        in_specs=[
            pl.BlockSpec((size, size), lambda n: (0, 0)),
            pl.BlockSpec((size, tile), lambda n: (0, n)),
        ],
        out_specs=[pl.BlockSpec((size, tile), lambda n: (0, n))] * 2,
        out_shape=[out, out],
        scratch_shapes=[pltpu.VMEM((size, size), jnp.bfloat16)] * 2,
        compiler_params=pltpu.CompilerParams(vmem_limit_bytes=VMEM_LIMIT),
        cost_estimate=pl.CostEstimate(flops=size, bytes_accessed=size, transcendentals=0),
        name="right",
    )(inverse, top)


def finish_kernel(
    part_cols, child_cols, blk, row_count, col_count, first, table, place,
    panel_ref, front_ref, updates_ref, one, two, three, inverse_ref, lower_ref, high_ref, low_ref,
    out_ref, inv_high, inv_low, left_ref, sum_ref,
):
    step = pl.program_id(0)
    block_row = step * row_count + place[0]
    panel_blocks = NP * col_count
    inside = block_row < panel_blocks
    columns = [pl.multiple_of((s * col_count + place[1]) * blk, blk) for s in range(NP)]

    @pl.when(step == 0)
    def _():
        inv_high[...], inv_low[...] = split(inverse_ref[...])

    @pl.when(jnp.logical_not(inside))
    def _():
        add_children(
            sum_ref, table, front_ref, updates_ref, (one, two, three),
            range(NP, part_cols), part_cols, child_cols, blk,
        )
        panel = jnp.concatenate(
            [
                panel_ref[c, :, s * blk : (s + 1) * blk]
                for s in range(NP)
                for c in range(col_count)
            ],
            axis=1,
        )
        left_ref[...] = product3(split(panel), (inv_high[...], inv_low[...]), True)
        left_pair = split(left_ref[...])
        for pair in range(NP, part_cols, 2):
            cols = slice((pair - NP) * blk, (pair - NP + 2) * blk)
            trailing = product3(left_pair, (high_ref[:, cols], low_ref[:, cols]))
            updated = sum_ref[:, pair * blk : (pair + 2) * blk] - trailing
            for half in range(2):
                out_ref[0, pl.ds(pair + half, blk, stride=part_cols), :] = updated[
                    :, half * blk : (half + 1) * blk
                ]
        for s in range(NP):
            out_ref[0, pl.ds(s, blk, stride=part_cols), :] = left_ref[:, pl.ds(columns[s], blk)]

    @pl.when(inside)
    def _():
        out_ref[...] = jnp.zeros_like(out_ref)
        begin = pl.multiple_of(block_row * blk, blk)
        for s in range(NP):
            out_ref[0, pl.ds(s, blk, stride=part_cols), :] = lower_ref[
                pl.ds(begin, blk), pl.ds(columns[s], blk)
            ]


def finish(table, place, panel, front, updates, received, inverse, lower, high, low, row_count, first):
    part_rows, blk, part_cols = front.shape[0], front.shape[2], front.shape[3]
    child_cols = updates.shape[4]
    size = inverse.shape[0]
    slots = received[0].shape[0]
    col_count = panel.shape[0]

    def resident(shape):
        return pl.BlockSpec(shape, lambda a, t, p: (0, 0), pipeline_mode=pl.Buffered(1))

    def late(a, t, p):
        return (0, jnp.maximum(a - first, 0), 0)

    return pl.pallas_call(
        functools.partial(finish_kernel, part_cols, child_cols, blk, row_count, col_count, first),
        grid_spec=pltpu.PrefetchScalarGridSpec(
            num_scalar_prefetch=2,
            grid=(part_rows,),
            in_specs=[
                pl.BlockSpec((col_count, blk, NP * blk), late),
                pl.BlockSpec((1, blk * part_cols, blk), lambda a, t, p: (a, 0, 0)),
                pl.BlockSpec((2, 1, blk * child_cols, blk), lambda a, t, p: (0, a, 0, 0)),
            ]
            + [pl.BlockSpec((slots, blk, blk), late)] * 3
            + [
                resident((size, size)),
                resident((size, size)),
                resident(high.shape),
                resident(low.shape),
            ],
            out_specs=pl.BlockSpec((1, blk * part_cols, blk), lambda a, t, p: (a, 0, 0)),
            scratch_shapes=[
                pltpu.VMEM((size, size), jnp.bfloat16),
                pltpu.VMEM((size, size), jnp.bfloat16),
                pltpu.VMEM((blk, size), jnp.float32),
                pltpu.VMEM((blk, part_cols * blk), jnp.float32),
            ],
        ),
        out_shape=jax.ShapeDtypeStruct((part_rows, blk * part_cols, blk), jnp.float32),
        compiler_params=pltpu.CompilerParams(vmem_limit_bytes=VMEM_LIMIT),
        name="finish",
    )(
        table, place, panel,
        front.reshape(part_rows, blk * part_cols, blk),
        updates.reshape(2, part_rows, blk * child_cols, blk),
        *received, inverse, lower, high, low,
    )


def tables(maps, col_index, col_count, child_cols, part_cols, cap):
    offsets = maps[:, ::col_count] - col_count * jnp.arange(child_cols, dtype=jnp.int32)[None, :]
    turn = offsets % col_count
    groups = jnp.arange(child_cols, dtype=jnp.int32)
    same = (turn[:, :, None] == turn[:, None, :]) & (groups[None, None, :] < groups[None, :, None])
    rank = jnp.sum(same.astype(jnp.int32), axis=2)
    turns = jnp.arange(col_count, dtype=jnp.int32)
    slots = jnp.arange(cap, dtype=jnp.int32)
    hot = (turn[None, :, None, :] == turns[:, None, None, None]) & (
        rank[None, :, None, :] == slots[None, None, :, None]
    )
    send = jnp.sum(jnp.where(hot, groups[None, None, None, :], 0), axis=3).reshape(-1)
    parents = jnp.arange(part_cols, dtype=jnp.int32) * col_count + col_index
    match = maps[:, None, :] == parents[None, :, None]
    spread = jnp.repeat(groups, col_count)
    group = jnp.sum(jnp.where(match, spread[None, None, :], 0), axis=2)
    present = jnp.any(match, axis=2)
    pick = group[:, :, None] == groups[None, None, :]
    kind = jnp.sum(jnp.where(pick, turn[:, None, :], 0), axis=2)
    order = jnp.sum(jnp.where(pick, rank[:, None, :], 0), axis=2)
    order = jnp.where(kind == 0, group, order + cap * jnp.arange(2, dtype=jnp.int32)[:, None])
    kind = jnp.where(present, kind, col_count)
    place = jnp.stack([kind, order], axis=2).reshape(-1)
    return send, place


def gather_top(piece, row_count, row_index, panel_blocks):
    if row_count == panel_blocks:
        return lax.all_gather(piece, "row", axis=0, tiled=True)
    ids = jnp.arange(panel_blocks, dtype=jnp.int32)
    kept = jnp.where((ids == row_index)[:, None, None], piece[None], 0.0)
    return lax.psum(kept, "row").reshape(panel_blocks * piece.shape[0], piece.shape[1])


def simple_body(front, updates, maps):
    row_count = lax.axis_size("row")
    col_count = lax.axis_size("col")
    row_index = lax.axis_index("row")
    col_index = lax.axis_index("col")
    front = front.reshape(front.shape[0], 1, *front.shape[2:4], front.shape[5])
    blk, part_cols = front.shape[2], front.shape[3]
    child_cols = updates.shape[4]
    cap = child_cols // 2
    panel_blocks = NP * col_count
    send, place = tables(maps, col_index, col_count, child_cols, part_cols, cap)
    part_rows = front.shape[0]
    first = 1 if part_rows > 1 and row_count == panel_blocks else part_rows

    def exchange(outgoing):
        return [
            lax.ppermute(
                outgoing[turn - 1], "col", [(c, (c + turn) % col_count) for c in range(col_count)]
            )
            for turn in range(1, col_count)
        ]

    early = exchange(pack(send, updates, cap, 0, first))
    if first < part_rows:
        outgoing = pack(send, updates, cap, first, part_rows - first)
        early, outgoing = lax.optimization_barrier((early, outgoing))
        received = exchange(outgoing)
    else:
        received = early
    head = assemble(place, front, updates, early, 0, 1, part_cols)
    square = jnp.concatenate(
        [
            lax.all_gather(head[:, s * blk : (s + 1) * blk], "col", axis=1, tiled=True)
            for s in range(NP)
        ],
        axis=1,
    )
    square = gather_top(square, row_count, row_index, panel_blocks)
    rest, square = lax.optimization_barrier((head[:, NP * blk :], square))
    top = gather_top(rest, row_count, row_index, panel_blocks)
    lower, inverse = factorize(square, blk)
    high, low = right_side(inverse, top, 2 * blk)
    received, high, low = lax.optimization_barrier((received, high, low))
    late = first if first < part_rows else 0
    panel = assemble(place, front, updates, received, late, part_rows - late, NP)
    panel = lax.all_gather(panel, "col", axis=0)
    where = jnp.stack([row_index, col_index]).astype(jnp.int32)
    result = finish(
        place, where, panel, front, updates, received, inverse, lower, high, low, row_count, late
    )
    return result.reshape(front.shape[0], 1, blk, part_cols, 1, blk)


def send_kernel(
    blk, front_ref, updates_ref, one, two, three, units_ref, got_one, got_two, got_three,
    front_part, updates_part, units, local, send, recv,
):
    row, col = lax.axis_index("row"), lax.axis_index("col")
    part_cols = front_part.shape[0] // blk
    child_cols = updates_part.shape[1] // blk
    width = units.shape[0]
    loads = [pltpu.make_async_copy(front_ref.at[0], front_part, local.at[0])]
    for member in range(2):
        loads.append(
            pltpu.make_async_copy(
                updates_ref.at[member, 0], updates_part.at[member], local.at[1 + member]
            )
        )
    for load in loads:
        load.start()
    others = [lax.rem(col + turn, 4) for turn in range(1, 4)]
    barrier = pltpu.get_barrier_semaphore()
    for other in others:
        pl.semaphore_signal(barrier, inc=1, device_id=(row, other), device_id_type=MESH)
    for load in loads:
        load.wait()
    for member in range(2):
        for g in range(2):
            units[member * 2 + g] = updates_part[member, pl.ds(g, blk, stride=child_cols), :]
    for s in range(NP):
        units[4 + s] = front_part[pl.ds(s, blk, stride=part_cols), :]
    pl.semaphore_wait(barrier, 3)

    def remote(source, target, index, device):
        return pltpu.make_async_remote_copy(
            src_ref=source, dst_ref=target, send_sem=send.at[index], recv_sem=recv.at[index],
            device_id=(row, device), device_id_type=MESH,
        )

    across = remote(units, units_ref.at[pl.ds(col * width, width)], 3, others[1])
    across.start()
    keep = pltpu.make_async_copy(units, units_ref.at[pl.ds(col * width, width)], local.at[0])
    keep.start()
    moves = []
    for turn, (source, target) in enumerate(((one, got_one), (two, got_two), (three, got_three))):
        moves.append(remote(source, target, turn, others[turn]))
        moves[-1].start()
    keep.wait()
    across.wait_send()
    remote(units, units_ref.at[pl.ds(others[1] * width, width)], 3, others[1]).wait_recv()
    for move in moves:
        move.wait()


def send_head(front, updates, early, identity):
    part_rows, blk, part_cols = front.shape[0], front.shape[2], front.shape[3]
    child_cols = updates.shape[4]
    anywhere = pl.BlockSpec(memory_space=pl.ANY)
    width = 4 + NP
    return pl.pallas_call(
        functools.partial(send_kernel, blk),
        in_specs=[anywhere] * 5,
        out_specs=[anywhere] * 4,
        out_shape=[jax.ShapeDtypeStruct((4 * width, blk, blk), jnp.float32)]
        + [jax.ShapeDtypeStruct(e.shape, e.dtype) for e in early],
        scratch_shapes=[
            pltpu.VMEM((blk * part_cols, blk), jnp.float32),
            pltpu.VMEM((2, blk * child_cols, blk), jnp.float32),
            pltpu.VMEM((width, blk, blk), jnp.float32),
            pltpu.SemaphoreType.DMA((3,)),
            pltpu.SemaphoreType.DMA((4,)),
            pltpu.SemaphoreType.DMA((4,)),
        ],
        compiler_params=pltpu.CompilerParams(
            vmem_limit_bytes=VMEM_LIMIT, collective_id=identity, has_side_effects=True
        ),
        cost_estimate=pl.CostEstimate(flops=blk, bytes_accessed=blk, transcendentals=0),
        name="send",
    )(
        front.reshape(part_rows, blk * part_cols, blk),
        updates.reshape(2, part_rows, blk * child_cols, blk),
        *early,
    )


def square_kernel(
    blk, row_count, turn, table, given_ref, sent_ref, square_ref, units_ref, got_ref,
    work, units, local, line_send, line_recv, col_send, col_recv, core_send, core_recv,
    turn_send, turn_recv,
):
    row, col = lax.axis_index("row"), lax.axis_index("col")
    width = units.shape[0] // 4
    half = row_count // 2
    core = lax.rem(col, 2)
    other_core = col + 1 - 2 * core
    other_chip = lax.rem(col + 2, 4)
    diagonal = lax.rem(other_core + 2, 4)

    def section(ref, owner):
        return ref.at[pl.ds(owner * width, width)]

    loads = []
    for index, owner in enumerate((col, other_chip)):
        loads.append(
            pltpu.make_async_copy(
                section(given_ref, owner), section(units, owner), local.at[index]
            )
        )
        loads[-1].start()

    def ring_row(position):
        position = lax.rem(position + row_count, row_count)
        return jnp.where(position < half, 2 * position, 2 * (row_count - position) - 1)

    place = jnp.where(lax.rem(row, 2) == 0, row // 2, row_count - 1 - row // 2)
    right, left = ring_row(place + 1), ring_row(place - 1)
    barrier = pltpu.get_barrier_semaphore()
    for device in (
        (row, other_core), (row, other_chip), (row, diagonal), (right, col), (left, col)
    ):
        pl.semaphore_signal(barrier, inc=1, device_id=device, device_id_type=MESH)
    for load in loads:
        load.wait()
    pl.semaphore_wait(barrier, 5)
    turned = pltpu.make_async_remote_copy(
        src_ref=sent_ref, dst_ref=got_ref, send_sem=turn_send, recv_sem=turn_recv,
        device_id=(row, lax.rem(col + turn, 4)), device_id_type=MESH,
    )
    turned.start()

    def share(owner, index):
        part = section(units, owner)
        return pltpu.make_async_remote_copy(
            src_ref=part, dst_ref=part, send_sem=col_send.at[index], recv_sem=col_recv.at[index],
            device_id=(row, other_core), device_id_type=MESH,
        )

    shares = [share(col, 0), share(other_chip, 1)]
    for move in shares:
        move.start()
    share(other_core, 0).wait_recv()
    share(diagonal, 1).wait_recv()
    here = pl.multiple_of(row * blk, blk)
    for q in range(row_count):
        s, owner = q // 4, q % 4
        total = units[owner * width + 4 + s]
        for member in range(2):
            entry = 2 * (member * row_count + q)
            total = total + units[table[entry]] * table[entry + 1].astype(jnp.float32)
        work[pl.ds(here, blk), q * blk : (q + 1) * blk] = total

    cols = work.shape[1] // 2

    def part(position, side):
        begin = pl.multiple_of(ring_row(position) * blk, blk)
        return work.at[pl.ds(begin, blk), pl.ds(pl.multiple_of(side * cols, cols), cols)]

    def copy(ref, device, send, recv):
        return pltpu.make_async_remote_copy(
            src_ref=ref, dst_ref=ref, send_sem=send, recv_sem=recv,
            device_id=device, device_id_type=MESH,
        )

    pending = []
    for step in range(half):
        ways = range(2 if step < half - 1 else 1)
        for way in ways:
            position = place - step if way == 0 else place + step
            target = right if way == 0 else left
            move = copy(
                part(position, core), (target, col), line_send.at[way, step], line_recv.at[way, step]
            )
            move.start()
            pending.append(move)
        for way in ways:
            origin = place - step - 1 if way == 0 else place + step + 1
            landed = part(origin, core)
            copy(
                landed, (right, col), line_send.at[way, step], line_recv.at[way, step]
            ).wait_recv()
            forward = copy(
                landed, (row, other_core), core_send.at[way, step], core_recv.at[way, step]
            )
            forward.start()
            pending.append(forward)
    for way in range(2):
        for step in range(half - way):
            origin = place - step - 1 if way == 0 else place + step + 1
            copy(
                part(origin, 1 - core), (row, other_core),
                core_send.at[way, step], core_recv.at[way, step],
            ).wait_recv()
    stores = [
        pltpu.make_async_copy(work, square_ref, local.at[0]),
        pltpu.make_async_copy(units, units_ref, local.at[1]),
    ]
    for store in stores:
        store.start()
    for move in shares + pending:
        move.wait_send()
    for store in stores:
        store.wait()
    turned.wait()


def gather_square(table, given, sent, turn, row_count, identity):
    blk = given.shape[1]
    size = row_count * blk
    half = row_count // 2
    anywhere = pl.BlockSpec(memory_space=pl.ANY)
    return pl.pallas_call(
        functools.partial(square_kernel, blk, row_count, turn),
        in_specs=[pl.BlockSpec(memory_space=pltpu.SMEM), anywhere, anywhere],
        out_specs=[anywhere] * 3,
        out_shape=[
            jax.ShapeDtypeStruct((size, size), jnp.float32),
            jax.ShapeDtypeStruct(given.shape, jnp.float32),
            jax.ShapeDtypeStruct(sent.shape, jnp.float32),
        ],
        scratch_shapes=[
            pltpu.VMEM((size, size), jnp.float32),
            pltpu.VMEM(given.shape, jnp.float32),
            pltpu.SemaphoreType.DMA((2,)),
            pltpu.SemaphoreType.DMA((2, half)),
            pltpu.SemaphoreType.DMA((2, half)),
            pltpu.SemaphoreType.DMA((2,)),
            pltpu.SemaphoreType.DMA((2,)),
            pltpu.SemaphoreType.DMA((2, half)),
            pltpu.SemaphoreType.DMA((2, half)),
            pltpu.SemaphoreType.DMA,
            pltpu.SemaphoreType.DMA,
        ],
        compiler_params=pltpu.CompilerParams(
            vmem_limit_bytes=VMEM_LIMIT, collective_id=identity, has_side_effects=True
        ),
        cost_estimate=pl.CostEstimate(flops=size, bytes_accessed=size, transcendentals=0),
        name="square",
    )(table, given, sent)


def pack_turns_kernel(caps, most, part_cols, child_cols, blk, table, front_ref, updates_ref, *outs):
    step = pl.program_id(0)
    turns = len(caps)

    def send(refs):
        for turn, cap in enumerate(caps):
            for slot in range(cap):
                entry = (turn * most + slot) * 2
                refs[turn][slot] = updates_ref[
                    table[entry], 0, pl.ds(table[entry + 1], blk, stride=child_cols), :
                ]

    @pl.when(step == 0)
    def _():
        send(outs[1 : 1 + turns])

    @pl.when(step > 0)
    def _():
        for member in range(2):
            for g in range(2):
                outs[0][member * 2 + g] = updates_ref[member, 0, pl.ds(g, blk, stride=child_cols), :]
        for s in range(NP):
            outs[0][4 + s] = front_ref[0, pl.ds(s, blk, stride=part_cols), :]
        send(outs[1 + turns :])


def pack_turns(table, front, updates, caps, most):
    part_rows, blk, part_cols = front.shape[0], front.shape[2], front.shape[3]
    child_cols = updates.shape[4]
    turns = len(caps)
    sizes = [(4 + NP, part_rows - 1)] + [(cap, 1) for cap in caps]
    sizes += [(cap, part_rows - 1) for cap in caps]

    def late(a, t):
        return (0, jnp.maximum(a - 1, 0), 0)

    outs = pl.pallas_call(
        functools.partial(pack_turns_kernel, caps, most, part_cols, child_cols, blk),
        grid_spec=pltpu.PrefetchScalarGridSpec(
            num_scalar_prefetch=1,
            grid=(part_rows,),
            in_specs=[
                pl.BlockSpec((1, blk * part_cols, blk), lambda a, t: (a, 0, 0)),
                pl.BlockSpec((2, 1, blk * child_cols, blk), lambda a, t: (0, a, 0, 0)),
            ],
            out_specs=[
                pl.BlockSpec((count, blk, blk), late if rows > 1 else lambda a, t: (0, 0, 0))
                for count, rows in sizes
            ],
        ),
        out_shape=[
            jax.ShapeDtypeStruct((count, rows * blk, blk), jnp.float32) for count, rows in sizes
        ],
        compiler_params=pltpu.CompilerParams(vmem_limit_bytes=VMEM_LIMIT),
        cost_estimate=pl.CostEstimate(flops=blk, bytes_accessed=blk, transcendentals=0),
        name="pack",
    )(
        table,
        front.reshape(part_rows, blk * part_cols, blk),
        updates.reshape(2, part_rows, blk * child_cols, blk),
    )
    return outs[0], outs[1 : 1 + turns], outs[1 + turns :]


def add_units(out_ref, table, front_ref, updates_ref, received, shared, slots, base, part_cols, child_cols, blk):
    for slot in slots:
        cols = slice((slot - base) * blk, (slot - base + 1) * blk)
        out_ref[:, cols] = front_ref[0, pl.ds(slot, blk, stride=part_cols), :]
        for member in range(2):
            turn = table[(member * part_cols + slot) * 2]
            index = table[(member * part_cols + slot) * 2 + 1]

            @pl.when(turn == 0)
            def _():
                out_ref[:, cols] += updates_ref[member, 0, pl.ds(index, blk, stride=child_cols), :]

            @pl.when(turn == SHARED)
            def _():
                out_ref[:, cols] += shared[index]

            for step, ref in enumerate(received):

                @pl.when(turn == step + 1)
                def _():
                    out_ref[:, cols] += ref[index]


def assemble_top(table, front, updates, received, shared):
    part_rows, blk, part_cols = front.shape[0], front.shape[2], front.shape[3]
    child_cols = updates.shape[4]
    slots = range(NP, part_cols)

    def kernel(table, front_ref, updates_ref, one, two, three, shared_ref, out_ref):
        add_units(
            out_ref, table, front_ref, updates_ref, (one, two, three), shared_ref,
            slots, NP, part_cols, child_cols, blk,
        )

    return pl.pallas_call(
        kernel,
        grid_spec=pltpu.PrefetchScalarGridSpec(
            num_scalar_prefetch=1,
            grid=(1,),
            in_specs=[
                pl.BlockSpec((1, blk * part_cols, blk), lambda a, t: (0, 0, 0)),
                pl.BlockSpec((2, 1, blk * child_cols, blk), lambda a, t: (0, 0, 0, 0)),
            ]
            + [pl.BlockSpec(r.shape, lambda a, t: (0, 0, 0)) for r in received]
            + [pl.BlockSpec(shared.shape, lambda a, t: (0, 0, 0))],
            out_specs=pl.BlockSpec((blk, len(slots) * blk), lambda a, t: (0, 0)),
        ),
        out_shape=jax.ShapeDtypeStruct((blk, len(slots) * blk), jnp.float32),
        compiler_params=pltpu.CompilerParams(vmem_limit_bytes=VMEM_LIMIT),
        cost_estimate=pl.CostEstimate(flops=blk, bytes_accessed=blk, transcendentals=0),
        name="assemble",
    )(
        table,
        front.reshape(part_rows, blk * part_cols, blk),
        updates.reshape(2, part_rows, blk * child_cols, blk),
        *received, shared,
    )


def prepare_kernel(
    part_cols, child_cols, blk, row_count, col_count, table, square_table, place,
    front_ref, updates_ref, own, chip, core, both, inverse_ref, lower_ref,
    out_ref, left_ref, inv_high, inv_low, units, sum_ref, panel_ref,
):
    step = pl.program_id(0)
    columns = [pl.multiple_of((s * col_count + place[1]) * blk, blk) for s in range(NP)]
    size = inverse_ref.shape[0]

    @pl.when(step == 0)
    def _():
        inv_high[...], inv_low[...] = split(inverse_ref[...])
        out_ref[...] = jnp.zeros_like(out_ref)
        begin = pl.multiple_of(place[0] * blk, blk)
        for s in range(NP):
            out_ref[0, pl.ds(s, blk, stride=part_cols), :] = lower_ref[
                pl.ds(begin, blk), pl.ds(columns[s], blk)
            ]

    @pl.when(step > 0)
    def _():
        width = own.shape[0]
        for ref, owner in ((own, place[1]), (chip, place[2]), (core, place[3]), (both, place[4])):
            for i in range(width):
                units[owner * width + i] = ref[i]
        for q in range(row_count):
            total = units[(q % col_count) * width + 4 + q // col_count]
            for member in range(2):
                entry = 2 * (member * row_count + q)
                total = total + units[square_table[entry]] * square_table[entry + 1].astype(
                    jnp.float32
                )
            panel_ref[:, q * blk : (q + 1) * blk] = total
        add_units(
            sum_ref, table, front_ref, updates_ref, (), units,
            range(NP, part_cols), 0, part_cols, child_cols, blk,
        )
        panel_pair = split(panel_ref[...])
        for begin in range(0, size, 2 * blk):
            end = begin + 2 * blk
            left_ref[:, begin:end] = product3(
                tuple(p[:, :end] for p in panel_pair),
                (inv_high[begin:end, :end], inv_low[begin:end, :end]),
                True,
            )
        for slot in range(NP, part_cols):
            out_ref[0, pl.ds(slot, blk, stride=part_cols), :] = sum_ref[
                :, slot * blk : (slot + 1) * blk
            ]
        for s in range(NP):
            out_ref[0, pl.ds(s, blk, stride=part_cols), :] = left_ref[:, pl.ds(columns[s], blk)]


def prepare(table, square_table, place, front, updates, gathered, inverse, lower, row_count, col_count):
    part_rows, blk, part_cols = front.shape[0], front.shape[2], front.shape[3]
    child_cols = updates.shape[4]
    size = inverse.shape[0]

    def resident(shape):
        return pl.BlockSpec(shape, lambda a, t, q, p: (0, 0), pipeline_mode=pl.Buffered(1))

    return pl.pallas_call(
        functools.partial(prepare_kernel, part_cols, child_cols, blk, row_count, col_count),
        grid_spec=pltpu.PrefetchScalarGridSpec(
            num_scalar_prefetch=3,
            grid=(part_rows,),
            in_specs=[
                pl.BlockSpec((1, blk * part_cols, blk), lambda a, t, q, p: (a, 0, 0)),
                pl.BlockSpec((2, 1, blk * child_cols, blk), lambda a, t, q, p: (0, a, 0, 0)),
            ]
            + [
                pl.BlockSpec((g.shape[0], blk, blk), lambda a, t, q, p: (0, jnp.maximum(a - 1, 0), 0))
                for g in gathered
            ]
            + [resident((size, size))] * 2,
            out_specs=[
                pl.BlockSpec((1, blk * part_cols, blk), lambda a, t, q, p: (a, 0, 0)),
                pl.BlockSpec((blk, size), lambda a, t, q, p: (jnp.maximum(a - 1, 0), 0)),
            ],
            scratch_shapes=[
                pltpu.VMEM((size, size), jnp.bfloat16),
                pltpu.VMEM((size, size), jnp.bfloat16),
                pltpu.VMEM((4 * (4 + NP), blk, blk), jnp.float32),
                pltpu.VMEM((blk, part_cols * blk), jnp.float32),
                pltpu.VMEM((blk, size), jnp.float32),
            ],
        ),
        out_shape=[
            jax.ShapeDtypeStruct((part_rows, blk * part_cols, blk), jnp.float32),
            jax.ShapeDtypeStruct(((part_rows - 1) * blk, size), jnp.float32),
        ],
        compiler_params=pltpu.CompilerParams(vmem_limit_bytes=VMEM_LIMIT),
        cost_estimate=pl.CostEstimate(flops=blk, bytes_accessed=blk, transcendentals=0),
        name="prepare",
    )(
        table, square_table, place,
        front.reshape(part_rows, blk * part_cols, blk),
        updates.reshape(2, part_rows, blk * child_cols, blk),
        *gathered, inverse, lower,
    )


def trail_kernel(part_cols, blk, given_ref, left_ref, high_ref, low_ref, out_ref):
    left_pair = split(left_ref[...])
    for s in range(NP):
        out_ref[0, pl.ds(s, blk, stride=part_cols), :] = given_ref[
            0, pl.ds(s, blk, stride=part_cols), :
        ]
    for pair in range(NP, part_cols, 2):
        cols = slice((pair - NP) * blk, (pair - NP + 2) * blk)
        trailing = product3(left_pair, (high_ref[:, cols], low_ref[:, cols]))
        for half in range(2):
            slot = pl.ds(pair + half, blk, stride=part_cols)
            out_ref[0, slot, :] = given_ref[0, slot, :] - trailing[:, half * blk : (half + 1) * blk]


def trail(given, left, high, low, part_cols, blk):
    block = pl.BlockSpec((1, blk * part_cols, blk), lambda a: (a + 1, 0, 0))

    def resident(shape):
        return pl.BlockSpec(shape, lambda a: (0, 0), pipeline_mode=pl.Buffered(1))

    return pl.pallas_call(
        functools.partial(trail_kernel, part_cols, blk),
        grid=(given.shape[0] - 1,),
        in_specs=[
            block,
            pl.BlockSpec((blk, left.shape[1]), lambda a: (a, 0)),
            resident(high.shape),
            resident(low.shape),
        ],
        out_specs=block,
        out_shape=jax.ShapeDtypeStruct(given.shape, given.dtype),
        input_output_aliases={0: 0},
        compiler_params=pltpu.CompilerParams(vmem_limit_bytes=VMEM_LIMIT),
        cost_estimate=pl.CostEstimate(flops=blk, bytes_accessed=blk, transcendentals=0),
        name="trail",
    )(given, left, high, low)


def right_rows_kernel(inverse_ref, top_ref, high_ref, low_ref, inv_high, inv_low):
    @pl.when(pl.program_id(0) == 0)
    def _():
        inv_high[...], inv_low[...] = split(inverse_ref[...])

    size = inverse_ref.shape[0]
    top_high, top_low = split(top_ref[...])
    for begin in range(0, size, 256):
        end = begin + 256
        result = product3(
            (inv_high[begin:end, :end], inv_low[begin:end, :end]), (top_high[:end], top_low[:end])
        )
        high_ref[begin:end, :], low_ref[begin:end, :] = split(result)


def right_rows(inverse, top, tile):
    size, cols = top.shape
    out = jax.ShapeDtypeStruct((size, cols), jnp.bfloat16)
    return pl.pallas_call(
        right_rows_kernel,
        grid=(cols // tile,),
        in_specs=[
            pl.BlockSpec((size, size), lambda n: (0, 0)),
            pl.BlockSpec((size, tile), lambda n: (0, n)),
        ],
        out_specs=[pl.BlockSpec((size, tile), lambda n: (0, n))] * 2,
        out_shape=[out, out],
        scratch_shapes=[pltpu.VMEM((size, size), jnp.bfloat16)] * 2,
        compiler_params=pltpu.CompilerParams(vmem_limit_bytes=VMEM_LIMIT),
        cost_estimate=pl.CostEstimate(flops=size, bytes_accessed=size, transcendentals=0),
        name="right",
    )(inverse, top)


def add_last_kernel(part_cols, blk, table, given_ref, one, two, three, out_ref):
    out_ref[...] = given_ref[...]
    for slot in range(NP, part_cols):
        for member in range(2):
            turn = table[(member * part_cols + slot) * 2]
            index = table[(member * part_cols + slot) * 2 + 1]
            for step, ref in enumerate((one, two, three)):

                @pl.when(turn == step + 1)
                def _():
                    out_ref[0, pl.ds(slot, blk, stride=part_cols), :] += ref[index]


def add_last(table, given, received, part_cols, blk):
    part_rows = given.shape[0]
    block = pl.BlockSpec((1, blk * part_cols, blk), lambda a, t: (a + 1, 0, 0))
    return pl.pallas_call(
        functools.partial(add_last_kernel, part_cols, blk),
        grid_spec=pltpu.PrefetchScalarGridSpec(
            num_scalar_prefetch=1,
            grid=(part_rows - 1,),
            in_specs=[block]
            + [pl.BlockSpec((r.shape[0], blk, blk), lambda a, t: (0, a, 0)) for r in received],
            out_specs=block,
        ),
        out_shape=jax.ShapeDtypeStruct(given.shape, given.dtype),
        input_output_aliases={1: 0},
        compiler_params=pltpu.CompilerParams(vmem_limit_bytes=VMEM_LIMIT),
        cost_estimate=pl.CostEstimate(flops=blk, bytes_accessed=blk, transcendentals=0),
        name="add_last",
    )(table, given, *received)


def turn_tables(maps, col_index, col_count, child_cols, part_cols, most, panel_blocks):
    groups = jnp.arange(child_cols, dtype=jnp.int32)
    turn = (maps[:, ::col_count] - col_count * groups[None, :]) % col_count
    flat = jnp.where(groups[None, :] < 2, col_count, turn).T.reshape(-1)
    order = jnp.arange(2 * child_cols, dtype=jnp.int32)
    same = (flat[:, None] == flat[None, :]) & (order[None, :] < order[:, None])
    rank = jnp.sum(same.astype(jnp.int32), axis=1)
    turns = jnp.arange(1, col_count, dtype=jnp.int32)
    counts = jnp.sum((flat[None, :] == turns[:, None]).astype(jnp.int32), axis=1)
    slots = jnp.arange(most, dtype=jnp.int32)
    hot = (flat[None, None, :] == turns[:, None, None]) & (
        rank[None, None, :] == slots[None, :, None]
    )
    chosen = jnp.sum(jnp.where(hot, order[None, None, :], 0), axis=2)
    send = jnp.stack([chosen % 2, chosen // 2], axis=2).reshape(-1)
    rank = rank.reshape(child_cols, 2).T
    spread = jnp.repeat(groups, col_count)

    def look(parents):
        match = maps[:, None, :] == parents[None, :, None]
        group = jnp.sum(jnp.where(match, spread[None, None, :], 0), axis=2)
        source = jnp.sum(
            jnp.where(match, jnp.arange(maps.shape[1], dtype=jnp.int32)[None, None, :], 0), axis=2
        )
        return jnp.any(match, axis=2), group, source

    present, group, source = look(jnp.arange(part_cols, dtype=jnp.int32) * col_count + col_index)
    pick = group[:, :, None] == groups[None, None, :]
    kind = jnp.sum(jnp.where(pick, turn[:, None, :], 0), axis=2)
    index = jnp.sum(jnp.where(pick, rank[:, None, :], 0), axis=2)
    members = jnp.arange(2, dtype=jnp.int32)[:, None]
    index = jnp.where(kind == 0, group, index)
    shared = (group < 2) & (kind > 0)
    index = jnp.where(shared, (source % col_count) * (4 + NP) + 2 * members + group, index)
    kind = jnp.where(shared, SHARED, kind)
    kind = jnp.where(present, kind, col_count)
    place = jnp.stack([kind, index], axis=2).reshape(-1)
    present, group, source = look(jnp.arange(panel_blocks, dtype=jnp.int32))
    group = jnp.minimum(group, 1)
    unit = (source % col_count) * (4 + NP) + 2 * members + group
    square = jnp.stack([unit, present.astype(jnp.int32)], axis=2).reshape(-1)
    return send, place, square, counts


def main_branch(level, most, row_count, front, updates, send, place, square_table, where):
    blk, part_cols = front.shape[2], front.shape[3]
    col_count = 4
    columns = range(col_count)

    def swap(value, mask):
        return lax.ppermute(value, "col", [(c, c ^ mask) for c in columns])

    def turned(value, turn):
        return lax.ppermute(value, "col", [(c, (c + turn) % col_count) for c in columns])

    units, early, late = pack_turns(send, front, updates, LEVELS[level], most)
    given, *early = send_head(front, updates, early, level + 1)
    soon = min((1, 3), key=lambda turn: abs(LEVELS[level][turn - 1] - 6))
    square, shared, arrived = gather_square(
        square_table, given, late[soon - 1], soon, row_count, len(LEVELS) + level + 1
    )
    units, late, square = lax.optimization_barrier((units, late, square))
    chip, core = swap(units, 2), swap(units, 1)
    top = assemble_top(place, front, updates, early, shared)
    top, square = lax.optimization_barrier((top, square))
    top = lax.all_gather(top, "row", axis=0, tiled=True)
    lower, inverse = factorize(square, blk)
    chip, core, inverse = lax.optimization_barrier((chip, core, inverse))
    both = swap(chip, 1)
    late = [
        arrived if turn == soon else turned(late[turn - 1], turn) for turn in range(1, col_count)
    ]
    result, left = prepare(
        place, square_table, where, front, updates, (units, chip, core, both), inverse, lower,
        row_count, col_count,
    )
    left, top = lax.optimization_barrier((left, top))
    high, low = right_rows(inverse, top, 2 * blk)
    result = trail(result, left, high, low, part_cols, blk)
    result, late = lax.optimization_barrier((result, late))
    return add_last(place, result, late, part_cols, blk)


def body(row_count, col_count, front, updates, maps):
    part_rows = front.shape[0]
    if part_rows == 1 or row_count != NP * col_count or col_count != 4:
        return simple_body(front, updates, maps)
    row_index = lax.axis_index("row")
    col_index = lax.axis_index("col")
    front = front.reshape(front.shape[0], 1, *front.shape[2:4], front.shape[5])
    blk, part_cols = front.shape[2], front.shape[3]
    child_cols = updates.shape[4]
    most = child_cols
    send, place, square_table, counts = turn_tables(
        maps, col_index, col_count, child_cols, part_cols, most, row_count
    )
    where = jnp.stack([row_index] + [col_index ^ mask for mask in (0, 2, 1, 3)]).astype(jnp.int32)
    branches = [functools.partial(main_branch, level, most, row_count) for level in range(len(LEVELS))]
    fits = jnp.all(counts[None, :] <= jnp.asarray(LEVELS, jnp.int32), axis=1)
    level = jnp.argmax(fits).astype(jnp.int32)
    operands = (front, updates, send, place, square_table, where)
    if len(branches) == 1:
        result = branches[0](*operands)
    else:
        result = lax.switch(level, branches, *operands)
    return result.reshape(part_rows, 1, blk, part_cols, 1, blk)


def solution(mesh):
    return jax.shard_map(
        functools.partial(body, mesh.shape["row"], mesh.shape["col"]),
        mesh=mesh,
        in_specs=(
            P(None, "row", None, None, "col", None),
            P(None, None, "row", None, None, "col", None),
            P(),
        ),
        out_specs=P(None, "row", None, None, "col", None),
        check_vma=False,
    )
```

```python
import functools
import typing

import jax
import jax.numpy as jnp
from jax import lax
from jax.experimental import pallas as pl
from jax.experimental.pallas import tpu as pltpu
from jax.sharding import PartitionSpec as P

NP = 2
highest = lax.Precision.HIGHEST
VMEM_LIMIT = 56 * 1024 * 1024
MESH = pl.DeviceIdType.MESH
SHARED = 5
LEVELS = (
    (5, 4, 7), (9, 2, 8), (8, 5, 6), (5, 6, 9), (8, 8, 4), (10, 4, 10), (6, 10, 5), (9, 8, 8),
    (12, 12, 12),
)


def split(value):
    high = value.astype(jnp.bfloat16)
    low = (value - high.astype(jnp.float32)).astype(jnp.bfloat16)
    return high, low


def dims(transposed):
    return (((1,), (1 if transposed else 0,)), ((), ()))


def product3(left_pair, right_pair, transposed=False):
    def one(a, b):
        return lax.dot_general(a, b, dims(transposed), preferred_element_type=jnp.float32)

    return (
        one(left_pair[0], right_pair[0])
        + one(left_pair[0], right_pair[1])
        + one(left_pair[1], right_pair[0])
    )


def product(a, b, transposed=False):
    return lax.dot_general(
        a, b, dims(transposed), precision=highest, preferred_element_type=jnp.float32
    )


def pack_kernel(child_cols, cap, blk, table, updates_ref, one_ref, two_ref, three_ref):
    for turn, out_ref in enumerate((one_ref, two_ref, three_ref)):
        for member in range(2):
            for slot in range(cap):
                source = table[(turn + 1) * 2 * cap + member * cap + slot]
                out_ref[member * cap + slot] = updates_ref[
                    member, 0, pl.ds(source, blk, stride=child_cols), :
                ]


def pack(table, updates, cap, begin, count):
    part_rows, blk, child_cols = updates.shape[1], updates.shape[3], updates.shape[4]
    flat = updates.reshape(2, part_rows, blk * child_cols, blk)
    return pl.pallas_call(
        functools.partial(pack_kernel, child_cols, cap, blk),
        grid_spec=pltpu.PrefetchScalarGridSpec(
            num_scalar_prefetch=1,
            grid=(count,),
            in_specs=[
                pl.BlockSpec((2, 1, blk * child_cols, blk), lambda a, t: (0, a + begin, 0, 0))
            ],
            out_specs=[pl.BlockSpec((2 * cap, blk, blk), lambda a, t: (0, a, 0))] * 3,
        ),
        out_shape=[jax.ShapeDtypeStruct((2 * cap, count * blk, blk), jnp.float32)] * 3,
        compiler_params=pltpu.CompilerParams(vmem_limit_bytes=VMEM_LIMIT),
        name="pack",
    )(table, flat)


def add_children(out_ref, table, front_ref, updates_ref, received, slots, part_cols, child_cols, blk):
    for slot in slots:
        cols = slice(slot * blk, (slot + 1) * blk)
        out_ref[:, cols] = front_ref[0, pl.ds(slot, blk, stride=part_cols), :]
        for member in range(2):
            turn = table[(member * part_cols + slot) * 2]
            index = table[(member * part_cols + slot) * 2 + 1]

            @pl.when(turn == 0)
            def _():
                out_ref[:, cols] += updates_ref[member, 0, pl.ds(index, blk, stride=child_cols), :]

            for step in range(3):

                @pl.when(turn == step + 1)
                def _():
                    out_ref[:, cols] += received[step][index]


def assemble(table, front, updates, received, begin, count, width):
    part_rows, blk, part_cols = front.shape[0], front.shape[2], front.shape[3]
    child_cols = updates.shape[4]
    slots = received[0].shape[0]

    def kernel(table, front_ref, updates_ref, one, two, three, out_ref):
        add_children(
            out_ref, table, front_ref, updates_ref, (one, two, three),
            range(width), part_cols, child_cols, blk,
        )

    return pl.pallas_call(
        kernel,
        grid_spec=pltpu.PrefetchScalarGridSpec(
            num_scalar_prefetch=1,
            grid=(count,),
            in_specs=[
                pl.BlockSpec((1, blk * part_cols, blk), lambda a, t: (a + begin, 0, 0)),
                pl.BlockSpec((2, 1, blk * child_cols, blk), lambda a, t: (0, a + begin, 0, 0)),
            ]
            + [pl.BlockSpec((slots, blk, blk), lambda a, t: (0, a, 0))] * 3,
            out_specs=pl.BlockSpec((blk, width * blk), lambda a, t: (a, 0)),
        ),
        out_shape=jax.ShapeDtypeStruct((count * blk, width * blk), jnp.float32),
        compiler_params=pltpu.CompilerParams(vmem_limit_bytes=VMEM_LIMIT),
        name="assemble",
    )(
        table,
        front.reshape(part_rows, blk * part_cols, blk),
        updates.reshape(2, part_rows, blk * child_cols, blk),
        *received,
    )


def eliminate(block):
    size = block.shape[0]
    group = 8
    tiles = size // group
    shape = (group, size)
    row_ids = lax.broadcasted_iota(jnp.int32, (size, size), 0)
    col_ids = lax.broadcasted_iota(jnp.int32, (size, size), 1)
    local = lax.broadcasted_iota(jnp.int32, shape, 0)
    start = (row_ids == col_ids).astype(jnp.float32)
    upper = [block[group * t : group * (t + 1), :] for t in range(tiles)]
    solved = [start[group * t : group * (t + 1), :] for t in range(tiles)]
    for h in range(tiles):
        def column(t, j):
            return jnp.broadcast_to(upper[t][:, group * h + j : group * h + j + 1], shape)
        home = [column(h, j) for j in range(group)]
        pivot = {
            (i, j): jnp.broadcast_to(home[j][i : i + 1, :], shape)
            for j in range(group) for i in range(j, group)
        }
        scale, ratio = [], {}
        for j in range(group):
            scale.append(1.0 / pivot[j, j])
            for i in range(j + 1, group):
                ratio[i, j] = pivot[i, j] * scale[j]
            for k in range(j + 1, group):
                for i in range(k, group):
                    pivot[i, k] = pivot[i, k] - ratio[i, j] * pivot[k, j]
        upper_rows, solved_rows = [], []
        for j in range(group):
            u = jnp.broadcast_to(upper[h][j : j + 1, :], shape)
            s = jnp.broadcast_to(solved[h][j : j + 1, :], shape)
            for i in range(j):
                u = u - ratio[j, i] * upper_rows[i]
                s = s - ratio[j, i] * solved_rows[i]
            upper_rows.append(u)
            solved_rows.append(s)
        for t in range(h, tiles):
            if t == h:
                u, s = upper_rows[0], solved_rows[0]
                for j in range(1, group):
                    u = jnp.where(local == j, upper_rows[j], u)
                    s = jnp.where(local == j, solved_rows[j], s)
                upper[t], solved[t] = u, s
                continue
            factors = []
            for j in range(group):
                c = column(t, j)
                for i in range(j):
                    c = c - factors[i] * pivot[j, i]
                factors.append(c * scale[j])
            for j in range(group):
                upper[t] = upper[t] - factors[j] * upper_rows[j]
                solved[t] = solved[t] - factors[j] * solved_rows[j]
    upper = jnp.concatenate(upper, axis=0)
    solved = jnp.concatenate(solved, axis=0)
    diagonal = jnp.sum(jnp.where(row_ids == col_ids, upper, 0.0), axis=1, keepdims=True)
    scale = 1.0 / jnp.sqrt(diagonal)
    lower = jnp.where(col_ids >= row_ids, upper * scale, 0.0).T
    return lower, solved * scale

def factor_kernel(blk, square_ref, lower_ref, inverse_ref, work):
    size = square_ref.shape[0]
    count = size // blk
    work[...] = square_ref[...]
    lower_ref[...] = jnp.zeros_like(lower_ref)
    inverse_ref[...] = jnp.zeros_like(inverse_ref)

    def spread(k, diag_inverse):
        begin, end = k * blk, (k + 1) * blk
        here = slice(begin, end)
        inverse_pair = split(diag_inverse)
        if k:
            done = product3(inverse_pair, split(inverse_ref[here, :begin]))
            inverse_ref[here, :begin] = done
        inverse_ref[here, here] = diag_inverse
        if end == size:
            return
        row_high, row_low = split(inverse_ref[here, :end])
        left_high, left_low = [], []
        for q in range(end, size, 256):
            top = min(q + 256, size)
            left = product3(split(work[q:top, here]), inverse_pair, True)
            lower_ref[q:top, here] = left
            high, low = split(left)
            left_high.append(high)
            left_low.append(low)
        high = jnp.concatenate(left_high, axis=0)
        low = jnp.concatenate(left_low, axis=0)
        for q in range(end, size, 256):
            top = min(q + 256, size)
            pair = high[q - end : top - end], low[q - end : top - end]
            below = high[: top - end], low[: top - end]
            work[q:top, end:top] -= product3(pair, below, True)
            inverse_ref[q:top, :end] -= product3(pair, (row_high, row_low))

    def step(k, carry):
        begin = pl.multiple_of(k * blk, blk)
        here = pl.ds(begin, blk)
        diag_lower, diag_inverse = eliminate(work[here, here])
        lower_ref[here, here] = diag_lower
        for t in range(count):
            pl.when(k == t)(functools.partial(spread, t, diag_inverse))
        return carry

    lax.fori_loop(0, count, step, 0)


def factorize(square, blk):
    size = square.shape[0]
    shape = jax.ShapeDtypeStruct((size, size), jnp.float32)
    return pl.pallas_call(
        functools.partial(factor_kernel, blk),
        out_shape=[shape, shape],
        scratch_shapes=[pltpu.VMEM((size, size), jnp.float32)],
        compiler_params=pltpu.CompilerParams(vmem_limit_bytes=VMEM_LIMIT),
        cost_estimate=pl.CostEstimate(flops=size, bytes_accessed=size, transcendentals=0),
        name="factorize",
    )(square)


def right_kernel(inverse_ref, top_ref, high_ref, low_ref, inv_high, inv_low):
    @pl.when(pl.program_id(0) == 0)
    def _():
        inv_high[...], inv_low[...] = split(inverse_ref[...])

    result = product3((inv_high[...], inv_low[...]), split(top_ref[...]))
    high_ref[...], low_ref[...] = split(result)


def right_side(inverse, top, tile):
    size, cols = top.shape
    out = jax.ShapeDtypeStruct((size, cols), jnp.bfloat16)
    return pl.pallas_call(
        right_kernel,
        grid=(cols // tile,),
        in_specs=[
            pl.BlockSpec((size, size), lambda n: (0, 0)),
            pl.BlockSpec((size, tile), lambda n: (0, n)),
        ],
        out_specs=[pl.BlockSpec((size, tile), lambda n: (0, n))] * 2,
        out_shape=[out, out],
        scratch_shapes=[pltpu.VMEM((size, size), jnp.bfloat16)] * 2,
        compiler_params=pltpu.CompilerParams(vmem_limit_bytes=VMEM_LIMIT),
        cost_estimate=pl.CostEstimate(flops=size, bytes_accessed=size, transcendentals=0),
        name="right",
    )(inverse, top)


def finish_kernel(
    part_cols, child_cols, blk, row_count, col_count, first, table, place,
    panel_ref, front_ref, updates_ref, one, two, three, inverse_ref, lower_ref, high_ref, low_ref,
    out_ref, inv_high, inv_low, left_ref, sum_ref,
):
    step = pl.program_id(0)
    block_row = step * row_count + place[0]
    panel_blocks = NP * col_count
    inside = block_row < panel_blocks
    columns = [pl.multiple_of((s * col_count + place[1]) * blk, blk) for s in range(NP)]

    @pl.when(step == 0)
    def _():
        inv_high[...], inv_low[...] = split(inverse_ref[...])

    @pl.when(jnp.logical_not(inside))
    def _():
        add_children(
            sum_ref, table, front_ref, updates_ref, (one, two, three),
            range(NP, part_cols), part_cols, child_cols, blk,
        )
        panel = jnp.concatenate(
            [
                panel_ref[c, :, s * blk : (s + 1) * blk]
                for s in range(NP)
                for c in range(col_count)
            ],
            axis=1,
        )
        left_ref[...] = product3(split(panel), (inv_high[...], inv_low[...]), True)
        left_pair = split(left_ref[...])
        for pair in range(NP, part_cols, 2):
            cols = slice((pair - NP) * blk, (pair - NP + 2) * blk)
            trailing = product3(left_pair, (high_ref[:, cols], low_ref[:, cols]))
            updated = sum_ref[:, pair * blk : (pair + 2) * blk] - trailing
            for half in range(2):
                out_ref[0, pl.ds(pair + half, blk, stride=part_cols), :] = updated[
                    :, half * blk : (half + 1) * blk
                ]
        for s in range(NP):
            out_ref[0, pl.ds(s, blk, stride=part_cols), :] = left_ref[:, pl.ds(columns[s], blk)]

    @pl.when(inside)
    def _():
        out_ref[...] = jnp.zeros_like(out_ref)
        begin = pl.multiple_of(block_row * blk, blk)
        for s in range(NP):
            out_ref[0, pl.ds(s, blk, stride=part_cols), :] = lower_ref[
                pl.ds(begin, blk), pl.ds(columns[s], blk)
            ]


def finish(table, place, panel, front, updates, received, inverse, lower, high, low, row_count, first):
    part_rows, blk, part_cols = front.shape[0], front.shape[2], front.shape[3]
    child_cols = updates.shape[4]
    size = inverse.shape[0]
    slots = received[0].shape[0]
    col_count = panel.shape[0]

    def resident(shape):
        return pl.BlockSpec(shape, lambda a, t, p: (0, 0), pipeline_mode=pl.Buffered(1))

    def late(a, t, p):
        return (0, jnp.maximum(a - first, 0), 0)

    return pl.pallas_call(
        functools.partial(finish_kernel, part_cols, child_cols, blk, row_count, col_count, first),
        grid_spec=pltpu.PrefetchScalarGridSpec(
            num_scalar_prefetch=2,
            grid=(part_rows,),
            in_specs=[
                pl.BlockSpec((col_count, blk, NP * blk), late),
                pl.BlockSpec((1, blk * part_cols, blk), lambda a, t, p: (a, 0, 0)),
                pl.BlockSpec((2, 1, blk * child_cols, blk), lambda a, t, p: (0, a, 0, 0)),
            ]
            + [pl.BlockSpec((slots, blk, blk), late)] * 3
            + [
                resident((size, size)),
                resident((size, size)),
                resident(high.shape),
                resident(low.shape),
            ],
            out_specs=pl.BlockSpec((1, blk * part_cols, blk), lambda a, t, p: (a, 0, 0)),
            scratch_shapes=[
                pltpu.VMEM((size, size), jnp.bfloat16),
                pltpu.VMEM((size, size), jnp.bfloat16),
                pltpu.VMEM((blk, size), jnp.float32),
                pltpu.VMEM((blk, part_cols * blk), jnp.float32),
            ],
        ),
        out_shape=jax.ShapeDtypeStruct((part_rows, blk * part_cols, blk), jnp.float32),
        compiler_params=pltpu.CompilerParams(vmem_limit_bytes=VMEM_LIMIT),
        name="finish",
    )(
        table, place, panel,
        front.reshape(part_rows, blk * part_cols, blk),
        updates.reshape(2, part_rows, blk * child_cols, blk),
        *received, inverse, lower, high, low,
    )


def tables(maps, col_index, col_count, child_cols, part_cols, cap):
    offsets = maps[:, ::col_count] - col_count * jnp.arange(child_cols, dtype=jnp.int32)[None, :]
    turn = offsets % col_count
    groups = jnp.arange(child_cols, dtype=jnp.int32)
    same = (turn[:, :, None] == turn[:, None, :]) & (groups[None, None, :] < groups[None, :, None])
    rank = jnp.sum(same.astype(jnp.int32), axis=2)
    turns = jnp.arange(col_count, dtype=jnp.int32)
    slots = jnp.arange(cap, dtype=jnp.int32)
    hot = (turn[None, :, None, :] == turns[:, None, None, None]) & (
        rank[None, :, None, :] == slots[None, None, :, None]
    )
    send = jnp.sum(jnp.where(hot, groups[None, None, None, :], 0), axis=3).reshape(-1)
    parents = jnp.arange(part_cols, dtype=jnp.int32) * col_count + col_index
    match = maps[:, None, :] == parents[None, :, None]
    spread = jnp.repeat(groups, col_count)
    group = jnp.sum(jnp.where(match, spread[None, None, :], 0), axis=2)
    present = jnp.any(match, axis=2)
    pick = group[:, :, None] == groups[None, None, :]
    kind = jnp.sum(jnp.where(pick, turn[:, None, :], 0), axis=2)
    order = jnp.sum(jnp.where(pick, rank[:, None, :], 0), axis=2)
    order = jnp.where(kind == 0, group, order + cap * jnp.arange(2, dtype=jnp.int32)[:, None])
    kind = jnp.where(present, kind, col_count)
    place = jnp.stack([kind, order], axis=2).reshape(-1)
    return send, place


def gather_top(piece, row_count, row_index, panel_blocks):
    if row_count == panel_blocks:
        return lax.all_gather(piece, "row", axis=0, tiled=True)
    ids = jnp.arange(panel_blocks, dtype=jnp.int32)
    kept = jnp.where((ids == row_index)[:, None, None], piece[None], 0.0)
    return lax.psum(kept, "row").reshape(panel_blocks * piece.shape[0], piece.shape[1])


def simple_body(front, updates, maps):
    row_count = lax.axis_size("row")
    col_count = lax.axis_size("col")
    row_index = lax.axis_index("row")
    col_index = lax.axis_index("col")
    front = front.reshape(front.shape[0], 1, *front.shape[2:4], front.shape[5])
    blk, part_cols = front.shape[2], front.shape[3]
    child_cols = updates.shape[4]
    cap = child_cols // 2
    panel_blocks = NP * col_count
    send, place = tables(maps, col_index, col_count, child_cols, part_cols, cap)
    part_rows = front.shape[0]
    first = 1 if part_rows > 1 and row_count == panel_blocks else part_rows

    def exchange(outgoing):
        return [
            lax.ppermute(
                outgoing[turn - 1], "col", [(c, (c + turn) % col_count) for c in range(col_count)]
            )
            for turn in range(1, col_count)
        ]

    early = exchange(pack(send, updates, cap, 0, first))
    if first < part_rows:
        outgoing = pack(send, updates, cap, first, part_rows - first)
        early, outgoing = lax.optimization_barrier((early, outgoing))
        received = exchange(outgoing)
    else:
        received = early
    head = assemble(place, front, updates, early, 0, 1, part_cols)
    square = jnp.concatenate(
        [
            lax.all_gather(head[:, s * blk : (s + 1) * blk], "col", axis=1, tiled=True)
            for s in range(NP)
        ],
        axis=1,
    )
    square = gather_top(square, row_count, row_index, panel_blocks)
    rest, square = lax.optimization_barrier((head[:, NP * blk :], square))
    top = gather_top(rest, row_count, row_index, panel_blocks)
    lower, inverse = factorize(square, blk)
    high, low = right_side(inverse, top, 2 * blk)
    received, high, low = lax.optimization_barrier((received, high, low))
    late = first if first < part_rows else 0
    panel = assemble(place, front, updates, received, late, part_rows - late, NP)
    panel = lax.all_gather(panel, "col", axis=0)
    where = jnp.stack([row_index, col_index]).astype(jnp.int32)
    result = finish(
        place, where, panel, front, updates, received, inverse, lower, high, low, row_count, late
    )
    return result.reshape(front.shape[0], 1, blk, part_cols, 1, blk)


def send_kernel(
    blk, caps, most, table, front_ref, updates_ref, units_ref, got_one, got_two, got_three,
    panel_ref, late_one, late_two, late_three,
    front_part, updates_part, columns, units, first, stage, stage_one, stage_two, stage_three,
    local, keep_sem, send, recv, out_sem,
):
    row, col = lax.axis_index("row"), lax.axis_index("col")
    part_rows = front_ref.shape[0]
    part_cols = front_part.shape[1] // blk
    child_cols = updates_part.shape[2] // blk
    width = units.shape[0]
    stages = (stage_one, stage_two, stage_three)

    def loads(a, side):
        copies = [pltpu.make_async_copy(front_ref.at[a], front_part.at[side], local.at[side, 0])]
        for member in range(2):
            copies.append(
                pltpu.make_async_copy(
                    updates_ref.at[member, a], updates_part.at[side, member],
                    local.at[side, 1 + member],
                )
            )
        return copies

    for load in loads(0, 0):
        load.start()
    for load in loads(1, 1):
        load.start()
    others = [lax.rem(col + turn, 4) for turn in range(1, 4)]
    barrier = pltpu.get_barrier_semaphore()
    for other in others:
        pl.semaphore_signal(barrier, inc=1, device_id=(row, other), device_id_type=MESH)

    def spread(side, target):
        for member in range(2):
            for g in range(child_cols):
                columns[member * child_cols + g] = updates_part[
                    side, member, pl.ds(g, blk, stride=child_cols), :
                ]
        for member in range(2):
            for g in range(2):
                target[member * 2 + g] = columns[member * child_cols + g]
        for s in range(NP):
            target[4 + s] = front_part[side, pl.ds(s, blk, stride=part_cols), :]

    for load in loads(0, 0):
        load.wait()
    spread(0, units)
    pl.semaphore_wait(barrier, 3)

    def remote(source, target, index, device):
        return pltpu.make_async_remote_copy(
            src_ref=source, dst_ref=target, send_sem=send.at[index], recv_sem=recv.at[index],
            device_id=(row, device), device_id_type=MESH,
        )

    across = remote(units, units_ref.at[pl.ds(col * width, width)], 3, others[1])
    across.start()
    keep = pltpu.make_async_copy(units, units_ref.at[pl.ds(col * width, width)], keep_sem)
    keep.start()
    moves = []
    begin = 0
    for turn, target in enumerate((got_one, got_two, got_three)):
        for slot in range(caps[turn]):
            first[begin + slot] = columns[table[turn * most + slot]]
        moves.append(remote(first.at[pl.ds(begin, caps[turn])], target, turn, others[turn]))
        moves[-1].start()
        begin += caps[turn]

    def stores(a, side):
        rows = pl.ds(pl.multiple_of((a - 1) * blk, blk), blk)
        copies = [pltpu.make_async_copy(stage.at[side], panel_ref.at[:, rows, :], out_sem.at[side, 0])]
        for turn, target in enumerate((late_one, late_two, late_three)):
            copies.append(
                pltpu.make_async_copy(
                    stages[turn].at[side], target.at[:, rows, :], out_sem.at[side, 1 + turn]
                )
            )
        return copies

    def step(a, carry):
        side = lax.rem(a, 2)
        for load in loads(a, side):
            load.wait()

        @pl.when(a + 1 < part_rows)
        def _():
            for load in loads(a + 1, 1 - side):
                load.start()

        @pl.when(a > 2)
        def _():
            for store in stores(a - 2, side):
                store.wait()

        spread(side, stage.at[side])
        for turn in range(3):
            for slot in range(caps[turn]):
                stages[turn][side, slot] = columns[table[turn * most + slot]]
        for store in stores(a, side):
            store.start()
        return carry

    lax.fori_loop(1, part_rows, step, 0)
    for a in range(max(1, part_rows - 2), part_rows):
        for store in stores(a, a % 2):
            store.wait()
    keep.wait()
    across.wait_send()
    remote(units, units_ref.at[pl.ds(others[1] * width, width)], 3, others[1]).wait_recv()
    for move in moves:
        move.wait()


def send_head(table, front, updates, caps, most, identity):
    part_rows, blk, part_cols = front.shape[0], front.shape[2], front.shape[3]
    child_cols = updates.shape[4]
    anywhere = pl.BlockSpec(memory_space=pl.ANY)
    width = 4 + NP
    rest = (part_rows - 1) * blk
    shapes = [(4 * width, blk, blk)] + [(cap, blk, blk) for cap in caps]
    shapes += [(width, rest, blk)] + [(cap, rest, blk) for cap in caps]
    outs = pl.pallas_call(
        functools.partial(send_kernel, blk, caps, most),
        in_specs=[pl.BlockSpec(memory_space=pltpu.SMEM), anywhere, anywhere],
        out_specs=[anywhere] * 8,
        out_shape=[jax.ShapeDtypeStruct(shape, jnp.float32) for shape in shapes],
        scratch_shapes=[
            pltpu.VMEM((2, blk * part_cols, blk), jnp.float32),
            pltpu.VMEM((2, 2, blk * child_cols, blk), jnp.float32),
            pltpu.VMEM((2 * child_cols, blk, blk), jnp.float32),
            pltpu.VMEM((width, blk, blk), jnp.float32),
            pltpu.VMEM((sum(caps), blk, blk), jnp.float32),
            pltpu.VMEM((2, width, blk, blk), jnp.float32),
        ]
        + [pltpu.VMEM((2, cap, blk, blk), jnp.float32) for cap in caps]
        + [
            pltpu.SemaphoreType.DMA((2, 3)),
            pltpu.SemaphoreType.DMA,
            pltpu.SemaphoreType.DMA((4,)),
            pltpu.SemaphoreType.DMA((4,)),
            pltpu.SemaphoreType.DMA((2, 4)),
        ],
        compiler_params=pltpu.CompilerParams(
            vmem_limit_bytes=VMEM_LIMIT, collective_id=identity, has_side_effects=True
        ),
        cost_estimate=pl.CostEstimate(flops=blk, bytes_accessed=blk, transcendentals=0),
        name="send",
    )(
        table,
        front.reshape(part_rows, blk * part_cols, blk),
        updates.reshape(2, part_rows, blk * child_cols, blk),
    )
    return outs[0], outs[1:4], outs[4], outs[5:]


def square_kernel(
    blk, row_count, turn, base, table, given_ref, sent_ref, square_ref, units_ref, got_ref,
    work, units, local, line_send, line_recv, col_send, col_recv, core_send, core_recv,
    turn_send, turn_recv,
):
    row, col = lax.axis_index("row"), lax.axis_index("col")
    width = units.shape[0] // 4
    half = row_count // 2
    core = lax.rem(col, 2)
    other_core = col + 1 - 2 * core
    other_chip = lax.rem(col + 2, 4)
    diagonal = lax.rem(other_core + 2, 4)

    def section(ref, owner):
        return ref.at[pl.ds(owner * width, width)]

    loads = []
    for index, owner in enumerate((col, other_chip)):
        loads.append(
            pltpu.make_async_copy(
                section(given_ref, owner), section(units, owner), local.at[index]
            )
        )
        loads[-1].start()

    def ring_row(position):
        position = lax.rem(position + row_count, row_count)
        return jnp.where(position < half, 2 * position, 2 * (row_count - position) - 1)

    place = jnp.where(lax.rem(row, 2) == 0, row // 2, row_count - 1 - row // 2)
    right, left = ring_row(place + 1), ring_row(place - 1)
    barrier = pltpu.get_barrier_semaphore()
    for device in (
        (row, other_core), (row, other_chip), (row, diagonal), (right, col), (left, col)
    ):
        pl.semaphore_signal(barrier, inc=1, device_id=device, device_id_type=MESH)
    for load in loads:
        load.wait()
    pl.semaphore_wait(barrier, 5)
    turned = pltpu.make_async_remote_copy(
        src_ref=sent_ref, dst_ref=got_ref, send_sem=turn_send, recv_sem=turn_recv,
        device_id=(row, lax.rem(col + turn, 4)), device_id_type=MESH,
    )
    turned.start()

    def share(owner, index):
        part = section(units, owner)
        return pltpu.make_async_remote_copy(
            src_ref=part, dst_ref=part, send_sem=col_send.at[index], recv_sem=col_recv.at[index],
            device_id=(row, other_core), device_id_type=MESH,
        )

    shares = [share(col, 0), share(other_chip, 1)]
    for move in shares:
        move.start()
    share(other_core, 0).wait_recv()
    share(diagonal, 1).wait_recv()
    here = pl.multiple_of(row * blk, blk)
    for q in range(row_count):
        s, owner = q // 4, q % 4
        total = units[owner * width + 4 + s]
        for member in range(2):
            entry = base + 2 * (member * row_count + q)
            total = total + units[table[entry]] * table[entry + 1].astype(jnp.float32)
        work[pl.ds(here, blk), q * blk : (q + 1) * blk] = total

    cols = work.shape[1] // 2

    def part(position, side):
        begin = pl.multiple_of(ring_row(position) * blk, blk)
        return work.at[pl.ds(begin, blk), pl.ds(pl.multiple_of(side * cols, cols), cols)]

    def copy(ref, device, send, recv):
        return pltpu.make_async_remote_copy(
            src_ref=ref, dst_ref=ref, send_sem=send, recv_sem=recv,
            device_id=device, device_id_type=MESH,
        )

    pending = []
    for step in range(half):
        ways = range(2 if step < half - 1 else 1)
        for way in ways:
            position = place - step if way == 0 else place + step
            target = right if way == 0 else left
            move = copy(
                part(position, core), (target, col), line_send.at[way, step], line_recv.at[way, step]
            )
            move.start()
            pending.append(move)
        for way in ways:
            origin = place - step - 1 if way == 0 else place + step + 1
            landed = part(origin, core)
            copy(
                landed, (right, col), line_send.at[way, step], line_recv.at[way, step]
            ).wait_recv()
            forward = copy(
                landed, (row, other_core), core_send.at[way, step], core_recv.at[way, step]
            )
            forward.start()
            pending.append(forward)
    for way in range(2):
        for step in range(half - way):
            origin = place - step - 1 if way == 0 else place + step + 1
            copy(
                part(origin, 1 - core), (row, other_core),
                core_send.at[way, step], core_recv.at[way, step],
            ).wait_recv()
    stores = [
        pltpu.make_async_copy(work, square_ref, local.at[0]),
        pltpu.make_async_copy(units, units_ref, local.at[1]),
    ]
    for store in stores:
        store.start()
    for move in shares + pending:
        move.wait_send()
    for store in stores:
        store.wait()
    turned.wait()


def gather_square(table, base, given, sent, turn, row_count, identity):
    blk = given.shape[1]
    size = row_count * blk
    half = row_count // 2
    anywhere = pl.BlockSpec(memory_space=pl.ANY)
    return pl.pallas_call(
        functools.partial(square_kernel, blk, row_count, turn, base),
        in_specs=[pl.BlockSpec(memory_space=pltpu.SMEM), anywhere, anywhere],
        out_specs=[anywhere] * 3,
        out_shape=[
            jax.ShapeDtypeStruct((size, size), jnp.float32),
            jax.ShapeDtypeStruct(given.shape, jnp.float32),
            jax.ShapeDtypeStruct(sent.shape, jnp.float32),
        ],
        scratch_shapes=[
            pltpu.VMEM((size, size), jnp.float32),
            pltpu.VMEM(given.shape, jnp.float32),
            pltpu.SemaphoreType.DMA((2,)),
            pltpu.SemaphoreType.DMA((2, half)),
            pltpu.SemaphoreType.DMA((2, half)),
            pltpu.SemaphoreType.DMA((2,)),
            pltpu.SemaphoreType.DMA((2,)),
            pltpu.SemaphoreType.DMA((2, half)),
            pltpu.SemaphoreType.DMA((2, half)),
            pltpu.SemaphoreType.DMA,
            pltpu.SemaphoreType.DMA,
        ],
        compiler_params=pltpu.CompilerParams(
            vmem_limit_bytes=VMEM_LIMIT, collective_id=identity, has_side_effects=True
        ),
        cost_estimate=pl.CostEstimate(flops=size, bytes_accessed=size, transcendentals=0),
        name="square",
    )(table, given, sent)


def pick(kind, index, wanted):
    hit = kind == wanted
    return jnp.where(hit, index, 0), hit.astype(jnp.float32)


def child_sum(total, table, base, slot, own, received, shared):
    for member in range(2):
        entry = base + (member * own.part_cols + slot) * 2
        kind, index = table[entry], table[entry + 1]
        if own.ref is not None:
            at, weight = pick(kind, index, 0)
            total = total + weight * own.ref[
                member, 0, pl.ds(at, own.blk, stride=own.child_cols), :
            ]
        if shared is not None:
            at, weight = pick(kind, index, SHARED)
            total = total + weight * shared[at]
        for step, ref in enumerate(received):
            at, weight = pick(kind, index, step + 1)
            total = total + weight * ref[at]
    return total


class Own(typing.NamedTuple):
    ref: typing.Any
    part_cols: int
    child_cols: int
    blk: int


def assemble_top(table, base, front, updates, received, shared):
    part_rows, blk, part_cols = front.shape[0], front.shape[2], front.shape[3]
    child_cols = updates.shape[4]
    slots = range(NP, part_cols)

    def kernel(table, front_ref, updates_ref, one, two, three, shared_ref, out_ref):
        own = Own(updates_ref, part_cols, child_cols, blk)
        for slot in slots:
            total = front_ref[0, pl.ds(slot, blk, stride=part_cols), :]
            out_ref[:, (slot - NP) * blk : (slot - NP + 1) * blk] = child_sum(
                total, table, base, slot, own, (one, two, three), shared_ref
            )

    return pl.pallas_call(
        kernel,
        grid_spec=pltpu.PrefetchScalarGridSpec(
            num_scalar_prefetch=1,
            grid=(1,),
            in_specs=[
                pl.BlockSpec((1, blk * part_cols, blk), lambda a, t: (0, 0, 0)),
                pl.BlockSpec((2, 1, blk * child_cols, blk), lambda a, t: (0, 0, 0, 0)),
            ]
            + [pl.BlockSpec(r.shape, lambda a, t: (0, 0, 0)) for r in received]
            + [pl.BlockSpec(shared.shape, lambda a, t: (0, 0, 0))],
            out_specs=pl.BlockSpec((blk, len(slots) * blk), lambda a, t: (0, 0)),
        ),
        out_shape=jax.ShapeDtypeStruct((blk, len(slots) * blk), jnp.float32),
        compiler_params=pltpu.CompilerParams(vmem_limit_bytes=VMEM_LIMIT),
        cost_estimate=pl.CostEstimate(flops=blk, bytes_accessed=blk, transcendentals=0),
        name="assemble",
    )(
        table,
        front.reshape(part_rows, blk * part_cols, blk),
        updates.reshape(2, part_rows, blk * child_cols, blk),
        *received, shared,
    )


def prepare_kernel(
    part_cols, child_cols, blk, row_count, col_count, bases, table,
    front_ref, updates_ref, own, chip, core, both, inverse_ref, lower_ref,
    out_ref, left_ref, inv_high, inv_low, units, panel_ref,
):
    step = pl.program_id(0)
    place_base, square_base, where = bases
    columns = [pl.multiple_of((s * col_count + table[where + 1]) * blk, blk) for s in range(NP)]
    size = inverse_ref.shape[0]

    @pl.when(step == 0)
    def _():
        inv_high[...], inv_low[...] = split(inverse_ref[...])
        out_ref[...] = jnp.zeros_like(out_ref)
        begin = pl.multiple_of(table[where] * blk, blk)
        for s in range(NP):
            out_ref[0, pl.ds(s, blk, stride=part_cols), :] = lower_ref[
                pl.ds(begin, blk), pl.ds(columns[s], blk)
            ]

    @pl.when(step > 0)
    def _():
        width = own.shape[0]
        for order, ref in enumerate((own, chip, core, both)):
            owner = table[where + 1 + order]
            for i in range(width):
                units[owner * width + i] = ref[i]
        for q in range(row_count):
            total = units[(q % col_count) * width + 4 + q // col_count]
            for member in range(2):
                entry = square_base + 2 * (member * row_count + q)
                total = total + units[table[entry]] * table[entry + 1].astype(jnp.float32)
            panel_ref[:, q * blk : (q + 1) * blk] = total
        mine = Own(updates_ref, part_cols, child_cols, blk)
        for slot in range(NP, part_cols):
            here = pl.ds(slot, blk, stride=part_cols)
            out_ref[0, here, :] = child_sum(
                front_ref[0, here, :], table, place_base, slot, mine, (), units
            )
        panel_pair = split(panel_ref[...])
        for begin in range(0, size, 2 * blk):
            end = begin + 2 * blk
            left_ref[:, begin:end] = product3(
                tuple(p[:, :end] for p in panel_pair),
                (inv_high[begin:end, :end], inv_low[begin:end, :end]),
                True,
            )
        for s in range(NP):
            out_ref[0, pl.ds(s, blk, stride=part_cols), :] = left_ref[:, pl.ds(columns[s], blk)]


def prepare(table, bases, front, updates, gathered, inverse, lower, row_count, col_count):
    part_rows, blk, part_cols = front.shape[0], front.shape[2], front.shape[3]
    child_cols = updates.shape[4]
    size = inverse.shape[0]

    def resident(shape):
        return pl.BlockSpec(shape, lambda a, t: (0, 0), pipeline_mode=pl.Buffered(1))

    return pl.pallas_call(
        functools.partial(prepare_kernel, part_cols, child_cols, blk, row_count, col_count, bases),
        grid_spec=pltpu.PrefetchScalarGridSpec(
            num_scalar_prefetch=1,
            grid=(part_rows,),
            in_specs=[
                pl.BlockSpec((1, blk * part_cols, blk), lambda a, t: (a, 0, 0)),
                pl.BlockSpec((2, 1, blk * child_cols, blk), lambda a, t: (0, a, 0, 0)),
            ]
            + [
                pl.BlockSpec((g.shape[0], blk, blk), lambda a, t: (0, jnp.maximum(a - 1, 0), 0))
                for g in gathered
            ]
            + [resident((size, size))] * 2,
            out_specs=[
                pl.BlockSpec((1, blk * part_cols, blk), lambda a, t: (a, 0, 0)),
                pl.BlockSpec((blk, size), lambda a, t: (jnp.maximum(a - 1, 0), 0)),
            ],
            scratch_shapes=[
                pltpu.VMEM((size, size), jnp.bfloat16),
                pltpu.VMEM((size, size), jnp.bfloat16),
                pltpu.VMEM((4 * (4 + NP), blk, blk), jnp.float32),
                pltpu.VMEM((blk, size), jnp.float32),
            ],
        ),
        out_shape=[
            jax.ShapeDtypeStruct((part_rows, blk * part_cols, blk), jnp.float32),
            jax.ShapeDtypeStruct(((part_rows - 1) * blk, size), jnp.float32),
        ],
        compiler_params=pltpu.CompilerParams(vmem_limit_bytes=VMEM_LIMIT),
        cost_estimate=pl.CostEstimate(flops=blk, bytes_accessed=blk, transcendentals=0),
        name="prepare",
    )(
        table,
        front.reshape(part_rows, blk * part_cols, blk),
        updates.reshape(2, part_rows, blk * child_cols, blk),
        *gathered, inverse, lower,
    )


def trail_kernel(part_cols, blk, given_ref, left_ref, high_ref, low_ref, out_ref):
    left_pair = split(left_ref[...])
    for s in range(NP):
        out_ref[0, pl.ds(s, blk, stride=part_cols), :] = given_ref[
            0, pl.ds(s, blk, stride=part_cols), :
        ]
    for pair in range(NP, part_cols, 2):
        cols = slice((pair - NP) * blk, (pair - NP + 2) * blk)
        trailing = product3(left_pair, (high_ref[:, cols], low_ref[:, cols]))
        for half in range(2):
            slot = pl.ds(pair + half, blk, stride=part_cols)
            out_ref[0, slot, :] = given_ref[0, slot, :] - trailing[:, half * blk : (half + 1) * blk]


def trail(given, left, high, low, part_cols, blk):
    block = pl.BlockSpec((1, blk * part_cols, blk), lambda a: (a + 1, 0, 0))

    def resident(shape):
        return pl.BlockSpec(shape, lambda a: (0, 0), pipeline_mode=pl.Buffered(1))

    return pl.pallas_call(
        functools.partial(trail_kernel, part_cols, blk),
        grid=(given.shape[0] - 1,),
        in_specs=[
            block,
            pl.BlockSpec((blk, left.shape[1]), lambda a: (a, 0)),
            resident(high.shape),
            resident(low.shape),
        ],
        out_specs=block,
        out_shape=jax.ShapeDtypeStruct(given.shape, given.dtype),
        input_output_aliases={0: 0},
        compiler_params=pltpu.CompilerParams(vmem_limit_bytes=VMEM_LIMIT),
        cost_estimate=pl.CostEstimate(flops=blk, bytes_accessed=blk, transcendentals=0),
        name="trail",
    )(given, left, high, low)


def right_rows_kernel(inverse_ref, top_ref, high_ref, low_ref, inv_high, inv_low):
    @pl.when(pl.program_id(0) == 0)
    def _():
        inv_high[...], inv_low[...] = split(inverse_ref[...])

    size = inverse_ref.shape[0]
    top_high, top_low = split(top_ref[...])
    for begin in range(0, size, 256):
        end = begin + 256
        result = product3(
            (inv_high[begin:end, :end], inv_low[begin:end, :end]), (top_high[:end], top_low[:end])
        )
        high_ref[begin:end, :], low_ref[begin:end, :] = split(result)


def right_rows(inverse, top, tile):
    size, cols = top.shape
    out = jax.ShapeDtypeStruct((size, cols), jnp.bfloat16)
    return pl.pallas_call(
        right_rows_kernel,
        grid=(cols // tile,),
        in_specs=[
            pl.BlockSpec((size, size), lambda n: (0, 0)),
            pl.BlockSpec((size, tile), lambda n: (0, n)),
        ],
        out_specs=[pl.BlockSpec((size, tile), lambda n: (0, n))] * 2,
        out_shape=[out, out],
        scratch_shapes=[pltpu.VMEM((size, size), jnp.bfloat16)] * 2,
        compiler_params=pltpu.CompilerParams(vmem_limit_bytes=VMEM_LIMIT),
        cost_estimate=pl.CostEstimate(flops=size, bytes_accessed=size, transcendentals=0),
        name="right",
    )(inverse, top)


def add_last_kernel(part_cols, blk, base, table, given_ref, one, two, three, out_ref):
    own = Own(None, part_cols, 0, blk)
    for slot in range(part_cols):
        here = pl.ds(slot, blk, stride=part_cols)
        total = given_ref[0, here, :]
        if slot >= NP:
            total = child_sum(total, table, base, slot, own, (one, two, three), None)
        out_ref[0, here, :] = total


def add_last(table, base, given, received, part_cols, blk):
    part_rows = given.shape[0]
    block = pl.BlockSpec((1, blk * part_cols, blk), lambda a, t: (a + 1, 0, 0))
    return pl.pallas_call(
        functools.partial(add_last_kernel, part_cols, blk, base),
        grid_spec=pltpu.PrefetchScalarGridSpec(
            num_scalar_prefetch=1,
            grid=(part_rows - 1,),
            in_specs=[block]
            + [pl.BlockSpec((r.shape[0], blk, blk), lambda a, t: (0, a, 0)) for r in received],
            out_specs=block,
        ),
        out_shape=jax.ShapeDtypeStruct(given.shape, given.dtype),
        input_output_aliases={1: 0},
        compiler_params=pltpu.CompilerParams(vmem_limit_bytes=VMEM_LIMIT),
        cost_estimate=pl.CostEstimate(flops=blk, bytes_accessed=blk, transcendentals=0),
        name="add_last",
    )(table, given, *received)


def table_layout(most, part_cols, panel_blocks):
    place = 3 * most
    square = place + 4 * part_cols
    where = square + 4 * panel_blocks
    return place, square, where, where + 8


def table_kernel(most, part_cols, panel_blocks, maps_ref, table, level_ref, ranks):
    place, square, where, size = table_layout(most, part_cols, panel_blocks)
    child_cols = maps_ref.shape[1] // 4
    row, col = lax.axis_index("row"), lax.axis_index("col")
    for i in range(size):
        table[i] = 0
    for i in range(2 * part_cols):
        table[place + 2 * i] = 4
    for i in range(4):
        ranks[i] = 0
    for g in range(child_cols):
        for member in range(2):
            turn = (maps_ref[member, 4 * g] - 4 * g) & 3
            slot = maps_ref[member, 4 * g + ((col - turn) & 3)] // 4
            entry = place + 2 * (member * part_cols + slot)
            if g < 2:
                unit = 2 * member + g
                table[entry] = jnp.where(turn == 0, 0, SHARED)
                table[entry + 1] = jnp.where(
                    turn == 0, g, ((col - turn) & 3) * (4 + NP) + unit
                )
                for j in range(4):
                    parent = maps_ref[member, 4 * g + j]

                    @pl.when(parent < panel_blocks)
                    def _():
                        table[square + 2 * (member * panel_blocks + parent)] = j * (4 + NP) + unit
                        table[square + 2 * (member * panel_blocks + parent) + 1] = 1

            else:
                rank = ranks[turn]
                ranks[turn] = rank + 1
                table[entry] = turn
                table[entry + 1] = jnp.where(turn == 0, g, rank)

                @pl.when(turn > 0)
                def _():
                    table[(turn - 1) * most + rank] = member * child_cols + g

    table[where] = row
    for i, mask in enumerate((0, 2, 1, 3)):
        table[where + 1 + i] = col ^ mask
    level = jnp.int32(len(LEVELS) - 1)
    for index in reversed(range(len(LEVELS) - 1)):
        one, two, three = LEVELS[index]
        fits = (ranks[1] <= one) & (ranks[2] <= two) & (ranks[3] <= three)
        level = jnp.where(fits, index, level)
    level_ref[0] = level


def make_table(maps, most, part_cols, panel_blocks):
    size = table_layout(most, part_cols, panel_blocks)[-1]
    scalars = pl.BlockSpec(memory_space=pltpu.SMEM)
    return pl.pallas_call(
        functools.partial(table_kernel, most, part_cols, panel_blocks),
        in_specs=[scalars],
        out_specs=[scalars] * 2,
        out_shape=[
            jax.ShapeDtypeStruct((size,), jnp.int32), jax.ShapeDtypeStruct((1,), jnp.int32)
        ],
        scratch_shapes=[pltpu.SMEM((4,), jnp.int32)],
        name="tables",
    )(maps)


def main_branch(level, most, row_count, front, updates, table):
    blk, part_cols = front.shape[2], front.shape[3]
    col_count = 4
    columns = range(col_count)

    def swap(value, mask):
        return lax.ppermute(value, "col", [(c, c ^ mask) for c in columns])

    def turned(value, turn):
        return lax.ppermute(value, "col", [(c, (c + turn) % col_count) for c in columns])

    place, square_base, where, _ = table_layout(most, part_cols, row_count)
    given, early, units, late = send_head(table, front, updates, LEVELS[level], most, level + 1)
    soon = min((1, 3), key=lambda turn: abs(LEVELS[level][turn - 1] - 6))
    square, shared, arrived = gather_square(
        table, square_base, given, late[soon - 1], soon, row_count, len(LEVELS) + level + 1
    )
    units, late, square = lax.optimization_barrier((units, late, square))
    chip, core = swap(units, 2), swap(units, 1)
    top = assemble_top(table, place, front, updates, early, shared)
    top, square = lax.optimization_barrier((top, square))
    top = lax.all_gather(top, "row", axis=0, tiled=True)
    lower, inverse = factorize(square, blk)
    chip, core, inverse = lax.optimization_barrier((chip, core, inverse))
    both = swap(chip, 1)
    late = [
        arrived if turn == soon else turned(late[turn - 1], turn) for turn in range(1, col_count)
    ]
    result, left = prepare(
        table, (place, square_base, where), front, updates, (units, chip, core, both), inverse,
        lower, row_count, col_count,
    )
    left, top = lax.optimization_barrier((left, top))
    high, low = right_rows(inverse, top, 2 * blk)
    result = trail(result, left, high, low, part_cols, blk)
    result, late = lax.optimization_barrier((result, late))
    return add_last(table, place, result, late, part_cols, blk)


def body(row_count, col_count, front, updates, maps):
    part_rows = front.shape[0]
    if part_rows < 3 or row_count != NP * col_count or col_count != 4:
        return simple_body(front, updates, maps)
    front = front.reshape(front.shape[0], 1, *front.shape[2:4], front.shape[5])
    blk, part_cols = front.shape[2], front.shape[3]
    most = updates.shape[4]
    table, level = make_table(maps, most, part_cols, row_count)
    branches = [
        functools.partial(main_branch, level, most, row_count) for level in range(len(LEVELS))
    ]
    result = lax.switch(level[0], branches, front, updates, table)
    return result.reshape(part_rows, 1, blk, part_cols, 1, blk)


def solution(mesh):
    return jax.shard_map(
        functools.partial(body, mesh.shape["row"], mesh.shape["col"]),
        mesh=mesh,
        in_specs=(
            P(None, "row", None, None, "col", None),
            P(None, None, "row", None, None, "col", None),
            P(),
        ),
        out_specs=P(None, "row", None, None, "col", None),
        check_vma=False,
    )
```

```python
import functools
import typing

import jax
import jax.numpy as jnp
from jax import lax
from jax.experimental import pallas as pl
from jax.experimental.pallas import tpu as pltpu
from jax.sharding import PartitionSpec as P

NP = 2
highest = lax.Precision.HIGHEST
VMEM_LIMIT = 56 * 1024 * 1024
MESH = pl.DeviceIdType.MESH
SHARED = 5
LEVELS = (
    (5, 4, 7), (9, 2, 8), (8, 5, 6), (5, 6, 9), (8, 8, 4), (10, 4, 10), (6, 10, 5), (9, 8, 8),
    (12, 12, 12),
)


def split(value):
    high = value.astype(jnp.bfloat16)
    low = (value - high.astype(jnp.float32)).astype(jnp.bfloat16)
    return high, low


def dims(transposed):
    return (((1,), (1 if transposed else 0,)), ((), ()))


def product3(left_pair, right_pair, transposed=False):
    def one(a, b):
        return lax.dot_general(a, b, dims(transposed), preferred_element_type=jnp.float32)

    return (
        one(left_pair[0], right_pair[0])
        + one(left_pair[0], right_pair[1])
        + one(left_pair[1], right_pair[0])
    )


def product(a, b, transposed=False):
    return lax.dot_general(
        a, b, dims(transposed), precision=highest, preferred_element_type=jnp.float32
    )


def pack_kernel(child_cols, cap, blk, table, updates_ref, one_ref, two_ref, three_ref):
    for turn, out_ref in enumerate((one_ref, two_ref, three_ref)):
        for member in range(2):
            for slot in range(cap):
                source = table[(turn + 1) * 2 * cap + member * cap + slot]
                out_ref[member * cap + slot] = updates_ref[
                    member, 0, pl.ds(source, blk, stride=child_cols), :
                ]


def pack(table, updates, cap, begin, count):
    part_rows, blk, child_cols = updates.shape[1], updates.shape[3], updates.shape[4]
    flat = updates.reshape(2, part_rows, blk * child_cols, blk)
    return pl.pallas_call(
        functools.partial(pack_kernel, child_cols, cap, blk),
        grid_spec=pltpu.PrefetchScalarGridSpec(
            num_scalar_prefetch=1,
            grid=(count,),
            in_specs=[
                pl.BlockSpec((2, 1, blk * child_cols, blk), lambda a, t: (0, a + begin, 0, 0))
            ],
            out_specs=[pl.BlockSpec((2 * cap, blk, blk), lambda a, t: (0, a, 0))] * 3,
        ),
        out_shape=[jax.ShapeDtypeStruct((2 * cap, count * blk, blk), jnp.float32)] * 3,
        compiler_params=pltpu.CompilerParams(vmem_limit_bytes=VMEM_LIMIT),
        name="pack",
    )(table, flat)


def add_children(out_ref, table, front_ref, updates_ref, received, slots, part_cols, child_cols, blk):
    for slot in slots:
        cols = slice(slot * blk, (slot + 1) * blk)
        out_ref[:, cols] = front_ref[0, pl.ds(slot, blk, stride=part_cols), :]
        for member in range(2):
            turn = table[(member * part_cols + slot) * 2]
            index = table[(member * part_cols + slot) * 2 + 1]

            @pl.when(turn == 0)
            def _():
                out_ref[:, cols] += updates_ref[member, 0, pl.ds(index, blk, stride=child_cols), :]

            for step in range(3):

                @pl.when(turn == step + 1)
                def _():
                    out_ref[:, cols] += received[step][index]


def assemble(table, front, updates, received, begin, count, width):
    part_rows, blk, part_cols = front.shape[0], front.shape[2], front.shape[3]
    child_cols = updates.shape[4]
    slots = received[0].shape[0]

    def kernel(table, front_ref, updates_ref, one, two, three, out_ref):
        add_children(
            out_ref, table, front_ref, updates_ref, (one, two, three),
            range(width), part_cols, child_cols, blk,
        )

    return pl.pallas_call(
        kernel,
        grid_spec=pltpu.PrefetchScalarGridSpec(
            num_scalar_prefetch=1,
            grid=(count,),
            in_specs=[
                pl.BlockSpec((1, blk * part_cols, blk), lambda a, t: (a + begin, 0, 0)),
                pl.BlockSpec((2, 1, blk * child_cols, blk), lambda a, t: (0, a + begin, 0, 0)),
            ]
            + [pl.BlockSpec((slots, blk, blk), lambda a, t: (0, a, 0))] * 3,
            out_specs=pl.BlockSpec((blk, width * blk), lambda a, t: (a, 0)),
        ),
        out_shape=jax.ShapeDtypeStruct((count * blk, width * blk), jnp.float32),
        compiler_params=pltpu.CompilerParams(vmem_limit_bytes=VMEM_LIMIT),
        name="assemble",
    )(
        table,
        front.reshape(part_rows, blk * part_cols, blk),
        updates.reshape(2, part_rows, blk * child_cols, blk),
        *received,
    )


def eliminate(block):
    size = block.shape[0]
    group = 8
    tiles = size // group
    shape = (group, size)
    row_ids = lax.broadcasted_iota(jnp.int32, (size, size), 0)
    col_ids = lax.broadcasted_iota(jnp.int32, (size, size), 1)
    local = lax.broadcasted_iota(jnp.int32, shape, 0)
    start = (row_ids == col_ids).astype(jnp.float32)
    upper = [block[group * t : group * (t + 1), :] for t in range(tiles)]
    solved = [start[group * t : group * (t + 1), :] for t in range(tiles)]
    for h in range(tiles):
        def column(t, j):
            return jnp.broadcast_to(upper[t][:, group * h + j : group * h + j + 1], shape)
        home = [column(h, j) for j in range(group)]
        pivot = {
            (i, j): jnp.broadcast_to(home[j][i : i + 1, :], shape)
            for j in range(group) for i in range(j, group)
        }
        scale, ratio = [], {}
        for j in range(group):
            scale.append(1.0 / pivot[j, j])
            for i in range(j + 1, group):
                ratio[i, j] = pivot[i, j] * scale[j]
            for k in range(j + 1, group):
                for i in range(k, group):
                    pivot[i, k] = pivot[i, k] - ratio[i, j] * pivot[k, j]
        upper_rows, solved_rows = [], []
        for j in range(group):
            u = jnp.broadcast_to(upper[h][j : j + 1, :], shape)
            s = jnp.broadcast_to(solved[h][j : j + 1, :], shape)
            for i in range(j):
                u = u - ratio[j, i] * upper_rows[i]
                s = s - ratio[j, i] * solved_rows[i]
            upper_rows.append(u)
            solved_rows.append(s)
        for t in range(h, tiles):
            if t == h:
                u, s = upper_rows[0], solved_rows[0]
                for j in range(1, group):
                    u = jnp.where(local == j, upper_rows[j], u)
                    s = jnp.where(local == j, solved_rows[j], s)
                upper[t], solved[t] = u, s
                continue
            factors = []
            for j in range(group):
                c = column(t, j)
                for i in range(j):
                    c = c - factors[i] * pivot[j, i]
                factors.append(c * scale[j])
            for j in range(group):
                upper[t] = upper[t] - factors[j] * upper_rows[j]
                solved[t] = solved[t] - factors[j] * solved_rows[j]
    upper = jnp.concatenate(upper, axis=0)
    solved = jnp.concatenate(solved, axis=0)
    diagonal = jnp.sum(jnp.where(row_ids == col_ids, upper, 0.0), axis=1, keepdims=True)
    scale = 1.0 / jnp.sqrt(diagonal)
    lower = jnp.where(col_ids >= row_ids, upper * scale, 0.0).T
    return lower, solved * scale

def factor_kernel(blk, square_ref, lower_ref, inverse_ref, work):
    size = square_ref.shape[0]
    count = size // blk
    work[...] = square_ref[...]
    lower_ref[...] = jnp.zeros_like(lower_ref)
    inverse_ref[...] = jnp.zeros_like(inverse_ref)

    def spread(k, diag_inverse):
        begin, end = k * blk, (k + 1) * blk
        here = slice(begin, end)
        inverse_pair = split(diag_inverse)
        if k:
            done = product3(inverse_pair, split(inverse_ref[here, :begin]))
            inverse_ref[here, :begin] = done
        inverse_ref[here, here] = diag_inverse
        if end == size:
            return
        row_high, row_low = split(inverse_ref[here, :end])
        left_high, left_low = [], []
        for q in range(end, size, 256):
            top = min(q + 256, size)
            left = product3(split(work[q:top, here]), inverse_pair, True)
            lower_ref[q:top, here] = left
            high, low = split(left)
            left_high.append(high)
            left_low.append(low)
        high = jnp.concatenate(left_high, axis=0)
        low = jnp.concatenate(left_low, axis=0)
        for q in range(end, size, 256):
            top = min(q + 256, size)
            pair = high[q - end : top - end], low[q - end : top - end]
            below = high[: top - end], low[: top - end]
            work[q:top, end:top] -= product3(pair, below, True)
            inverse_ref[q:top, :end] -= product3(pair, (row_high, row_low))

    def step(k, carry):
        begin = pl.multiple_of(k * blk, blk)
        here = pl.ds(begin, blk)
        diag_lower, diag_inverse = eliminate(work[here, here])
        lower_ref[here, here] = diag_lower
        for t in range(count):
            pl.when(k == t)(functools.partial(spread, t, diag_inverse))
        return carry

    lax.fori_loop(0, count, step, 0)


def factorize(square, blk):
    size = square.shape[0]
    shape = jax.ShapeDtypeStruct((size, size), jnp.float32)
    return pl.pallas_call(
        functools.partial(factor_kernel, blk),
        out_shape=[shape, shape],
        scratch_shapes=[pltpu.VMEM((size, size), jnp.float32)],
        compiler_params=pltpu.CompilerParams(vmem_limit_bytes=VMEM_LIMIT),
        cost_estimate=pl.CostEstimate(flops=size, bytes_accessed=size, transcendentals=0),
        name="factorize",
    )(square)


def right_kernel(inverse_ref, top_ref, high_ref, low_ref, inv_high, inv_low):
    @pl.when(pl.program_id(0) == 0)
    def _():
        inv_high[...], inv_low[...] = split(inverse_ref[...])

    result = product3((inv_high[...], inv_low[...]), split(top_ref[...]))
    high_ref[...], low_ref[...] = split(result)


def right_side(inverse, top, tile):
    size, cols = top.shape
    out = jax.ShapeDtypeStruct((size, cols), jnp.bfloat16)
    return pl.pallas_call(
        right_kernel,
        grid=(cols // tile,),
        in_specs=[
            pl.BlockSpec((size, size), lambda n: (0, 0)),
            pl.BlockSpec((size, tile), lambda n: (0, n)),
        ],
        out_specs=[pl.BlockSpec((size, tile), lambda n: (0, n))] * 2,
        out_shape=[out, out],
        scratch_shapes=[pltpu.VMEM((size, size), jnp.bfloat16)] * 2,
        compiler_params=pltpu.CompilerParams(vmem_limit_bytes=VMEM_LIMIT),
        cost_estimate=pl.CostEstimate(flops=size, bytes_accessed=size, transcendentals=0),
        name="right",
    )(inverse, top)


def finish_kernel(
    part_cols, child_cols, blk, row_count, col_count, first, table, place,
    panel_ref, front_ref, updates_ref, one, two, three, inverse_ref, lower_ref, high_ref, low_ref,
    out_ref, inv_high, inv_low, left_ref, sum_ref,
):
    step = pl.program_id(0)
    block_row = step * row_count + place[0]
    panel_blocks = NP * col_count
    inside = block_row < panel_blocks
    columns = [pl.multiple_of((s * col_count + place[1]) * blk, blk) for s in range(NP)]

    @pl.when(step == 0)
    def _():
        inv_high[...], inv_low[...] = split(inverse_ref[...])

    @pl.when(jnp.logical_not(inside))
    def _():
        add_children(
            sum_ref, table, front_ref, updates_ref, (one, two, three),
            range(NP, part_cols), part_cols, child_cols, blk,
        )
        panel = jnp.concatenate(
            [
                panel_ref[c, :, s * blk : (s + 1) * blk]
                for s in range(NP)
                for c in range(col_count)
            ],
            axis=1,
        )
        left_ref[...] = product3(split(panel), (inv_high[...], inv_low[...]), True)
        left_pair = split(left_ref[...])
        for pair in range(NP, part_cols, 2):
            cols = slice((pair - NP) * blk, (pair - NP + 2) * blk)
            trailing = product3(left_pair, (high_ref[:, cols], low_ref[:, cols]))
            updated = sum_ref[:, pair * blk : (pair + 2) * blk] - trailing
            for half in range(2):
                out_ref[0, pl.ds(pair + half, blk, stride=part_cols), :] = updated[
                    :, half * blk : (half + 1) * blk
                ]
        for s in range(NP):
            out_ref[0, pl.ds(s, blk, stride=part_cols), :] = left_ref[:, pl.ds(columns[s], blk)]

    @pl.when(inside)
    def _():
        out_ref[...] = jnp.zeros_like(out_ref)
        begin = pl.multiple_of(block_row * blk, blk)
        for s in range(NP):
            out_ref[0, pl.ds(s, blk, stride=part_cols), :] = lower_ref[
                pl.ds(begin, blk), pl.ds(columns[s], blk)
            ]


def finish(table, place, panel, front, updates, received, inverse, lower, high, low, row_count, first):
    part_rows, blk, part_cols = front.shape[0], front.shape[2], front.shape[3]
    child_cols = updates.shape[4]
    size = inverse.shape[0]
    slots = received[0].shape[0]
    col_count = panel.shape[0]

    def resident(shape):
        return pl.BlockSpec(shape, lambda a, t, p: (0, 0), pipeline_mode=pl.Buffered(1))

    def late(a, t, p):
        return (0, jnp.maximum(a - first, 0), 0)

    return pl.pallas_call(
        functools.partial(finish_kernel, part_cols, child_cols, blk, row_count, col_count, first),
        grid_spec=pltpu.PrefetchScalarGridSpec(
            num_scalar_prefetch=2,
            grid=(part_rows,),
            in_specs=[
                pl.BlockSpec((col_count, blk, NP * blk), late),
                pl.BlockSpec((1, blk * part_cols, blk), lambda a, t, p: (a, 0, 0)),
                pl.BlockSpec((2, 1, blk * child_cols, blk), lambda a, t, p: (0, a, 0, 0)),
            ]
            + [pl.BlockSpec((slots, blk, blk), late)] * 3
            + [
                resident((size, size)),
                resident((size, size)),
                resident(high.shape),
                resident(low.shape),
            ],
            out_specs=pl.BlockSpec((1, blk * part_cols, blk), lambda a, t, p: (a, 0, 0)),
            scratch_shapes=[
                pltpu.VMEM((size, size), jnp.bfloat16),
                pltpu.VMEM((size, size), jnp.bfloat16),
                pltpu.VMEM((blk, size), jnp.float32),
                pltpu.VMEM((blk, part_cols * blk), jnp.float32),
            ],
        ),
        out_shape=jax.ShapeDtypeStruct((part_rows, blk * part_cols, blk), jnp.float32),
        compiler_params=pltpu.CompilerParams(vmem_limit_bytes=VMEM_LIMIT),
        name="finish",
    )(
        table, place, panel,
        front.reshape(part_rows, blk * part_cols, blk),
        updates.reshape(2, part_rows, blk * child_cols, blk),
        *received, inverse, lower, high, low,
    )


def tables(maps, col_index, col_count, child_cols, part_cols, cap):
    offsets = maps[:, ::col_count] - col_count * jnp.arange(child_cols, dtype=jnp.int32)[None, :]
    turn = offsets % col_count
    groups = jnp.arange(child_cols, dtype=jnp.int32)
    same = (turn[:, :, None] == turn[:, None, :]) & (groups[None, None, :] < groups[None, :, None])
    rank = jnp.sum(same.astype(jnp.int32), axis=2)
    turns = jnp.arange(col_count, dtype=jnp.int32)
    slots = jnp.arange(cap, dtype=jnp.int32)
    hot = (turn[None, :, None, :] == turns[:, None, None, None]) & (
        rank[None, :, None, :] == slots[None, None, :, None]
    )
    send = jnp.sum(jnp.where(hot, groups[None, None, None, :], 0), axis=3).reshape(-1)
    parents = jnp.arange(part_cols, dtype=jnp.int32) * col_count + col_index
    match = maps[:, None, :] == parents[None, :, None]
    spread = jnp.repeat(groups, col_count)
    group = jnp.sum(jnp.where(match, spread[None, None, :], 0), axis=2)
    present = jnp.any(match, axis=2)
    pick = group[:, :, None] == groups[None, None, :]
    kind = jnp.sum(jnp.where(pick, turn[:, None, :], 0), axis=2)
    order = jnp.sum(jnp.where(pick, rank[:, None, :], 0), axis=2)
    order = jnp.where(kind == 0, group, order + cap * jnp.arange(2, dtype=jnp.int32)[:, None])
    kind = jnp.where(present, kind, col_count)
    place = jnp.stack([kind, order], axis=2).reshape(-1)
    return send, place


def gather_top(piece, row_count, row_index, panel_blocks):
    if row_count == panel_blocks:
        return lax.all_gather(piece, "row", axis=0, tiled=True)
    ids = jnp.arange(panel_blocks, dtype=jnp.int32)
    kept = jnp.where((ids == row_index)[:, None, None], piece[None], 0.0)
    return lax.psum(kept, "row").reshape(panel_blocks * piece.shape[0], piece.shape[1])


def simple_body(front, updates, maps):
    row_count = lax.axis_size("row")
    col_count = lax.axis_size("col")
    row_index = lax.axis_index("row")
    col_index = lax.axis_index("col")
    front = front.reshape(front.shape[0], 1, *front.shape[2:4], front.shape[5])
    blk, part_cols = front.shape[2], front.shape[3]
    child_cols = updates.shape[4]
    cap = child_cols // 2
    panel_blocks = NP * col_count
    send, place = tables(maps, col_index, col_count, child_cols, part_cols, cap)
    part_rows = front.shape[0]
    first = 1 if part_rows > 1 and row_count == panel_blocks else part_rows

    def exchange(outgoing):
        return [
            lax.ppermute(
                outgoing[turn - 1], "col", [(c, (c + turn) % col_count) for c in range(col_count)]
            )
            for turn in range(1, col_count)
        ]

    early = exchange(pack(send, updates, cap, 0, first))
    if first < part_rows:
        outgoing = pack(send, updates, cap, first, part_rows - first)
        early, outgoing = lax.optimization_barrier((early, outgoing))
        received = exchange(outgoing)
    else:
        received = early
    head = assemble(place, front, updates, early, 0, 1, part_cols)
    square = jnp.concatenate(
        [
            lax.all_gather(head[:, s * blk : (s + 1) * blk], "col", axis=1, tiled=True)
            for s in range(NP)
        ],
        axis=1,
    )
    square = gather_top(square, row_count, row_index, panel_blocks)
    rest, square = lax.optimization_barrier((head[:, NP * blk :], square))
    top = gather_top(rest, row_count, row_index, panel_blocks)
    lower, inverse = factorize(square, blk)
    high, low = right_side(inverse, top, 2 * blk)
    received, high, low = lax.optimization_barrier((received, high, low))
    late = first if first < part_rows else 0
    panel = assemble(place, front, updates, received, late, part_rows - late, NP)
    panel = lax.all_gather(panel, "col", axis=0)
    where = jnp.stack([row_index, col_index]).astype(jnp.int32)
    result = finish(
        place, where, panel, front, updates, received, inverse, lower, high, low, row_count, late
    )
    return result.reshape(front.shape[0], 1, blk, part_cols, 1, blk)


def send_kernel(
    blk, caps, most, table, front_ref, updates_ref, units_ref, got_one, got_two, got_three,
    panel_ref, late_one, late_two, late_three,
    front_part, updates_part, columns, units, first, stage, stage_one, stage_two, stage_three,
    local, keep_sem, send, recv, out_sem,
):
    row, col = lax.axis_index("row"), lax.axis_index("col")
    part_rows = front_ref.shape[0]
    part_cols = front_part.shape[1] // blk
    child_cols = updates_part.shape[2] // blk
    width = units.shape[0]
    stages = (stage_one, stage_two, stage_three)

    def loads(a, side):
        copies = [pltpu.make_async_copy(front_ref.at[a], front_part.at[side], local.at[side, 0])]
        for member in range(2):
            copies.append(
                pltpu.make_async_copy(
                    updates_ref.at[member, a], updates_part.at[side, member],
                    local.at[side, 1 + member],
                )
            )
        return copies

    for load in loads(0, 0):
        load.start()
    for load in loads(1, 1):
        load.start()
    others = [lax.rem(col + turn, 4) for turn in range(1, 4)]
    barrier = pltpu.get_barrier_semaphore()
    for other in others:
        pl.semaphore_signal(barrier, inc=1, device_id=(row, other), device_id_type=MESH)

    def spread(side, target):
        for member in range(2):
            for g in range(child_cols):
                columns[member * child_cols + g] = updates_part[
                    side, member, pl.ds(g, blk, stride=child_cols), :
                ]
        for member in range(2):
            for g in range(2):
                target[member * 2 + g] = columns[member * child_cols + g]
        for s in range(NP):
            target[4 + s] = front_part[side, pl.ds(s, blk, stride=part_cols), :]

    for load in loads(0, 0):
        load.wait()
    spread(0, units)
    pl.semaphore_wait(barrier, 3)

    def remote(source, target, index, device):
        return pltpu.make_async_remote_copy(
            src_ref=source, dst_ref=target, send_sem=send.at[index], recv_sem=recv.at[index],
            device_id=(row, device), device_id_type=MESH,
        )

    across = remote(units, units_ref.at[pl.ds(col * width, width)], 3, others[1])
    across.start()
    keep = pltpu.make_async_copy(units, units_ref.at[pl.ds(col * width, width)], keep_sem)
    keep.start()
    other_core = col + 1 - 2 * lax.rem(col, 2)

    def beside(owner, index):
        section = units_ref.at[pl.ds(owner * width, width)]
        source = units if index == 4 else section
        return remote(source, section, index, other_core)

    mine = beside(col, 4)
    mine.start()
    moves = []
    begin = 0
    for turn, target in enumerate((got_one, got_two, got_three)):
        for slot in range(caps[turn]):
            first[begin + slot] = columns[table[turn * most + slot]]
        moves.append(remote(first.at[pl.ds(begin, caps[turn])], target, turn, others[turn]))
        moves[-1].start()
        begin += caps[turn]

    def stores(a, side):
        rows = pl.ds(pl.multiple_of((a - 1) * blk, blk), blk)
        copies = [pltpu.make_async_copy(stage.at[side], panel_ref.at[:, rows, :], out_sem.at[side, 0])]
        for turn, target in enumerate((late_one, late_two, late_three)):
            copies.append(
                pltpu.make_async_copy(
                    stages[turn].at[side], target.at[:, rows, :], out_sem.at[side, 1 + turn]
                )
            )
        return copies

    def step(a, carry):
        side = lax.rem(a, 2)
        for load in loads(a, side):
            load.wait()

        @pl.when(a + 1 < part_rows)
        def _():
            for load in loads(a + 1, 1 - side):
                load.start()

        @pl.when(a > 2)
        def _():
            for store in stores(a - 2, side):
                store.wait()

        spread(side, stage.at[side])
        for turn in range(3):
            for slot in range(caps[turn]):
                stages[turn][side, slot] = columns[table[turn * most + slot]]
        for store in stores(a, side):
            store.start()
        return carry

    lax.fori_loop(1, part_rows, step, 0)
    for a in range(max(1, part_rows - 2), part_rows):
        for store in stores(a, a % 2):
            store.wait()
    keep.wait()
    across.wait_send()
    remote(units, units_ref.at[pl.ds(others[1] * width, width)], 3, others[1]).wait_recv()
    passed = beside(others[1], 5)
    passed.start()
    for index, owner in enumerate((other_core, lax.rem(other_core + 2, 4))):
        beside(owner, 4 + index).wait_recv()
    for move in (mine, passed):
        move.wait_send()
    for move in moves:
        move.wait()


def send_head(table, front, updates, caps, most, identity):
    part_rows, blk, part_cols = front.shape[0], front.shape[2], front.shape[3]
    child_cols = updates.shape[4]
    anywhere = pl.BlockSpec(memory_space=pl.ANY)
    width = 4 + NP
    rest = (part_rows - 1) * blk
    shapes = [(4 * width, blk, blk)] + [(cap, blk, blk) for cap in caps]
    shapes += [(width, rest, blk)] + [(cap, rest, blk) for cap in caps]
    outs = pl.pallas_call(
        functools.partial(send_kernel, blk, caps, most),
        in_specs=[pl.BlockSpec(memory_space=pltpu.SMEM), anywhere, anywhere],
        out_specs=[anywhere] * 8,
        out_shape=[jax.ShapeDtypeStruct(shape, jnp.float32) for shape in shapes],
        scratch_shapes=[
            pltpu.VMEM((2, blk * part_cols, blk), jnp.float32),
            pltpu.VMEM((2, 2, blk * child_cols, blk), jnp.float32),
            pltpu.VMEM((2 * child_cols, blk, blk), jnp.float32),
            pltpu.VMEM((width, blk, blk), jnp.float32),
            pltpu.VMEM((sum(caps), blk, blk), jnp.float32),
            pltpu.VMEM((2, width, blk, blk), jnp.float32),
        ]
        + [pltpu.VMEM((2, cap, blk, blk), jnp.float32) for cap in caps]
        + [
            pltpu.SemaphoreType.DMA((2, 3)),
            pltpu.SemaphoreType.DMA,
            pltpu.SemaphoreType.DMA((6,)),
            pltpu.SemaphoreType.DMA((6,)),
            pltpu.SemaphoreType.DMA((2, 4)),
        ],
        compiler_params=pltpu.CompilerParams(
            vmem_limit_bytes=VMEM_LIMIT, collective_id=identity, has_side_effects=True
        ),
        cost_estimate=pl.CostEstimate(flops=blk, bytes_accessed=blk, transcendentals=0),
        name="send",
    )(
        table,
        front.reshape(part_rows, blk * part_cols, blk),
        updates.reshape(2, part_rows, blk * child_cols, blk),
    )
    return outs[0], outs[1:4], outs[4], outs[5:]


def square_kernel(
    blk, row_count, turn, base, table, given_ref, sent_ref, square_ref, got_ref,
    work, units, local, line_send, line_recv, core_send, core_recv, turn_send, turn_recv,
):
    row, col = lax.axis_index("row"), lax.axis_index("col")
    width = units.shape[0] // 4
    half = row_count // 2
    core = lax.rem(col, 2)
    other_core = col + 1 - 2 * core
    other_chip = lax.rem(col + 2, 4)
    diagonal = lax.rem(other_core + 2, 4)

    load = pltpu.make_async_copy(given_ref, units, local)
    load.start()

    def ring_row(position):
        position = lax.rem(position + row_count, row_count)
        return jnp.where(position < half, 2 * position, 2 * (row_count - position) - 1)

    place = jnp.where(lax.rem(row, 2) == 0, row // 2, row_count - 1 - row // 2)
    right, left = ring_row(place + 1), ring_row(place - 1)
    barrier = pltpu.get_barrier_semaphore()
    for device in (
        (row, other_core), (row, other_chip), (row, diagonal), (right, col), (left, col)
    ):
        pl.semaphore_signal(barrier, inc=1, device_id=device, device_id_type=MESH)
    load.wait()
    pl.semaphore_wait(barrier, 5)
    turned = pltpu.make_async_remote_copy(
        src_ref=sent_ref, dst_ref=got_ref, send_sem=turn_send, recv_sem=turn_recv,
        device_id=(row, lax.rem(col + turn, 4)), device_id_type=MESH,
    )
    turned.start()

    here = pl.multiple_of(row * blk, blk)
    for q in range(row_count):
        s, owner = q // 4, q % 4
        total = units[owner * width + 4 + s]
        for member in range(2):
            entry = base + 2 * (member * row_count + q)
            total = total + units[table[entry]] * table[entry + 1].astype(jnp.float32)
        work[pl.ds(here, blk), q * blk : (q + 1) * blk] = total

    cols = work.shape[1] // 2

    def part(position, side):
        begin = pl.multiple_of(ring_row(position) * blk, blk)
        return work.at[pl.ds(begin, blk), pl.ds(pl.multiple_of(side * cols, cols), cols)]

    def copy(ref, device, send, recv):
        return pltpu.make_async_remote_copy(
            src_ref=ref, dst_ref=ref, send_sem=send, recv_sem=recv,
            device_id=device, device_id_type=MESH,
        )

    pending = []
    for step in range(half):
        ways = range(2 if step < half - 1 else 1)
        for way in ways:
            position = place - step if way == 0 else place + step
            target = right if way == 0 else left
            move = copy(
                part(position, core), (target, col), line_send.at[way, step], line_recv.at[way, step]
            )
            move.start()
            pending.append(move)
        for way in ways:
            origin = place - step - 1 if way == 0 else place + step + 1
            landed = part(origin, core)
            copy(
                landed, (right, col), line_send.at[way, step], line_recv.at[way, step]
            ).wait_recv()
            forward = copy(
                landed, (row, other_core), core_send.at[way, step], core_recv.at[way, step]
            )
            forward.start()
            pending.append(forward)
    for way in range(2):
        for step in range(half - way):
            origin = place - step - 1 if way == 0 else place + step + 1
            copy(
                part(origin, 1 - core), (row, other_core),
                core_send.at[way, step], core_recv.at[way, step],
            ).wait_recv()
    store = pltpu.make_async_copy(work, square_ref, local)
    store.start()
    for move in pending:
        move.wait_send()
    store.wait()
    turned.wait()


def gather_square(table, base, given, sent, turn, row_count, identity):
    blk = given.shape[1]
    size = row_count * blk
    half = row_count // 2
    anywhere = pl.BlockSpec(memory_space=pl.ANY)
    return pl.pallas_call(
        functools.partial(square_kernel, blk, row_count, turn, base),
        in_specs=[pl.BlockSpec(memory_space=pltpu.SMEM), anywhere, anywhere],
        out_specs=[anywhere] * 2,
        out_shape=[
            jax.ShapeDtypeStruct((size, size), jnp.float32),
            jax.ShapeDtypeStruct(sent.shape, jnp.float32),
        ],
        scratch_shapes=[
            pltpu.VMEM((size, size), jnp.float32),
            pltpu.VMEM(given.shape, jnp.float32),
            pltpu.SemaphoreType.DMA,
            pltpu.SemaphoreType.DMA((2, half)),
            pltpu.SemaphoreType.DMA((2, half)),
            pltpu.SemaphoreType.DMA((2, half)),
            pltpu.SemaphoreType.DMA((2, half)),
            pltpu.SemaphoreType.DMA,
            pltpu.SemaphoreType.DMA,
        ],
        compiler_params=pltpu.CompilerParams(
            vmem_limit_bytes=VMEM_LIMIT, collective_id=identity, has_side_effects=True
        ),
        cost_estimate=pl.CostEstimate(flops=size, bytes_accessed=size, transcendentals=0),
        name="square",
    )(table, given, sent)


def pick(kind, index, wanted):
    hit = kind == wanted
    return jnp.where(hit, index, 0), hit.astype(jnp.float32)


def child_sum(total, table, base, slot, own, received, shared):
    for member in range(2):
        entry = base + (member * own.part_cols + slot) * 2
        kind, index = table[entry], table[entry + 1]
        if own.ref is not None:
            at, weight = pick(kind, index, 0)
            total = total + weight * own.ref[
                member, 0, pl.ds(at, own.blk, stride=own.child_cols), :
            ]
        if shared is not None:
            at, weight = pick(kind, index, SHARED)
            total = total + weight * shared[at]
        for step, ref in enumerate(received):
            at, weight = pick(kind, index, step + 1)
            total = total + weight * ref[at]
    return total


class Own(typing.NamedTuple):
    ref: typing.Any
    part_cols: int
    child_cols: int
    blk: int


def assemble_top(table, base, front, updates, received, shared):
    part_rows, blk, part_cols = front.shape[0], front.shape[2], front.shape[3]
    child_cols = updates.shape[4]
    slots = range(NP, part_cols)

    def kernel(table, front_ref, updates_ref, one, two, three, shared_ref, out_ref):
        own = Own(updates_ref, part_cols, child_cols, blk)
        for slot in slots:
            total = front_ref[0, pl.ds(slot, blk, stride=part_cols), :]
            out_ref[:, (slot - NP) * blk : (slot - NP + 1) * blk] = child_sum(
                total, table, base, slot, own, (one, two, three), shared_ref
            )

    return pl.pallas_call(
        kernel,
        grid_spec=pltpu.PrefetchScalarGridSpec(
            num_scalar_prefetch=1,
            grid=(1,),
            in_specs=[
                pl.BlockSpec((1, blk * part_cols, blk), lambda a, t: (0, 0, 0)),
                pl.BlockSpec((2, 1, blk * child_cols, blk), lambda a, t: (0, 0, 0, 0)),
            ]
            + [pl.BlockSpec(r.shape, lambda a, t: (0, 0, 0)) for r in received]
            + [pl.BlockSpec(shared.shape, lambda a, t: (0, 0, 0))],
            out_specs=pl.BlockSpec((blk, len(slots) * blk), lambda a, t: (0, 0)),
        ),
        out_shape=jax.ShapeDtypeStruct((blk, len(slots) * blk), jnp.float32),
        compiler_params=pltpu.CompilerParams(vmem_limit_bytes=VMEM_LIMIT),
        cost_estimate=pl.CostEstimate(flops=blk, bytes_accessed=blk, transcendentals=0),
        name="assemble",
    )(
        table,
        front.reshape(part_rows, blk * part_cols, blk),
        updates.reshape(2, part_rows, blk * child_cols, blk),
        *received, shared,
    )


def prepare_kernel(
    part_cols, child_cols, blk, row_count, col_count, bases, table,
    front_ref, updates_ref, own, chip, core, both, inverse_ref,
    sum_ref, left_ref, inv_high, inv_low, units, panel_ref,
):
    place_base, square_base, where = bases
    size = inverse_ref.shape[0]

    @pl.when(pl.program_id(0) == 0)
    def _():
        inv_high[...], inv_low[...] = split(inverse_ref[...])

    width = own.shape[0]
    for order, ref in enumerate((own, chip, core, both)):
        owner = table[where + 1 + order]
        for i in range(width):
            units[owner * width + i] = ref[i]
    for q in range(row_count):
        total = units[(q % col_count) * width + 4 + q // col_count]
        for member in range(2):
            entry = square_base + 2 * (member * row_count + q)
            total = total + units[table[entry]] * table[entry + 1].astype(jnp.float32)
        panel_ref[:, q * blk : (q + 1) * blk] = total
    mine = Own(None, part_cols, child_cols, blk)
    for slot in range(NP, part_cols):
        cols = slice((slot - NP) * blk, (slot - NP + 1) * blk)
        sum_ref[:, cols] = child_sum(
            front_ref[0, pl.ds(slot, blk, stride=part_cols), :],
            table, place_base, slot, mine, (), units,
        )
    for slot in range(NP, part_cols):
        cols = slice((slot - NP) * blk, (slot - NP + 1) * blk)
        for member in range(2):
            entry = place_base + (member * part_cols + slot) * 2

            @pl.when(table[entry] == 0)
            def _():
                sum_ref[:, cols] += updates_ref[
                    member, 0, pl.ds(table[entry + 1], blk, stride=child_cols), :
                ]

    panel_pair = split(panel_ref[...])
    for begin in range(0, size, 2 * blk):
        end = begin + 2 * blk
        left_ref[:, begin:end] = product3(
            tuple(p[:, :end] for p in panel_pair),
            (inv_high[begin:end, :end], inv_low[begin:end, :end]),
            True,
        )


def prepare(table, bases, front, updates, gathered, inverse, row_count, col_count):
    part_rows, blk, part_cols = front.shape[0], front.shape[2], front.shape[3]
    child_cols = updates.shape[4]
    size = inverse.shape[0]
    rows, width = (part_rows - 1) * blk, (part_cols - NP) * blk
    return pl.pallas_call(
        functools.partial(prepare_kernel, part_cols, child_cols, blk, row_count, col_count, bases),
        grid_spec=pltpu.PrefetchScalarGridSpec(
            num_scalar_prefetch=1,
            grid=(part_rows - 1,),
            in_specs=[
                pl.BlockSpec((1, blk * part_cols, blk), lambda a, t: (a + 1, 0, 0)),
                pl.BlockSpec((2, 1, blk * child_cols, blk), lambda a, t: (0, a + 1, 0, 0)),
            ]
            + [pl.BlockSpec((g.shape[0], blk, blk), lambda a, t: (0, a, 0)) for g in gathered]
            + [pl.BlockSpec((size, size), lambda a, t: (0, 0), pipeline_mode=pl.Buffered(1))],
            out_specs=[
                pl.BlockSpec((blk, width), lambda a, t: (a, 0)),
                pl.BlockSpec((blk, size), lambda a, t: (a, 0)),
            ],
            scratch_shapes=[
                pltpu.VMEM((size, size), jnp.bfloat16),
                pltpu.VMEM((size, size), jnp.bfloat16),
                pltpu.VMEM((4 * (4 + NP), blk, blk), jnp.float32),
                pltpu.VMEM((blk, size), jnp.float32),
            ],
        ),
        out_shape=[
            jax.ShapeDtypeStruct((rows, width), jnp.float32),
            jax.ShapeDtypeStruct((rows, size), jnp.float32),
        ],
        compiler_params=pltpu.CompilerParams(vmem_limit_bytes=VMEM_LIMIT),
        cost_estimate=pl.CostEstimate(flops=blk, bytes_accessed=blk, transcendentals=0),
        name="prepare",
    )(
        table,
        front.reshape(part_rows, blk * part_cols, blk),
        updates.reshape(2, part_rows, blk * child_cols, blk),
        *gathered, inverse,
    )


def trail_kernel(given_ref, left_ref, high_ref, low_ref, out_ref):
    left_pair = split(left_ref[...])
    for begin in range(0, given_ref.shape[1], 256):
        cols = slice(begin, begin + 256)
        trailing = product3(left_pair, (high_ref[:, cols], low_ref[:, cols]))
        out_ref[:, cols] = given_ref[:, cols] - trailing


def trail(given, left, high, low, blk):
    block = pl.BlockSpec((blk, given.shape[1]), lambda a: (a, 0))

    def resident(shape):
        return pl.BlockSpec(shape, lambda a: (0, 0), pipeline_mode=pl.Buffered(1))

    return pl.pallas_call(
        trail_kernel,
        grid=(given.shape[0] // blk,),
        in_specs=[
            block,
            pl.BlockSpec((blk, left.shape[1]), lambda a: (a, 0)),
            resident(high.shape),
            resident(low.shape),
        ],
        out_specs=block,
        out_shape=jax.ShapeDtypeStruct(given.shape, given.dtype),
        compiler_params=pltpu.CompilerParams(vmem_limit_bytes=VMEM_LIMIT),
        cost_estimate=pl.CostEstimate(flops=blk, bytes_accessed=blk, transcendentals=0),
        name="trail",
    )(given, left, high, low)


def right_rows_kernel(inverse_ref, top_ref, high_ref, low_ref, inv_high, inv_low):
    @pl.when(pl.program_id(0) == 0)
    def _():
        inv_high[...], inv_low[...] = split(inverse_ref[...])

    size = inverse_ref.shape[0]
    top_high, top_low = split(top_ref[...])
    for begin in range(0, size, 256):
        end = begin + 256
        result = product3(
            (inv_high[begin:end, :end], inv_low[begin:end, :end]), (top_high[:end], top_low[:end])
        )
        high_ref[begin:end, :], low_ref[begin:end, :] = split(result)


def right_rows(inverse, top, tile):
    size, cols = top.shape
    out = jax.ShapeDtypeStruct((size, cols), jnp.bfloat16)
    return pl.pallas_call(
        right_rows_kernel,
        grid=(cols // tile,),
        in_specs=[
            pl.BlockSpec((size, size), lambda n: (0, 0)),
            pl.BlockSpec((size, tile), lambda n: (0, n)),
        ],
        out_specs=[pl.BlockSpec((size, tile), lambda n: (0, n))] * 2,
        out_shape=[out, out],
        scratch_shapes=[pltpu.VMEM((size, size), jnp.bfloat16)] * 2,
        compiler_params=pltpu.CompilerParams(vmem_limit_bytes=VMEM_LIMIT),
        cost_estimate=pl.CostEstimate(flops=size, bytes_accessed=size, transcendentals=0),
        name="right",
    )(inverse, top)


def add_last_kernel(part_cols, blk, base, table, given_ref, *refs):
    lefts, lowers, received, out_ref = refs[:NP], refs[NP : 2 * NP], refs[2 * NP : -1], refs[-1]
    step = pl.program_id(0)

    @pl.when(step == 0)
    def _():
        out_ref[...] = jnp.zeros_like(out_ref)
        for s in range(NP):
            out_ref[0, pl.ds(s, blk, stride=part_cols), :] = lowers[s][...]

    @pl.when(step > 0)
    def _():
        own = Own(None, part_cols, 0, blk)
        for s in range(NP):
            out_ref[0, pl.ds(s, blk, stride=part_cols), :] = lefts[s][...]
        for slot in range(NP, part_cols):
            total = given_ref[:, (slot - NP) * blk : (slot - NP + 1) * blk]
            out_ref[0, pl.ds(slot, blk, stride=part_cols), :] = child_sum(
                total, table, base, slot, own, received, None
            )


def add_last(table, bases, given, left, lower, received, part_rows, part_cols, blk):
    place_base, _, where = bases

    def late(a):
        return jnp.maximum(a - 1, 0)

    def left_spec(s):
        return pl.BlockSpec((blk, blk), lambda a, t: (late(a), s * 4 + t[where + 1]))

    def lower_spec(s):
        return pl.BlockSpec((blk, blk), lambda a, t: (t[where], s * 4 + t[where + 1]))

    return pl.pallas_call(
        functools.partial(add_last_kernel, part_cols, blk, place_base),
        grid_spec=pltpu.PrefetchScalarGridSpec(
            num_scalar_prefetch=1,
            grid=(part_rows,),
            in_specs=[pl.BlockSpec((blk, given.shape[1]), lambda a, t: (late(a), 0))]
            + [left_spec(s) for s in range(NP)]
            + [lower_spec(s) for s in range(NP)]
            + [pl.BlockSpec((r.shape[0], blk, blk), lambda a, t: (0, late(a), 0)) for r in received],
            out_specs=pl.BlockSpec((1, blk * part_cols, blk), lambda a, t: (a, 0, 0)),
        ),
        out_shape=jax.ShapeDtypeStruct((part_rows, blk * part_cols, blk), given.dtype),
        compiler_params=pltpu.CompilerParams(vmem_limit_bytes=VMEM_LIMIT),
        cost_estimate=pl.CostEstimate(flops=blk, bytes_accessed=blk, transcendentals=0),
        name="add_last",
    )(table, given, *[left] * NP, *[lower] * NP, *received)


def table_layout(most, part_cols, panel_blocks):
    place = 3 * most
    square = place + 4 * part_cols
    where = square + 4 * panel_blocks
    return place, square, where, where + 8


def table_kernel(most, part_cols, panel_blocks, maps_ref, table, level_ref, ranks):
    place, square, where, size = table_layout(most, part_cols, panel_blocks)
    child_cols = maps_ref.shape[1] // 4
    row, col = lax.axis_index("row"), lax.axis_index("col")
    for i in range(size):
        table[i] = 0
    for i in range(2 * part_cols):
        table[place + 2 * i] = 4
    for i in range(4):
        ranks[i] = 0
    for g in range(child_cols):
        for member in range(2):
            turn = (maps_ref[member, 4 * g] - 4 * g) & 3
            slot = maps_ref[member, 4 * g + ((col - turn) & 3)] // 4
            entry = place + 2 * (member * part_cols + slot)
            if g < 2:
                unit = 2 * member + g
                table[entry] = jnp.where(turn == 0, 0, SHARED)
                table[entry + 1] = jnp.where(
                    turn == 0, g, ((col - turn) & 3) * (4 + NP) + unit
                )
                for j in range(4):
                    parent = maps_ref[member, 4 * g + j]

                    @pl.when(parent < panel_blocks)
                    def _():
                        table[square + 2 * (member * panel_blocks + parent)] = j * (4 + NP) + unit
                        table[square + 2 * (member * panel_blocks + parent) + 1] = 1

            else:
                rank = ranks[turn]
                ranks[turn] = rank + 1
                table[entry] = turn
                table[entry + 1] = jnp.where(turn == 0, g, rank)

                @pl.when(turn > 0)
                def _():
                    table[(turn - 1) * most + rank] = member * child_cols + g

    table[where] = row
    for i, mask in enumerate((0, 2, 1, 3)):
        table[where + 1 + i] = col ^ mask
    level = jnp.int32(len(LEVELS) - 1)
    for index in reversed(range(len(LEVELS) - 1)):
        one, two, three = LEVELS[index]
        fits = (ranks[1] <= one) & (ranks[2] <= two) & (ranks[3] <= three)
        level = jnp.where(fits, index, level)
    level_ref[0] = level


def make_table(maps, most, part_cols, panel_blocks):
    size = table_layout(most, part_cols, panel_blocks)[-1]
    scalars = pl.BlockSpec(memory_space=pltpu.SMEM)
    return pl.pallas_call(
        functools.partial(table_kernel, most, part_cols, panel_blocks),
        in_specs=[scalars],
        out_specs=[scalars] * 2,
        out_shape=[
            jax.ShapeDtypeStruct((size,), jnp.int32), jax.ShapeDtypeStruct((1,), jnp.int32)
        ],
        scratch_shapes=[pltpu.SMEM((4,), jnp.int32)],
        name="tables",
    )(maps)


def main_branch(level, most, row_count, front, updates, table):
    part_rows, blk, part_cols = front.shape[0], front.shape[2], front.shape[3]
    col_count = 4
    columns = range(col_count)

    def swap(value, mask):
        return lax.ppermute(value, "col", [(c, c ^ mask) for c in columns])

    def turned(value, turn):
        return lax.ppermute(value, "col", [(c, (c + turn) % col_count) for c in columns])

    place, square_base, where, _ = table_layout(most, part_cols, row_count)
    given, early, units, late = send_head(table, front, updates, LEVELS[level], most, level + 1)
    bases = (place, square_base, where)
    top = assemble_top(table, place, front, updates, early, given)
    top, given = lax.optimization_barrier((top, given))
    top = lax.all_gather(top, "row", axis=0, tiled=True)
    soon = min((1, 3), key=lambda turn: abs(LEVELS[level][turn - 1] - 6))
    square, arrived = gather_square(
        table, square_base, given, late[soon - 1], soon, row_count, len(LEVELS) + level + 1
    )
    units, late, square = lax.optimization_barrier((units, late, square))
    chip, core = swap(units, 2), swap(units, 1)
    lower, inverse = factorize(square, blk)
    chip, core, inverse = lax.optimization_barrier((chip, core, inverse))
    both = swap(chip, 1)
    late = [
        arrived if turn == soon else turned(late[turn - 1], turn) for turn in range(1, col_count)
    ]
    result, left = prepare(
        table, bases, front, updates, (units, chip, core, both), inverse, row_count, col_count
    )
    result, top = lax.optimization_barrier((result, top))
    high, low = right_rows(inverse, top, 2 * blk)
    result = trail(result, left, high, low, blk)
    result, late = lax.optimization_barrier((result, late))
    return add_last(table, bases, result, left, lower, late, part_rows, part_cols, blk)


def body(row_count, col_count, front, updates, maps):
    part_rows = front.shape[0]
    if part_rows < 3 or row_count != NP * col_count or col_count != 4:
        return simple_body(front, updates, maps)
    front = front.reshape(front.shape[0], 1, *front.shape[2:4], front.shape[5])
    blk, part_cols = front.shape[2], front.shape[3]
    most = updates.shape[4]
    table, level = make_table(maps, most, part_cols, row_count)
    branches = [
        functools.partial(main_branch, level, most, row_count) for level in range(len(LEVELS))
    ]
    result = lax.switch(level[0], branches, front, updates, table)
    return result.reshape(part_rows, 1, blk, part_cols, 1, blk)


def solution(mesh):
    return jax.shard_map(
        functools.partial(body, mesh.shape["row"], mesh.shape["col"]),
        mesh=mesh,
        in_specs=(
            P(None, "row", None, None, "col", None),
            P(None, None, "row", None, None, "col", None),
            P(),
        ),
        out_specs=P(None, "row", None, None, "col", None),
        check_vma=False,
    )
```

```python
import functools

import jax
import jax.numpy as jnp
from jax import lax
from jax.experimental import pallas as pl
from jax.experimental.pallas import tpu as pltpu
from jax.sharding import PartitionSpec as P

NP = 2
highest = lax.Precision.HIGHEST
VMEM_LIMIT = 56 * 1024 * 1024
MESH = pl.DeviceIdType.MESH
SHARED = 5
LEVELS = (
    (6, 5, 8), (4, 8, 10), (8, 2, 9), (10, 4, 12), (10, 6, 6), (8, 9, 4), (6, 10, 8), (12, 8, 9),
    (12, 12, 12),
)


def split(value):
    high = value.astype(jnp.bfloat16)
    low = (value - high.astype(jnp.float32)).astype(jnp.bfloat16)
    return high, low


def dims(transposed):
    return (((1,), (1 if transposed else 0,)), ((), ()))


def product3(left_pair, right_pair, transposed=False):
    def one(a, b):
        return lax.dot_general(a, b, dims(transposed), preferred_element_type=jnp.float32)

    return (
        one(left_pair[0], right_pair[0])
        + one(left_pair[0], right_pair[1])
        + one(left_pair[1], right_pair[0])
    )


def product(a, b, transposed=False):
    return lax.dot_general(
        a, b, dims(transposed), precision=highest, preferred_element_type=jnp.float32
    )


def pack_kernel(child_cols, cap, blk, table, updates_ref, one_ref, two_ref, three_ref):
    for turn, out_ref in enumerate((one_ref, two_ref, three_ref)):
        for member in range(2):
            for slot in range(cap):
                source = table[(turn + 1) * 2 * cap + member * cap + slot]
                out_ref[member * cap + slot] = updates_ref[
                    member, 0, pl.ds(source, blk, stride=child_cols), :
                ]


def pack(table, updates, cap, begin, count):
    part_rows, blk, child_cols = updates.shape[1], updates.shape[3], updates.shape[4]
    flat = updates.reshape(2, part_rows, blk * child_cols, blk)
    return pl.pallas_call(
        functools.partial(pack_kernel, child_cols, cap, blk),
        grid_spec=pltpu.PrefetchScalarGridSpec(
            num_scalar_prefetch=1,
            grid=(count,),
            in_specs=[
                pl.BlockSpec((2, 1, blk * child_cols, blk), lambda a, t: (0, a + begin, 0, 0))
            ],
            out_specs=[pl.BlockSpec((2 * cap, blk, blk), lambda a, t: (0, a, 0))] * 3,
        ),
        out_shape=[jax.ShapeDtypeStruct((2 * cap, count * blk, blk), jnp.float32)] * 3,
        compiler_params=pltpu.CompilerParams(vmem_limit_bytes=VMEM_LIMIT),
        name="pack",
    )(table, flat)


def add_children(out_ref, table, front_ref, updates_ref, received, slots, part_cols, child_cols, blk):
    for slot in slots:
        cols = slice(slot * blk, (slot + 1) * blk)
        out_ref[:, cols] = front_ref[0, pl.ds(slot, blk, stride=part_cols), :]
        for member in range(2):
            turn = table[(member * part_cols + slot) * 2]
            index = table[(member * part_cols + slot) * 2 + 1]

            @pl.when(turn == 0)
            def _():
                out_ref[:, cols] += updates_ref[member, 0, pl.ds(index, blk, stride=child_cols), :]

            for step in range(3):

                @pl.when(turn == step + 1)
                def _():
                    out_ref[:, cols] += received[step][index]


def assemble(table, front, updates, received, begin, count, width):
    part_rows, blk, part_cols = front.shape[0], front.shape[2], front.shape[3]
    child_cols = updates.shape[4]
    slots = received[0].shape[0]

    def kernel(table, front_ref, updates_ref, one, two, three, out_ref):
        add_children(
            out_ref, table, front_ref, updates_ref, (one, two, three),
            range(width), part_cols, child_cols, blk,
        )

    return pl.pallas_call(
        kernel,
        grid_spec=pltpu.PrefetchScalarGridSpec(
            num_scalar_prefetch=1,
            grid=(count,),
            in_specs=[
                pl.BlockSpec((1, blk * part_cols, blk), lambda a, t: (a + begin, 0, 0)),
                pl.BlockSpec((2, 1, blk * child_cols, blk), lambda a, t: (0, a + begin, 0, 0)),
            ]
            + [pl.BlockSpec((slots, blk, blk), lambda a, t: (0, a, 0))] * 3,
            out_specs=pl.BlockSpec((blk, width * blk), lambda a, t: (a, 0)),
        ),
        out_shape=jax.ShapeDtypeStruct((count * blk, width * blk), jnp.float32),
        compiler_params=pltpu.CompilerParams(vmem_limit_bytes=VMEM_LIMIT),
        name="assemble",
    )(
        table,
        front.reshape(part_rows, blk * part_cols, blk),
        updates.reshape(2, part_rows, blk * child_cols, blk),
        *received,
    )


def eliminate(block):
    size = block.shape[0]
    group = 8
    tiles = size // group
    shape = (group, size)
    row_ids = lax.broadcasted_iota(jnp.int32, (size, size), 0)
    col_ids = lax.broadcasted_iota(jnp.int32, (size, size), 1)
    local = lax.broadcasted_iota(jnp.int32, shape, 0)
    start = (row_ids == col_ids).astype(jnp.float32)
    upper = [block[group * t : group * (t + 1), :] for t in range(tiles)]
    solved = [start[group * t : group * (t + 1), :] for t in range(tiles)]
    for h in range(tiles):
        def column(t, j):
            return jnp.broadcast_to(upper[t][:, group * h + j : group * h + j + 1], shape)
        home = [column(h, j) for j in range(group)]
        pivot = {
            (i, j): jnp.broadcast_to(home[j][i : i + 1, :], shape)
            for j in range(group) for i in range(j, group)
        }
        scale, ratio = [], {}
        for j in range(group):
            scale.append(1.0 / pivot[j, j])
            for i in range(j + 1, group):
                ratio[i, j] = pivot[i, j] * scale[j]
            for k in range(j + 1, group):
                for i in range(k, group):
                    pivot[i, k] = pivot[i, k] - ratio[i, j] * pivot[k, j]
        upper_rows, solved_rows = [], []
        for j in range(group):
            u = jnp.broadcast_to(upper[h][j : j + 1, :], shape)
            s = jnp.broadcast_to(solved[h][j : j + 1, :], shape)
            for i in range(j):
                u = u - ratio[j, i] * upper_rows[i]
                s = s - ratio[j, i] * solved_rows[i]
            upper_rows.append(u)
            solved_rows.append(s)
        for t in range(h, tiles):
            if t == h:
                u, s = upper_rows[0], solved_rows[0]
                for j in range(1, group):
                    u = jnp.where(local == j, upper_rows[j], u)
                    s = jnp.where(local == j, solved_rows[j], s)
                upper[t], solved[t] = u, s
                continue
            factors = []
            for j in range(group):
                c = column(t, j)
                for i in range(j):
                    c = c - factors[i] * pivot[j, i]
                factors.append(c * scale[j])
            for j in range(group):
                upper[t] = upper[t] - factors[j] * upper_rows[j]
                solved[t] = solved[t] - factors[j] * solved_rows[j]
    upper = jnp.concatenate(upper, axis=0)
    solved = jnp.concatenate(solved, axis=0)
    diagonal = jnp.sum(jnp.where(row_ids == col_ids, upper, 0.0), axis=1, keepdims=True)
    scale = 1.0 / jnp.sqrt(diagonal)
    lower = jnp.where(col_ids >= row_ids, upper * scale, 0.0).T
    return lower, solved * scale

def factor_kernel(blk, square_ref, lower_ref, inverse_ref, work):
    size = square_ref.shape[0]
    count = size // blk
    work[...] = square_ref[...]
    lower_ref[...] = jnp.zeros_like(lower_ref)
    inverse_ref[...] = jnp.zeros_like(inverse_ref)

    def spread(k, diag_inverse):
        begin, end = k * blk, (k + 1) * blk
        here = slice(begin, end)
        inverse_pair = split(diag_inverse)
        if k:
            done = product3(inverse_pair, split(inverse_ref[here, :begin]))
            inverse_ref[here, :begin] = done
        inverse_ref[here, here] = diag_inverse
        if end == size:
            return
        row_high, row_low = split(inverse_ref[here, :end])
        left_high, left_low = [], []
        for q in range(end, size, 256):
            top = min(q + 256, size)
            left = product3(split(work[q:top, here]), inverse_pair, True)
            lower_ref[q:top, here] = left
            high, low = split(left)
            left_high.append(high)
            left_low.append(low)
        high = jnp.concatenate(left_high, axis=0)
        low = jnp.concatenate(left_low, axis=0)
        for q in range(end, size, 256):
            top = min(q + 256, size)
            pair = high[q - end : top - end], low[q - end : top - end]
            below = high[: top - end], low[: top - end]
            work[q:top, end:top] -= product3(pair, below, True)
            inverse_ref[q:top, :end] -= product3(pair, (row_high, row_low))

    def step(k, carry):
        begin = pl.multiple_of(k * blk, blk)
        here = pl.ds(begin, blk)
        diag_lower, diag_inverse = eliminate(work[here, here])
        lower_ref[here, here] = diag_lower
        for t in range(count):
            pl.when(k == t)(functools.partial(spread, t, diag_inverse))
        return carry

    lax.fori_loop(0, count, step, 0)


def factorize(square, blk):
    size = square.shape[0]
    shape = jax.ShapeDtypeStruct((size, size), jnp.float32)
    return pl.pallas_call(
        functools.partial(factor_kernel, blk),
        out_shape=[shape, shape],
        scratch_shapes=[pltpu.VMEM((size, size), jnp.float32)],
        compiler_params=pltpu.CompilerParams(vmem_limit_bytes=VMEM_LIMIT),
        cost_estimate=pl.CostEstimate(flops=size, bytes_accessed=size, transcendentals=0),
        name="factorize",
    )(square)


def right_kernel(inverse_ref, top_ref, high_ref, low_ref, inv_high, inv_low):
    @pl.when(pl.program_id(0) == 0)
    def _():
        inv_high[...], inv_low[...] = split(inverse_ref[...])

    result = product3((inv_high[...], inv_low[...]), split(top_ref[...]))
    high_ref[...], low_ref[...] = split(result)


def right_side(inverse, top, tile):
    size, cols = top.shape
    out = jax.ShapeDtypeStruct((size, cols), jnp.bfloat16)
    return pl.pallas_call(
        right_kernel,
        grid=(cols // tile,),
        in_specs=[
            pl.BlockSpec((size, size), lambda n: (0, 0)),
            pl.BlockSpec((size, tile), lambda n: (0, n)),
        ],
        out_specs=[pl.BlockSpec((size, tile), lambda n: (0, n))] * 2,
        out_shape=[out, out],
        scratch_shapes=[pltpu.VMEM((size, size), jnp.bfloat16)] * 2,
        compiler_params=pltpu.CompilerParams(vmem_limit_bytes=VMEM_LIMIT),
        cost_estimate=pl.CostEstimate(flops=size, bytes_accessed=size, transcendentals=0),
        name="right",
    )(inverse, top)


def finish_kernel(
    part_cols, child_cols, blk, row_count, col_count, first, table, place,
    panel_ref, front_ref, updates_ref, one, two, three, inverse_ref, lower_ref, high_ref, low_ref,
    out_ref, inv_high, inv_low, left_ref, sum_ref,
):
    step = pl.program_id(0)
    block_row = step * row_count + place[0]
    panel_blocks = NP * col_count
    inside = block_row < panel_blocks
    columns = [pl.multiple_of((s * col_count + place[1]) * blk, blk) for s in range(NP)]

    @pl.when(step == 0)
    def _():
        inv_high[...], inv_low[...] = split(inverse_ref[...])

    @pl.when(jnp.logical_not(inside))
    def _():
        add_children(
            sum_ref, table, front_ref, updates_ref, (one, two, three),
            range(NP, part_cols), part_cols, child_cols, blk,
        )
        panel = jnp.concatenate(
            [
                panel_ref[c, :, s * blk : (s + 1) * blk]
                for s in range(NP)
                for c in range(col_count)
            ],
            axis=1,
        )
        left_ref[...] = product3(split(panel), (inv_high[...], inv_low[...]), True)
        left_pair = split(left_ref[...])
        for pair in range(NP, part_cols, 2):
            cols = slice((pair - NP) * blk, (pair - NP + 2) * blk)
            trailing = product3(left_pair, (high_ref[:, cols], low_ref[:, cols]))
            updated = sum_ref[:, pair * blk : (pair + 2) * blk] - trailing
            for half in range(2):
                out_ref[0, pl.ds(pair + half, blk, stride=part_cols), :] = updated[
                    :, half * blk : (half + 1) * blk
                ]
        for s in range(NP):
            out_ref[0, pl.ds(s, blk, stride=part_cols), :] = left_ref[:, pl.ds(columns[s], blk)]

    @pl.when(inside)
    def _():
        out_ref[...] = jnp.zeros_like(out_ref)
        begin = pl.multiple_of(block_row * blk, blk)
        for s in range(NP):
            out_ref[0, pl.ds(s, blk, stride=part_cols), :] = lower_ref[
                pl.ds(begin, blk), pl.ds(columns[s], blk)
            ]


def finish(table, place, panel, front, updates, received, inverse, lower, high, low, row_count, first):
    part_rows, blk, part_cols = front.shape[0], front.shape[2], front.shape[3]
    child_cols = updates.shape[4]
    size = inverse.shape[0]
    slots = received[0].shape[0]
    col_count = panel.shape[0]

    def resident(shape):
        return pl.BlockSpec(shape, lambda a, t, p: (0, 0), pipeline_mode=pl.Buffered(1))

    def late(a, t, p):
        return (0, jnp.maximum(a - first, 0), 0)

    return pl.pallas_call(
        functools.partial(finish_kernel, part_cols, child_cols, blk, row_count, col_count, first),
        grid_spec=pltpu.PrefetchScalarGridSpec(
            num_scalar_prefetch=2,
            grid=(part_rows,),
            in_specs=[
                pl.BlockSpec((col_count, blk, NP * blk), late),
                pl.BlockSpec((1, blk * part_cols, blk), lambda a, t, p: (a, 0, 0)),
                pl.BlockSpec((2, 1, blk * child_cols, blk), lambda a, t, p: (0, a, 0, 0)),
            ]
            + [pl.BlockSpec((slots, blk, blk), late)] * 3
            + [
                resident((size, size)),
                resident((size, size)),
                resident(high.shape),
                resident(low.shape),
            ],
            out_specs=pl.BlockSpec((1, blk * part_cols, blk), lambda a, t, p: (a, 0, 0)),
            scratch_shapes=[
                pltpu.VMEM((size, size), jnp.bfloat16),
                pltpu.VMEM((size, size), jnp.bfloat16),
                pltpu.VMEM((blk, size), jnp.float32),
                pltpu.VMEM((blk, part_cols * blk), jnp.float32),
            ],
        ),
        out_shape=jax.ShapeDtypeStruct((part_rows, blk * part_cols, blk), jnp.float32),
        compiler_params=pltpu.CompilerParams(vmem_limit_bytes=VMEM_LIMIT),
        name="finish",
    )(
        table, place, panel,
        front.reshape(part_rows, blk * part_cols, blk),
        updates.reshape(2, part_rows, blk * child_cols, blk),
        *received, inverse, lower, high, low,
    )


def tables(maps, col_index, col_count, child_cols, part_cols, cap):
    offsets = maps[:, ::col_count] - col_count * jnp.arange(child_cols, dtype=jnp.int32)[None, :]
    turn = offsets % col_count
    groups = jnp.arange(child_cols, dtype=jnp.int32)
    same = (turn[:, :, None] == turn[:, None, :]) & (groups[None, None, :] < groups[None, :, None])
    rank = jnp.sum(same.astype(jnp.int32), axis=2)
    turns = jnp.arange(col_count, dtype=jnp.int32)
    slots = jnp.arange(cap, dtype=jnp.int32)
    hot = (turn[None, :, None, :] == turns[:, None, None, None]) & (
        rank[None, :, None, :] == slots[None, None, :, None]
    )
    send = jnp.sum(jnp.where(hot, groups[None, None, None, :], 0), axis=3).reshape(-1)
    parents = jnp.arange(part_cols, dtype=jnp.int32) * col_count + col_index
    match = maps[:, None, :] == parents[None, :, None]
    spread = jnp.repeat(groups, col_count)
    group = jnp.sum(jnp.where(match, spread[None, None, :], 0), axis=2)
    present = jnp.any(match, axis=2)
    pick = group[:, :, None] == groups[None, None, :]
    kind = jnp.sum(jnp.where(pick, turn[:, None, :], 0), axis=2)
    order = jnp.sum(jnp.where(pick, rank[:, None, :], 0), axis=2)
    order = jnp.where(kind == 0, group, order + cap * jnp.arange(2, dtype=jnp.int32)[:, None])
    kind = jnp.where(present, kind, col_count)
    place = jnp.stack([kind, order], axis=2).reshape(-1)
    return send, place


def gather_top(piece, row_count, row_index, panel_blocks):
    if row_count == panel_blocks:
        return lax.all_gather(piece, "row", axis=0, tiled=True)
    ids = jnp.arange(panel_blocks, dtype=jnp.int32)
    kept = jnp.where((ids == row_index)[:, None, None], piece[None], 0.0)
    return lax.psum(kept, "row").reshape(panel_blocks * piece.shape[0], piece.shape[1])


def simple_body(front, updates, maps):
    row_count = lax.axis_size("row")
    col_count = lax.axis_size("col")
    row_index = lax.axis_index("row")
    col_index = lax.axis_index("col")
    front = front.reshape(front.shape[0], 1, *front.shape[2:4], front.shape[5])
    blk, part_cols = front.shape[2], front.shape[3]
    child_cols = updates.shape[4]
    cap = child_cols // 2
    panel_blocks = NP * col_count
    send, place = tables(maps, col_index, col_count, child_cols, part_cols, cap)
    part_rows = front.shape[0]
    first = 1 if part_rows > 1 and row_count == panel_blocks else part_rows

    def exchange(outgoing):
        return [
            lax.ppermute(
                outgoing[turn - 1], "col", [(c, (c + turn) % col_count) for c in range(col_count)]
            )
            for turn in range(1, col_count)
        ]

    early = exchange(pack(send, updates, cap, 0, first))
    if first < part_rows:
        outgoing = pack(send, updates, cap, first, part_rows - first)
        early, outgoing = lax.optimization_barrier((early, outgoing))
        received = exchange(outgoing)
    else:
        received = early
    head = assemble(place, front, updates, early, 0, 1, part_cols)
    square = jnp.concatenate(
        [
            lax.all_gather(head[:, s * blk : (s + 1) * blk], "col", axis=1, tiled=True)
            for s in range(NP)
        ],
        axis=1,
    )
    square = gather_top(square, row_count, row_index, panel_blocks)
    rest, square = lax.optimization_barrier((head[:, NP * blk :], square))
    top = gather_top(rest, row_count, row_index, panel_blocks)
    lower, inverse = factorize(square, blk)
    high, low = right_side(inverse, top, 2 * blk)
    received, high, low = lax.optimization_barrier((received, high, low))
    late = first if first < part_rows else 0
    panel = assemble(place, front, updates, received, late, part_rows - late, NP)
    panel = lax.all_gather(panel, "col", axis=0)
    where = jnp.stack([row_index, col_index]).astype(jnp.int32)
    result = finish(
        place, where, panel, front, updates, received, inverse, lower, high, low, row_count, late
    )
    return result.reshape(front.shape[0], 1, blk, part_cols, 1, blk)


def send_kernel(
    blk, caps, most, table, front_ref, updates_ref, units_ref, columns_ref,
    got_one, got_two, got_three, panel_ref, late_one, late_two, late_three,
    front_part, updates_part, columns, units, first, stage, stage_one, stage_two, stage_three,
    local, keep_sem, send, recv, out_sem,
):
    row, col = lax.axis_index("row"), lax.axis_index("col")
    part_rows = front_ref.shape[0]
    part_cols = front_part.shape[1] // blk
    child_cols = updates_part.shape[2] // blk
    width = units.shape[0]
    stages = (stage_one, stage_two, stage_three)

    def loads(a, side):
        copies = [pltpu.make_async_copy(front_ref.at[a], front_part.at[side], local.at[side, 0])]
        for member in range(2):
            copies.append(
                pltpu.make_async_copy(
                    updates_ref.at[member, a], updates_part.at[side, member],
                    local.at[side, 1 + member],
                )
            )
        return copies

    for load in loads(0, 0):
        load.start()
    for load in loads(1, 1):
        load.start()
    others = [lax.rem(col + turn, 4) for turn in range(1, 4)]
    barrier = pltpu.get_barrier_semaphore()
    for other in others:
        pl.semaphore_signal(barrier, inc=1, device_id=(row, other), device_id_type=MESH)

    def spread(side, target):
        def unpack(g, carry):
            for member in range(2):
                columns[member * child_cols + g] = updates_part[
                    side, member, pl.ds(g, blk, stride=child_cols), :
                ]
            return carry

        lax.fori_loop(0, child_cols, unpack, 0)
        for member in range(2):
            for g in range(2):
                target[member * 2 + g] = columns[member * child_cols + g]
        for s in range(NP):
            target[4 + s] = front_part[side, pl.ds(s, blk, stride=part_cols), :]

    def fill(target, turn):
        def put(slot, carry):
            target[slot] = columns[table[turn * most + slot]]
            return carry

        lax.fori_loop(0, caps[turn], put, 0)

    for load in loads(0, 0):
        load.wait()
    spread(0, units)
    pl.semaphore_wait(barrier, 3)

    def remote(source, target, index, device):
        return pltpu.make_async_remote_copy(
            src_ref=source, dst_ref=target, send_sem=send.at[index], recv_sem=recv.at[index],
            device_id=(row, device), device_id_type=MESH,
        )

    across = remote(units, units_ref.at[pl.ds(col * width, width)], 3, others[1])
    across.start()
    keep = [
        pltpu.make_async_copy(units, units_ref.at[pl.ds(col * width, width)], keep_sem.at[0]),
        pltpu.make_async_copy(columns, columns_ref, keep_sem.at[1]),
    ]
    for move in keep:
        move.start()
    other_core = col + 1 - 2 * lax.rem(col, 2)

    def beside(owner, index):
        section = units_ref.at[pl.ds(owner * width, width)]
        source = units if index == 4 else section
        return remote(source, section, index, other_core)

    mine = beside(col, 4)
    mine.start()
    moves = []
    begin = 0
    for turn, target in enumerate((got_one, got_two, got_three)):
        fill(first.at[pl.ds(begin, caps[turn])], turn)
        moves.append(remote(first.at[pl.ds(begin, caps[turn])], target, turn, others[turn]))
        moves[-1].start()
        begin += caps[turn]

    def stores(a, side):
        rows = pl.ds(pl.multiple_of((a - 1) * blk, blk), blk)
        copies = [pltpu.make_async_copy(stage.at[side], panel_ref.at[:, rows, :], out_sem.at[side, 0])]
        for turn, target in enumerate((late_one, late_two, late_three)):
            copies.append(
                pltpu.make_async_copy(
                    stages[turn].at[side], target.at[:, rows, :], out_sem.at[side, 1 + turn]
                )
            )
        return copies

    def step(a, carry):
        side = lax.rem(a, 2)
        for load in loads(a, side):
            load.wait()

        @pl.when(a + 1 < part_rows)
        def _():
            for load in loads(a + 1, 1 - side):
                load.start()

        @pl.when(a > 2)
        def _():
            for store in stores(a - 2, side):
                store.wait()

        spread(side, stage.at[side])
        for turn in range(3):
            fill(stages[turn].at[side], turn)
        for store in stores(a, side):
            store.start()
        return carry

    keep[1].wait()
    lax.fori_loop(1, part_rows, step, 0)
    for a in range(max(1, part_rows - 2), part_rows):
        for store in stores(a, a % 2):
            store.wait()
    keep[0].wait()
    across.wait_send()
    remote(units, units_ref.at[pl.ds(others[1] * width, width)], 3, others[1]).wait_recv()
    passed = beside(others[1], 5)
    passed.start()
    for index, owner in enumerate((other_core, lax.rem(other_core + 2, 4))):
        beside(owner, 4 + index).wait_recv()
    for move in (mine, passed):
        move.wait_send()
    for move in moves:
        move.wait()


def send_head(table, front, updates, caps, most, identity):
    part_rows, blk, part_cols = front.shape[0], front.shape[2], front.shape[3]
    child_cols = updates.shape[4]
    anywhere = pl.BlockSpec(memory_space=pl.ANY)
    width = 4 + NP
    rest = (part_rows - 1) * blk
    shapes = [(4 * width, blk, blk), (2 * child_cols, blk, blk)] + [(cap, blk, blk) for cap in caps]
    shapes += [(width, rest, blk)] + [(cap, rest, blk) for cap in caps]
    outs = pl.pallas_call(
        functools.partial(send_kernel, blk, caps, most),
        in_specs=[pl.BlockSpec(memory_space=pltpu.SMEM), anywhere, anywhere],
        out_specs=[anywhere] * 9,
        out_shape=[jax.ShapeDtypeStruct(shape, jnp.float32) for shape in shapes],
        scratch_shapes=[
            pltpu.VMEM((2, blk * part_cols, blk), jnp.float32),
            pltpu.VMEM((2, 2, blk * child_cols, blk), jnp.float32),
            pltpu.VMEM((2 * child_cols, blk, blk), jnp.float32),
            pltpu.VMEM((width, blk, blk), jnp.float32),
            pltpu.VMEM((sum(caps), blk, blk), jnp.float32),
            pltpu.VMEM((2, width, blk, blk), jnp.float32),
        ]
        + [pltpu.VMEM((2, cap, blk, blk), jnp.float32) for cap in caps]
        + [
            pltpu.SemaphoreType.DMA((2, 3)),
            pltpu.SemaphoreType.DMA((2,)),
            pltpu.SemaphoreType.DMA((6,)),
            pltpu.SemaphoreType.DMA((6,)),
            pltpu.SemaphoreType.DMA((2, 4)),
        ],
        compiler_params=pltpu.CompilerParams(
            vmem_limit_bytes=VMEM_LIMIT, collective_id=identity, has_side_effects=True
        ),
        cost_estimate=pl.CostEstimate(flops=blk, bytes_accessed=blk, transcendentals=0),
        name="send",
    )(
        table,
        front.reshape(part_rows, blk * part_cols, blk),
        updates.reshape(2, part_rows, blk * child_cols, blk),
    )
    return outs[0], outs[1], outs[2:5], outs[5], outs[6:]


def square_kernel(
    blk, row_count, turn, bases, table, given_ref, sent_ref, front_ref, columns_ref,
    early_one, early_two, early_three, square_ref, got_ref, top_ref,
    work, units, front_part, columns, one, two, three, top, local, line_send, line_recv, core_send, core_recv, turn_send, turn_recv,
):
    row, col = lax.axis_index("row"), lax.axis_index("col")
    width = units.shape[0] // 4
    half = row_count // 2
    core = lax.rem(col, 2)
    other_core = col + 1 - 2 * core
    other_chip = lax.rem(col + 2, 4)
    diagonal = lax.rem(other_core + 2, 4)

    part_cols = front_part.shape[0] // blk
    early = ((1, one), (2, two), (3, three))
    loads = [
        pltpu.make_async_copy(source, target, local.at[index])
        for index, (source, target) in enumerate(
            (
                (given_ref, units), (front_ref.at[0], front_part), (columns_ref, columns),
                (early_one, one), (early_two, two), (early_three, three),
            )
        )
    ]
    for load in loads:
        load.start()

    def ring_row(position):
        position = lax.rem(position + row_count, row_count)
        return jnp.where(position < half, 2 * position, 2 * (row_count - position) - 1)

    place = jnp.where(lax.rem(row, 2) == 0, row // 2, row_count - 1 - row // 2)
    right, left = ring_row(place + 1), ring_row(place - 1)
    barrier = pltpu.get_barrier_semaphore()
    for device in (
        (row, other_core), (row, other_chip), (row, diagonal), (right, col), (left, col)
    ):
        pl.semaphore_signal(barrier, inc=1, device_id=device, device_id_type=MESH)
    for load in loads:
        load.wait()
    pl.semaphore_wait(barrier, 5)
    turned = pltpu.make_async_remote_copy(
        src_ref=sent_ref, dst_ref=got_ref, send_sem=turn_send, recv_sem=turn_recv,
        device_id=(row, lax.rem(col + turn, 4)), device_id_type=MESH,
    )
    turned.start()

    here = pl.multiple_of(row * blk, blk)
    for q in range(row_count):
        s, owner = q // 4, q % 4
        total = units[owner * width + 4 + s]
        for member in range(2):
            entry = bases[1] + 2 * (member * row_count + q)
            total = total + units[table[entry]] * table[entry + 1].astype(jnp.float32)
        work[pl.ds(here, blk), q * blk : (q + 1) * blk] = total

    cols = work.shape[1] // 2

    def part(position, side):
        begin = pl.multiple_of(ring_row(position) * blk, blk)
        return work.at[pl.ds(begin, blk), pl.ds(pl.multiple_of(side * cols, cols), cols)]

    def copy(ref, device, send, recv):
        return pltpu.make_async_remote_copy(
            src_ref=ref, dst_ref=ref, send_sem=send, recv_sem=recv,
            device_id=device, device_id_type=MESH,
        )

    pending = []
    for step in range(half):
        ways = range(2 if step < half - 1 else 1)
        for way in ways:
            position = place - step if way == 0 else place + step
            target = right if way == 0 else left
            move = copy(
                part(position, core), (target, col), line_send.at[way, step], line_recv.at[way, step]
            )
            move.start()
            pending.append(move)
        for slot in range(NP + step, part_cols, half):
            top[:, (slot - NP) * blk : (slot - NP + 1) * blk] = child_sum(
                front_part[pl.ds(slot, blk, stride=part_cols), :],
                table, bases[0], slot, part_cols, columns, early, units,
            )
        for way in ways:
            origin = place - step - 1 if way == 0 else place + step + 1
            landed = part(origin, core)
            copy(
                landed, (right, col), line_send.at[way, step], line_recv.at[way, step]
            ).wait_recv()
            forward = copy(
                landed, (row, other_core), core_send.at[way, step], core_recv.at[way, step]
            )
            forward.start()
            pending.append(forward)
    for way in range(2):
        for step in range(half - way):
            origin = place - step - 1 if way == 0 else place + step + 1
            copy(
                part(origin, 1 - core), (row, other_core),
                core_send.at[way, step], core_recv.at[way, step],
            ).wait_recv()
    stores = [
        pltpu.make_async_copy(work, square_ref, local.at[0]),
        pltpu.make_async_copy(top, top_ref, local.at[1]),
    ]
    for store in stores:
        store.start()
    for move in pending:
        move.wait_send()
    for store in stores:
        store.wait()
    turned.wait()


def gather_square(table, bases, given, sent, turn, front, columns, early, row_count, identity):
    part_rows, blk, part_cols = front.shape[0], front.shape[2], front.shape[3]
    size = row_count * blk
    half = row_count // 2
    anywhere = pl.BlockSpec(memory_space=pl.ANY)
    top = jax.ShapeDtypeStruct((blk, (part_cols - NP) * blk), jnp.float32)
    return pl.pallas_call(
        functools.partial(square_kernel, blk, row_count, turn, bases),
        in_specs=[pl.BlockSpec(memory_space=pltpu.SMEM)] + [anywhere] * 7,
        out_specs=[anywhere] * 3,
        out_shape=[
            jax.ShapeDtypeStruct((size, size), jnp.float32),
            jax.ShapeDtypeStruct(sent.shape, jnp.float32),
            top,
        ],
        scratch_shapes=[
            pltpu.VMEM((size, size), jnp.float32),
            pltpu.VMEM(given.shape, jnp.float32),
            pltpu.VMEM((blk * part_cols, blk), jnp.float32),
            pltpu.VMEM(columns.shape, jnp.float32),
        ]
        + [pltpu.VMEM(e.shape, jnp.float32) for e in early]
        + [
            pltpu.VMEM(top.shape, jnp.float32),
            pltpu.SemaphoreType.DMA((6,)),
            pltpu.SemaphoreType.DMA((2, half)),
            pltpu.SemaphoreType.DMA((2, half)),
            pltpu.SemaphoreType.DMA((2, half)),
            pltpu.SemaphoreType.DMA((2, half)),
            pltpu.SemaphoreType.DMA,
            pltpu.SemaphoreType.DMA,
        ],
        compiler_params=pltpu.CompilerParams(
            vmem_limit_bytes=VMEM_LIMIT, collective_id=identity, has_side_effects=True
        ),
        cost_estimate=pl.CostEstimate(flops=size, bytes_accessed=size, transcendentals=0),
        name="square",
    )(table, given, sent, front.reshape(part_rows, blk * part_cols, blk), columns, *early)


def pick(kind, index, wanted):
    hit = kind == wanted
    return jnp.where(hit, index, 0), hit.astype(jnp.float32)


def child_sum(total, table, base, slot, part_cols, columns, received, shared):
    for member in range(2):
        entry = base + (member * part_cols + slot) * 2
        kind, index = table[entry], table[entry + 1]
        if columns is not None:
            at, weight = pick(kind, index, 0)
            total = total + weight * columns[member * (columns.shape[0] // 2) + at]
        if shared is not None:
            at, weight = pick(kind, index, SHARED)
            total = total + weight * shared[at]
        for turn, ref in received:
            at, weight = pick(kind, index, turn)
            total = total + weight * ref[at]
    return total


def prepare_kernel(
    part_cols, child_cols, blk, row_count, col_count, bases, soon, table,
    front_ref, updates_ref, own, chip, core, both, arrived, inverse_ref,
    sum_ref, left_ref, inv_high, inv_low, units, panel_ref,
):
    place_base, square_base, where = bases
    size = inverse_ref.shape[0]

    @pl.when(pl.program_id(0) == 0)
    def _():
        inv_high[...], inv_low[...] = split(inverse_ref[...])

    width = own.shape[0]
    for order, ref in enumerate((own, chip, core, both)):
        owner = table[where + 1 + order]
        for i in range(width):
            units[owner * width + i] = ref[i]
    for q in range(row_count):
        total = units[(q % col_count) * width + 4 + q // col_count]
        for member in range(2):
            entry = square_base + 2 * (member * row_count + q)
            total = total + units[table[entry]] * table[entry + 1].astype(jnp.float32)
        panel_ref[:, q * blk : (q + 1) * blk] = total
    for slot in range(NP, part_cols):
        cols = slice((slot - NP) * blk, (slot - NP + 1) * blk)
        sum_ref[:, cols] = child_sum(
            front_ref[0, pl.ds(slot, blk, stride=part_cols), :],
            table, place_base, slot, part_cols, None, ((soon, arrived),), units,
        )
    for slot in range(NP, part_cols):
        cols = slice((slot - NP) * blk, (slot - NP + 1) * blk)
        for member in range(2):
            entry = place_base + (member * part_cols + slot) * 2

            @pl.when(table[entry] == 0)
            def _():
                sum_ref[:, cols] += updates_ref[
                    member, 0, pl.ds(table[entry + 1], blk, stride=child_cols), :
                ]

    panel_pair = split(panel_ref[...])
    for begin in range(0, size, 2 * blk):
        end = begin + 2 * blk
        left_ref[:, begin:end] = product3(
            tuple(p[:, :end] for p in panel_pair),
            (inv_high[begin:end, :end], inv_low[begin:end, :end]),
            True,
        )


def prepare(table, bases, front, updates, gathered, arrived, soon, inverse, row_count, col_count):
    part_rows, blk, part_cols = front.shape[0], front.shape[2], front.shape[3]
    child_cols = updates.shape[4]
    size = inverse.shape[0]
    rows, width = (part_rows - 1) * blk, (part_cols - NP) * blk
    return pl.pallas_call(
        functools.partial(
            prepare_kernel, part_cols, child_cols, blk, row_count, col_count, bases, soon
        ),
        grid_spec=pltpu.PrefetchScalarGridSpec(
            num_scalar_prefetch=1,
            grid=(part_rows - 1,),
            in_specs=[
                pl.BlockSpec((1, blk * part_cols, blk), lambda a, t: (a + 1, 0, 0)),
                pl.BlockSpec((2, 1, blk * child_cols, blk), lambda a, t: (0, a + 1, 0, 0)),
            ]
            + [pl.BlockSpec((g.shape[0], blk, blk), lambda a, t: (0, a, 0)) for g in (*gathered, arrived)]
            + [pl.BlockSpec((size, size), lambda a, t: (0, 0), pipeline_mode=pl.Buffered(1))],
            out_specs=[
                pl.BlockSpec((blk, width), lambda a, t: (a, 0)),
                pl.BlockSpec((blk, size), lambda a, t: (a, 0)),
            ],
            scratch_shapes=[
                pltpu.VMEM((size, size), jnp.bfloat16),
                pltpu.VMEM((size, size), jnp.bfloat16),
                pltpu.VMEM((4 * (4 + NP), blk, blk), jnp.float32),
                pltpu.VMEM((blk, size), jnp.float32),
            ],
        ),
        out_shape=[
            jax.ShapeDtypeStruct((rows, width), jnp.float32),
            jax.ShapeDtypeStruct((rows, size), jnp.float32),
        ],
        compiler_params=pltpu.CompilerParams(vmem_limit_bytes=VMEM_LIMIT),
        cost_estimate=pl.CostEstimate(flops=blk, bytes_accessed=blk, transcendentals=0),
        name="prepare",
    )(
        table,
        front.reshape(part_rows, blk * part_cols, blk),
        updates.reshape(2, part_rows, blk * child_cols, blk),
        *gathered, arrived, inverse,
    )


def trail_kernel(parts, inverse_ref, top_ref, given_ref, left_ref, out_ref, inv_high, inv_low, high, low):
    step = pl.program_id(0)
    size = inverse_ref.shape[0]
    width = top_ref.shape[1]

    @pl.when(step == 0)
    def _():
        inv_high[...], inv_low[...] = split(inverse_ref[...])

    @pl.when(step < parts)
    def _():
        here = pl.ds(pl.multiple_of(step * width, width), width)
        top_high, top_low = split(top_ref[...])
        for begin in range(0, size, 256):
            end = begin + 256
            result = product3(
                (inv_high[begin:end, :end], inv_low[begin:end, :end]),
                (top_high[:end], top_low[:end]),
            )
            high[begin:end, here], low[begin:end, here] = split(result)

    @pl.when(step >= parts)
    def _():
        left_pair = split(left_ref[...])
        for begin in range(0, given_ref.shape[1], 256):
            cols = slice(begin, begin + 256)
            trailing = product3(left_pair, (high[:, cols], low[:, cols]))
            out_ref[:, cols] = given_ref[:, cols] - trailing


def trail(inverse, top, given, left, blk):
    size, cols = top.shape
    width = 2 * blk
    parts = cols // width

    def late(a):
        return (jnp.maximum(a - parts, 0), 0)

    return pl.pallas_call(
        functools.partial(trail_kernel, parts),
        grid=(parts + given.shape[0] // blk,),
        in_specs=[
            pl.BlockSpec((size, size), lambda a: (0, 0), pipeline_mode=pl.Buffered(1)),
            pl.BlockSpec((size, width), lambda a: (0, jnp.minimum(a, parts - 1))),
            pl.BlockSpec((blk, cols), late),
            pl.BlockSpec((blk, size), late),
        ],
        out_specs=pl.BlockSpec((blk, cols), late),
        out_shape=jax.ShapeDtypeStruct(given.shape, given.dtype),
        scratch_shapes=[pltpu.VMEM((size, size), jnp.bfloat16)] * 2
        + [pltpu.VMEM((size, cols), jnp.bfloat16)] * 2,
        compiler_params=pltpu.CompilerParams(vmem_limit_bytes=VMEM_LIMIT),
        cost_estimate=pl.CostEstimate(flops=blk, bytes_accessed=blk, transcendentals=0),
        name="trail",
    )(inverse, top, given, left)


def add_last_kernel(part_cols, blk, base, turns, table, given_ref, *refs):
    lefts, lowers, out_ref = refs[:NP], refs[NP : 2 * NP], refs[-1]
    received = list(zip(turns, refs[2 * NP : -1]))
    step = pl.program_id(0)

    @pl.when(step == 0)
    def _():
        out_ref[...] = jnp.zeros_like(out_ref)
        for s in range(NP):
            out_ref[0, pl.ds(s, blk, stride=part_cols), :] = lowers[s][...]

    @pl.when(step > 0)
    def _():
        for s in range(NP):
            out_ref[0, pl.ds(s, blk, stride=part_cols), :] = lefts[s][...]
        for slot in range(NP, part_cols):
            total = given_ref[:, (slot - NP) * blk : (slot - NP + 1) * blk]
            out_ref[0, pl.ds(slot, blk, stride=part_cols), :] = child_sum(
                total, table, base, slot, part_cols, None, received, None
            )


def add_last(table, bases, given, left, lower, received, turns, part_rows, part_cols, blk):
    place_base, _, where = bases

    def late(a):
        return jnp.maximum(a - 1, 0)

    def left_spec(s):
        return pl.BlockSpec((blk, blk), lambda a, t: (late(a), s * 4 + t[where + 1]))

    def lower_spec(s):
        return pl.BlockSpec((blk, blk), lambda a, t: (t[where], s * 4 + t[where + 1]))

    return pl.pallas_call(
        functools.partial(add_last_kernel, part_cols, blk, place_base, turns),
        grid_spec=pltpu.PrefetchScalarGridSpec(
            num_scalar_prefetch=1,
            grid=(part_rows,),
            in_specs=[pl.BlockSpec((blk, given.shape[1]), lambda a, t: (late(a), 0))]
            + [left_spec(s) for s in range(NP)]
            + [lower_spec(s) for s in range(NP)]
            + [pl.BlockSpec((r.shape[0], blk, blk), lambda a, t: (0, late(a), 0)) for r in received],
            out_specs=pl.BlockSpec((1, blk * part_cols, blk), lambda a, t: (a, 0, 0)),
        ),
        out_shape=jax.ShapeDtypeStruct((part_rows, blk * part_cols, blk), given.dtype),
        compiler_params=pltpu.CompilerParams(vmem_limit_bytes=VMEM_LIMIT),
        cost_estimate=pl.CostEstimate(flops=blk, bytes_accessed=blk, transcendentals=0),
        name="add_last",
    )(table, given, *[left] * NP, *[lower] * NP, *received)


def table_layout(most, part_cols, panel_blocks):
    place = 3 * most
    square = place + 4 * part_cols
    where = square + 4 * panel_blocks
    return place, square, where, where + 8


def table_kernel(most, part_cols, panel_blocks, maps_ref, table, level_ref, ranks):
    place, square, where, size = table_layout(most, part_cols, panel_blocks)
    child_cols = maps_ref.shape[1] // 4
    row, col = lax.axis_index("row"), lax.axis_index("col")
    for i in range(size):
        table[i] = 0
    for i in range(2 * part_cols):
        table[place + 2 * i] = 4
    for i in range(4):
        ranks[i] = 0
    for g in range(child_cols):
        for member in range(2):
            turn = (maps_ref[member, 4 * g] - 4 * g) & 3
            slot = maps_ref[member, 4 * g + ((col - turn) & 3)] // 4
            entry = place + 2 * (member * part_cols + slot)
            if g < 2:
                unit = 2 * member + g
                table[entry] = jnp.where(turn == 0, 0, SHARED)
                table[entry + 1] = jnp.where(
                    turn == 0, g, ((col - turn) & 3) * (4 + NP) + unit
                )
                for j in range(4):
                    parent = maps_ref[member, 4 * g + j]

                    @pl.when(parent < panel_blocks)
                    def _():
                        table[square + 2 * (member * panel_blocks + parent)] = j * (4 + NP) + unit
                        table[square + 2 * (member * panel_blocks + parent) + 1] = 1

            else:
                rank = ranks[turn]
                ranks[turn] = rank + 1
                table[entry] = turn
                table[entry + 1] = jnp.where(turn == 0, g, rank)

                @pl.when(turn > 0)
                def _():
                    table[(turn - 1) * most + rank] = member * child_cols + g

    table[where] = row
    for i, mask in enumerate((0, 2, 1, 3)):
        table[where + 1 + i] = col ^ mask
    order = sorted(range(len(LEVELS)), key=lambda index: crossing(LEVELS[index]))
    level = jnp.int32(order[-1])
    for index in reversed(order[:-1]):
        one, two, three = LEVELS[index]
        fits = (ranks[1] <= one) & (ranks[2] <= two) & (ranks[3] <= three)
        level = jnp.where(fits, index, level)
    level_ref[0] = level


def make_table(maps, most, part_cols, panel_blocks):
    size = table_layout(most, part_cols, panel_blocks)[-1]
    scalars = pl.BlockSpec(memory_space=pltpu.SMEM)
    return pl.pallas_call(
        functools.partial(table_kernel, most, part_cols, panel_blocks),
        in_specs=[scalars],
        out_specs=[scalars] * 2,
        out_shape=[
            jax.ShapeDtypeStruct((size,), jnp.int32), jax.ShapeDtypeStruct((1,), jnp.int32)
        ],
        scratch_shapes=[pltpu.SMEM((4,), jnp.int32)],
        name="tables",
    )(maps)


def crossing(caps):
    return caps[0] + 2 * caps[1] + caps[2]


def first_turn(caps):
    loads = {1: caps[0], 2: 2 * caps[1], 3: caps[2]}
    light = [turn for turn in loads if loads[turn] <= 6]
    heavy = [turn for turn in loads if loads[turn] >= 6]
    if crossing(caps) <= 22 and light:
        return max(light, key=loads.get)
    return min(heavy, key=loads.get)


def main_branch(level, most, row_count, front, updates, table):
    part_rows, blk, part_cols = front.shape[0], front.shape[2], front.shape[3]
    col_count = 4
    cols = range(col_count)

    def swap(value, mask):
        return lax.ppermute(value, "col", [(c, c ^ mask) for c in cols])

    def turned(value, turn):
        return lax.ppermute(value, "col", [(c, (c + turn) % col_count) for c in cols])

    place, square_base, where, _ = table_layout(most, part_cols, row_count)
    given, columns, early, units, late = send_head(table, front, updates, LEVELS[level], most, level + 1)
    bases = (place, square_base, where)
    soon = first_turn(LEVELS[level])
    turns = [turn for turn in range(1, col_count) if turn != soon]
    square, arrived, top = gather_square(
        table, bases, given, late[soon - 1], soon, front, columns, early, row_count,
        len(LEVELS) + level + 1,
    )
    top, square = lax.optimization_barrier((top, square))
    top = lax.all_gather(top, "row", axis=0, tiled=True)
    units, late, square = lax.optimization_barrier((units, late, square))
    chip, core = swap(units, 2), swap(units, 1)
    lower, inverse = factorize(square, blk)
    chip, core, inverse = lax.optimization_barrier((chip, core, inverse))
    both = swap(chip, 1)
    late = [turned(late[turn - 1], turn) for turn in turns]
    result, left = prepare(
        table, bases, front, updates, (units, chip, core, both), arrived, soon, inverse,
        row_count, col_count,
    )
    result, top = lax.optimization_barrier((result, top))
    result = trail(inverse, top, result, left, blk)
    result, late = lax.optimization_barrier((result, late))
    return add_last(table, bases, result, left, lower, late, turns, part_rows, part_cols, blk)


def body(row_count, col_count, front, updates, maps):
    part_rows = front.shape[0]
    if part_rows < 3 or row_count != NP * col_count or col_count != 4:
        return simple_body(front, updates, maps)
    front = front.reshape(front.shape[0], 1, *front.shape[2:4], front.shape[5])
    blk, part_cols = front.shape[2], front.shape[3]
    most = updates.shape[4]
    table, level = make_table(maps, most, part_cols, row_count)
    branches = [
        functools.partial(main_branch, level, most, row_count) for level in range(len(LEVELS))
    ]
    result = lax.switch(level[0], branches, front, updates, table)
    return result.reshape(part_rows, 1, blk, part_cols, 1, blk)


def solution(mesh):
    return jax.shard_map(
        functools.partial(body, mesh.shape["row"], mesh.shape["col"]),
        mesh=mesh,
        in_specs=(
            P(None, "row", None, None, "col", None),
            P(None, None, "row", None, None, "col", None),
            P(),
        ),
        out_specs=P(None, "row", None, None, "col", None),
        check_vma=False,
    )
```

```python
import functools

import jax
import jax.numpy as jnp
from jax import lax
from jax.experimental import pallas as pl
from jax.experimental.pallas import tpu as pltpu
from jax.sharding import PartitionSpec as P

NP = 2
highest = lax.Precision.HIGHEST
VMEM_LIMIT = 56 * 1024 * 1024
MESH = pl.DeviceIdType.MESH
SHARED = 5
LEVELS = (
    (10, 10, 5), (6, 8, 8), (10, 4, 10), (8, 5, 6),
    (12, 12, 12),
)


def split(value):
    high = value.astype(jnp.bfloat16)
    low = (value - high.astype(jnp.float32)).astype(jnp.bfloat16)
    return high, low


def dims(transposed):
    return (((1,), (1 if transposed else 0,)), ((), ()))


def product3(left_pair, right_pair, transposed=False):
    def one(a, b):
        return lax.dot_general(a, b, dims(transposed), preferred_element_type=jnp.float32)

    return (
        one(left_pair[0], right_pair[0])
        + one(left_pair[0], right_pair[1])
        + one(left_pair[1], right_pair[0])
    )


def product(a, b, transposed=False):
    return lax.dot_general(
        a, b, dims(transposed), precision=highest, preferred_element_type=jnp.float32
    )


def pack_kernel(child_cols, cap, blk, table, updates_ref, one_ref, two_ref, three_ref):
    for turn, out_ref in enumerate((one_ref, two_ref, three_ref)):
        for member in range(2):
            for slot in range(cap):
                source = table[(turn + 1) * 2 * cap + member * cap + slot]
                out_ref[member * cap + slot] = updates_ref[
                    member, 0, pl.ds(source, blk, stride=child_cols), :
                ]


def pack(table, updates, cap, begin, count):
    part_rows, blk, child_cols = updates.shape[1], updates.shape[3], updates.shape[4]
    flat = updates.reshape(2, part_rows, blk * child_cols, blk)
    return pl.pallas_call(
        functools.partial(pack_kernel, child_cols, cap, blk),
        grid_spec=pltpu.PrefetchScalarGridSpec(
            num_scalar_prefetch=1,
            grid=(count,),
            in_specs=[
                pl.BlockSpec((2, 1, blk * child_cols, blk), lambda a, t: (0, a + begin, 0, 0))
            ],
            out_specs=[pl.BlockSpec((2 * cap, blk, blk), lambda a, t: (0, a, 0))] * 3,
        ),
        out_shape=[jax.ShapeDtypeStruct((2 * cap, count * blk, blk), jnp.float32)] * 3,
        compiler_params=pltpu.CompilerParams(vmem_limit_bytes=VMEM_LIMIT),
        name="pack",
    )(table, flat)


def add_children(out_ref, table, front_ref, updates_ref, received, slots, part_cols, child_cols, blk):
    for slot in slots:
        cols = slice(slot * blk, (slot + 1) * blk)
        out_ref[:, cols] = front_ref[0, pl.ds(slot, blk, stride=part_cols), :]
        for member in range(2):
            turn = table[(member * part_cols + slot) * 2]
            index = table[(member * part_cols + slot) * 2 + 1]

            @pl.when(turn == 0)
            def _():
                out_ref[:, cols] += updates_ref[member, 0, pl.ds(index, blk, stride=child_cols), :]

            for step in range(3):

                @pl.when(turn == step + 1)
                def _():
                    out_ref[:, cols] += received[step][index]


def assemble(table, front, updates, received, begin, count, width):
    part_rows, blk, part_cols = front.shape[0], front.shape[2], front.shape[3]
    child_cols = updates.shape[4]
    slots = received[0].shape[0]

    def kernel(table, front_ref, updates_ref, one, two, three, out_ref):
        add_children(
            out_ref, table, front_ref, updates_ref, (one, two, three),
            range(width), part_cols, child_cols, blk,
        )

    return pl.pallas_call(
        kernel,
        grid_spec=pltpu.PrefetchScalarGridSpec(
            num_scalar_prefetch=1,
            grid=(count,),
            in_specs=[
                pl.BlockSpec((1, blk * part_cols, blk), lambda a, t: (a + begin, 0, 0)),
                pl.BlockSpec((2, 1, blk * child_cols, blk), lambda a, t: (0, a + begin, 0, 0)),
            ]
            + [pl.BlockSpec((slots, blk, blk), lambda a, t: (0, a, 0))] * 3,
            out_specs=pl.BlockSpec((blk, width * blk), lambda a, t: (a, 0)),
        ),
        out_shape=jax.ShapeDtypeStruct((count * blk, width * blk), jnp.float32),
        compiler_params=pltpu.CompilerParams(vmem_limit_bytes=VMEM_LIMIT),
        name="assemble",
    )(
        table,
        front.reshape(part_rows, blk * part_cols, blk),
        updates.reshape(2, part_rows, blk * child_cols, blk),
        *received,
    )


def eliminate(block):
    size = block.shape[0]
    group = 8
    tiles = size // group
    shape = (group, size)
    row_ids = lax.broadcasted_iota(jnp.int32, (size, size), 0)
    col_ids = lax.broadcasted_iota(jnp.int32, (size, size), 1)
    local = lax.broadcasted_iota(jnp.int32, shape, 0)
    start = (row_ids == col_ids).astype(jnp.float32)
    upper = [block[group * t : group * (t + 1), :] for t in range(tiles)]
    solved = [start[group * t : group * (t + 1), :] for t in range(tiles)]
    for h in range(tiles):
        def column(t, j):
            return jnp.broadcast_to(upper[t][:, group * h + j : group * h + j + 1], shape)
        home = [column(h, j) for j in range(group)]
        pivot = {
            (i, j): jnp.broadcast_to(home[j][i : i + 1, :], shape)
            for j in range(group) for i in range(j, group)
        }
        scale, ratio = [], {}
        for j in range(group):
            scale.append(1.0 / pivot[j, j])
            for i in range(j + 1, group):
                ratio[i, j] = pivot[i, j] * scale[j]
            for k in range(j + 1, group):
                for i in range(k, group):
                    pivot[i, k] = pivot[i, k] - ratio[i, j] * pivot[k, j]
        upper_rows, solved_rows = [], []
        for j in range(group):
            u = jnp.broadcast_to(upper[h][j : j + 1, :], shape)
            s = jnp.broadcast_to(solved[h][j : j + 1, :], shape)
            for i in range(j):
                u = u - ratio[j, i] * upper_rows[i]
                s = s - ratio[j, i] * solved_rows[i]
            upper_rows.append(u)
            solved_rows.append(s)
        for t in range(h, tiles):
            if t == h:
                u, s = upper_rows[0], solved_rows[0]
                for j in range(1, group):
                    u = jnp.where(local == j, upper_rows[j], u)
                    s = jnp.where(local == j, solved_rows[j], s)
                upper[t], solved[t] = u, s
                continue
            factors = []
            for j in range(group):
                c = column(t, j)
                for i in range(j):
                    c = c - factors[i] * pivot[j, i]
                factors.append(c * scale[j])
            for j in range(group):
                upper[t] = upper[t] - factors[j] * upper_rows[j]
                solved[t] = solved[t] - factors[j] * solved_rows[j]
    upper = jnp.concatenate(upper, axis=0)
    solved = jnp.concatenate(solved, axis=0)
    diagonal = jnp.sum(jnp.where(row_ids == col_ids, upper, 0.0), axis=1, keepdims=True)
    scale = 1.0 / jnp.sqrt(diagonal)
    lower = jnp.where(col_ids >= row_ids, upper * scale, 0.0).T
    return lower, solved * scale

def factor_kernel(blk, square_ref, lower_ref, inverse_ref, work):
    size = square_ref.shape[0]
    count = size // blk
    work[...] = square_ref[...]
    lower_ref[...] = jnp.zeros_like(lower_ref)
    inverse_ref[...] = jnp.zeros_like(inverse_ref)

    def spread(k, diag_inverse):
        begin, end = k * blk, (k + 1) * blk
        here = slice(begin, end)
        inverse_pair = split(diag_inverse)
        if k:
            done = product3(inverse_pair, split(inverse_ref[here, :begin]))
            inverse_ref[here, :begin] = done
        inverse_ref[here, here] = diag_inverse
        if end == size:
            return
        row_high, row_low = split(inverse_ref[here, :end])
        left_high, left_low = [], []
        for q in range(end, size, 256):
            top = min(q + 256, size)
            left = product3(split(work[q:top, here]), inverse_pair, True)
            lower_ref[q:top, here] = left
            high, low = split(left)
            left_high.append(high)
            left_low.append(low)
        high = jnp.concatenate(left_high, axis=0)
        low = jnp.concatenate(left_low, axis=0)
        for q in range(end, size, 256):
            top = min(q + 256, size)
            pair = high[q - end : top - end], low[q - end : top - end]
            below = high[: top - end], low[: top - end]
            work[q:top, end:top] -= product3(pair, below, True)
            inverse_ref[q:top, :end] -= product3(pair, (row_high, row_low))

    def step(k, carry):
        begin = pl.multiple_of(k * blk, blk)
        here = pl.ds(begin, blk)
        diag_lower, diag_inverse = eliminate(work[here, here])
        lower_ref[here, here] = diag_lower
        for t in range(count):
            pl.when(k == t)(functools.partial(spread, t, diag_inverse))
        return carry

    lax.fori_loop(0, count, step, 0)


def factorize(square, blk):
    size = square.shape[0]
    shape = jax.ShapeDtypeStruct((size, size), jnp.float32)
    return pl.pallas_call(
        functools.partial(factor_kernel, blk),
        out_shape=[shape, shape],
        scratch_shapes=[pltpu.VMEM((size, size), jnp.float32)],
        compiler_params=pltpu.CompilerParams(vmem_limit_bytes=VMEM_LIMIT),
        cost_estimate=pl.CostEstimate(flops=size, bytes_accessed=size, transcendentals=0),
        name="factorize",
    )(square)


def right_kernel(inverse_ref, top_ref, high_ref, low_ref, inv_high, inv_low):
    @pl.when(pl.program_id(0) == 0)
    def _():
        inv_high[...], inv_low[...] = split(inverse_ref[...])

    result = product3((inv_high[...], inv_low[...]), split(top_ref[...]))
    high_ref[...], low_ref[...] = split(result)


def right_side(inverse, top, tile):
    size, cols = top.shape
    out = jax.ShapeDtypeStruct((size, cols), jnp.bfloat16)
    return pl.pallas_call(
        right_kernel,
        grid=(cols // tile,),
        in_specs=[
            pl.BlockSpec((size, size), lambda n: (0, 0)),
            pl.BlockSpec((size, tile), lambda n: (0, n)),
        ],
        out_specs=[pl.BlockSpec((size, tile), lambda n: (0, n))] * 2,
        out_shape=[out, out],
        scratch_shapes=[pltpu.VMEM((size, size), jnp.bfloat16)] * 2,
        compiler_params=pltpu.CompilerParams(vmem_limit_bytes=VMEM_LIMIT),
        cost_estimate=pl.CostEstimate(flops=size, bytes_accessed=size, transcendentals=0),
        name="right",
    )(inverse, top)


def finish_kernel(
    part_cols, child_cols, blk, row_count, col_count, first, table, place,
    panel_ref, front_ref, updates_ref, one, two, three, inverse_ref, lower_ref, high_ref, low_ref,
    out_ref, inv_high, inv_low, left_ref, sum_ref,
):
    step = pl.program_id(0)
    block_row = step * row_count + place[0]
    panel_blocks = NP * col_count
    inside = block_row < panel_blocks
    columns = [pl.multiple_of((s * col_count + place[1]) * blk, blk) for s in range(NP)]

    @pl.when(step == 0)
    def _():
        inv_high[...], inv_low[...] = split(inverse_ref[...])

    @pl.when(jnp.logical_not(inside))
    def _():
        add_children(
            sum_ref, table, front_ref, updates_ref, (one, two, three),
            range(NP, part_cols), part_cols, child_cols, blk,
        )
        panel = jnp.concatenate(
            [
                panel_ref[c, :, s * blk : (s + 1) * blk]
                for s in range(NP)
                for c in range(col_count)
            ],
            axis=1,
        )
        left_ref[...] = product3(split(panel), (inv_high[...], inv_low[...]), True)
        left_pair = split(left_ref[...])
        for pair in range(NP, part_cols, 2):
            cols = slice((pair - NP) * blk, (pair - NP + 2) * blk)
            trailing = product3(left_pair, (high_ref[:, cols], low_ref[:, cols]))
            updated = sum_ref[:, pair * blk : (pair + 2) * blk] - trailing
            for half in range(2):
                out_ref[0, pl.ds(pair + half, blk, stride=part_cols), :] = updated[
                    :, half * blk : (half + 1) * blk
                ]
        for s in range(NP):
            out_ref[0, pl.ds(s, blk, stride=part_cols), :] = left_ref[:, pl.ds(columns[s], blk)]

    @pl.when(inside)
    def _():
        out_ref[...] = jnp.zeros_like(out_ref)
        begin = pl.multiple_of(block_row * blk, blk)
        for s in range(NP):
            out_ref[0, pl.ds(s, blk, stride=part_cols), :] = lower_ref[
                pl.ds(begin, blk), pl.ds(columns[s], blk)
            ]


def finish(table, place, panel, front, updates, received, inverse, lower, high, low, row_count, first):
    part_rows, blk, part_cols = front.shape[0], front.shape[2], front.shape[3]
    child_cols = updates.shape[4]
    size = inverse.shape[0]
    slots = received[0].shape[0]
    col_count = panel.shape[0]

    def resident(shape):
        return pl.BlockSpec(shape, lambda a, t, p: (0, 0), pipeline_mode=pl.Buffered(1))

    def late(a, t, p):
        return (0, jnp.maximum(a - first, 0), 0)

    return pl.pallas_call(
        functools.partial(finish_kernel, part_cols, child_cols, blk, row_count, col_count, first),
        grid_spec=pltpu.PrefetchScalarGridSpec(
            num_scalar_prefetch=2,
            grid=(part_rows,),
            in_specs=[
                pl.BlockSpec((col_count, blk, NP * blk), late),
                pl.BlockSpec((1, blk * part_cols, blk), lambda a, t, p: (a, 0, 0)),
                pl.BlockSpec((2, 1, blk * child_cols, blk), lambda a, t, p: (0, a, 0, 0)),
            ]
            + [pl.BlockSpec((slots, blk, blk), late)] * 3
            + [
                resident((size, size)),
                resident((size, size)),
                resident(high.shape),
                resident(low.shape),
            ],
            out_specs=pl.BlockSpec((1, blk * part_cols, blk), lambda a, t, p: (a, 0, 0)),
            scratch_shapes=[
                pltpu.VMEM((size, size), jnp.bfloat16),
                pltpu.VMEM((size, size), jnp.bfloat16),
                pltpu.VMEM((blk, size), jnp.float32),
                pltpu.VMEM((blk, part_cols * blk), jnp.float32),
            ],
        ),
        out_shape=jax.ShapeDtypeStruct((part_rows, blk * part_cols, blk), jnp.float32),
        compiler_params=pltpu.CompilerParams(vmem_limit_bytes=VMEM_LIMIT),
        name="finish",
    )(
        table, place, panel,
        front.reshape(part_rows, blk * part_cols, blk),
        updates.reshape(2, part_rows, blk * child_cols, blk),
        *received, inverse, lower, high, low,
    )


def tables(maps, col_index, col_count, child_cols, part_cols, cap):
    offsets = maps[:, ::col_count] - col_count * jnp.arange(child_cols, dtype=jnp.int32)[None, :]
    turn = offsets % col_count
    groups = jnp.arange(child_cols, dtype=jnp.int32)
    same = (turn[:, :, None] == turn[:, None, :]) & (groups[None, None, :] < groups[None, :, None])
    rank = jnp.sum(same.astype(jnp.int32), axis=2)
    turns = jnp.arange(col_count, dtype=jnp.int32)
    slots = jnp.arange(cap, dtype=jnp.int32)
    hot = (turn[None, :, None, :] == turns[:, None, None, None]) & (
        rank[None, :, None, :] == slots[None, None, :, None]
    )
    send = jnp.sum(jnp.where(hot, groups[None, None, None, :], 0), axis=3).reshape(-1)
    parents = jnp.arange(part_cols, dtype=jnp.int32) * col_count + col_index
    match = maps[:, None, :] == parents[None, :, None]
    spread = jnp.repeat(groups, col_count)
    group = jnp.sum(jnp.where(match, spread[None, None, :], 0), axis=2)
    present = jnp.any(match, axis=2)
    pick = group[:, :, None] == groups[None, None, :]
    kind = jnp.sum(jnp.where(pick, turn[:, None, :], 0), axis=2)
    order = jnp.sum(jnp.where(pick, rank[:, None, :], 0), axis=2)
    order = jnp.where(kind == 0, group, order + cap * jnp.arange(2, dtype=jnp.int32)[:, None])
    kind = jnp.where(present, kind, col_count)
    place = jnp.stack([kind, order], axis=2).reshape(-1)
    return send, place


def gather_top(piece, row_count, row_index, panel_blocks):
    if row_count == panel_blocks:
        return lax.all_gather(piece, "row", axis=0, tiled=True)
    ids = jnp.arange(panel_blocks, dtype=jnp.int32)
    kept = jnp.where((ids == row_index)[:, None, None], piece[None], 0.0)
    return lax.psum(kept, "row").reshape(panel_blocks * piece.shape[0], piece.shape[1])


def simple_body(front, updates, maps):
    row_count = lax.axis_size("row")
    col_count = lax.axis_size("col")
    row_index = lax.axis_index("row")
    col_index = lax.axis_index("col")
    front = front.reshape(front.shape[0], 1, *front.shape[2:4], front.shape[5])
    blk, part_cols = front.shape[2], front.shape[3]
    child_cols = updates.shape[4]
    cap = child_cols // 2
    panel_blocks = NP * col_count
    send, place = tables(maps, col_index, col_count, child_cols, part_cols, cap)
    part_rows = front.shape[0]
    first = 1 if part_rows > 1 and row_count == panel_blocks else part_rows

    def exchange(outgoing):
        return [
            lax.ppermute(
                outgoing[turn - 1], "col", [(c, (c + turn) % col_count) for c in range(col_count)]
            )
            for turn in range(1, col_count)
        ]

    early = exchange(pack(send, updates, cap, 0, first))
    if first < part_rows:
        outgoing = pack(send, updates, cap, first, part_rows - first)
        early, outgoing = lax.optimization_barrier((early, outgoing))
        received = exchange(outgoing)
    else:
        received = early
    head = assemble(place, front, updates, early, 0, 1, part_cols)
    square = jnp.concatenate(
        [
            lax.all_gather(head[:, s * blk : (s + 1) * blk], "col", axis=1, tiled=True)
            for s in range(NP)
        ],
        axis=1,
    )
    square = gather_top(square, row_count, row_index, panel_blocks)
    rest, square = lax.optimization_barrier((head[:, NP * blk :], square))
    top = gather_top(rest, row_count, row_index, panel_blocks)
    lower, inverse = factorize(square, blk)
    high, low = right_side(inverse, top, 2 * blk)
    received, high, low = lax.optimization_barrier((received, high, low))
    late = first if first < part_rows else 0
    panel = assemble(place, front, updates, received, late, part_rows - late, NP)
    panel = lax.all_gather(panel, "col", axis=0)
    where = jnp.stack([row_index, col_index]).astype(jnp.int32)
    result = finish(
        place, where, panel, front, updates, received, inverse, lower, high, low, row_count, late
    )
    return result.reshape(front.shape[0], 1, blk, part_cols, 1, blk)


def send_kernel(
    blk, caps, most, table, front_ref, updates_ref, units_ref, columns_ref,
    got_one, got_two, got_three, panel_ref, late_one, late_two, late_three,
    front_part, updates_part, columns, units, first, stage, stage_one, stage_two, stage_three,
    local, keep_sem, send, recv, out_sem,
):
    row, col = lax.axis_index("row"), lax.axis_index("col")
    part_rows = front_ref.shape[0]
    part_cols = front_part.shape[1] // blk
    child_cols = updates_part.shape[2] // blk
    width = units.shape[0]
    stages = (stage_one, stage_two, stage_three)

    def loads(a, side):
        copies = [pltpu.make_async_copy(front_ref.at[a], front_part.at[side], local.at[side, 0])]
        for member in range(2):
            copies.append(
                pltpu.make_async_copy(
                    updates_ref.at[member, a], updates_part.at[side, member],
                    local.at[side, 1 + member],
                )
            )
        return copies

    for load in loads(0, 0):
        load.start()
    for load in loads(1, 1):
        load.start()
    others = [lax.rem(col + turn, 4) for turn in range(1, 4)]
    barrier = pltpu.get_barrier_semaphore()
    for other in others:
        pl.semaphore_signal(barrier, inc=1, device_id=(row, other), device_id_type=MESH)

    def spread(side, target):
        def unpack(g, carry):
            for member in range(2):
                columns[member * child_cols + g] = updates_part[
                    side, member, pl.ds(g, blk, stride=child_cols), :
                ]
            return carry

        lax.fori_loop(0, child_cols, unpack, 0)
        for member in range(2):
            for g in range(2):
                target[member * 2 + g] = columns[member * child_cols + g]
        for s in range(NP):
            target[4 + s] = front_part[side, pl.ds(s, blk, stride=part_cols), :]

    def fill(target, turn):
        def put(slot, carry):
            target[slot] = columns[table[turn * most + slot]]
            return carry

        lax.fori_loop(0, caps[turn], put, 0)

    for load in loads(0, 0):
        load.wait()
    spread(0, units)
    pl.semaphore_wait(barrier, 3)

    def remote(source, target, index, device):
        return pltpu.make_async_remote_copy(
            src_ref=source, dst_ref=target, send_sem=send.at[index], recv_sem=recv.at[index],
            device_id=(row, device), device_id_type=MESH,
        )

    across = remote(units, units_ref.at[pl.ds(col * width, width)], 3, others[1])
    across.start()
    keep = [
        pltpu.make_async_copy(units, units_ref.at[pl.ds(col * width, width)], keep_sem.at[0]),
        pltpu.make_async_copy(columns, columns_ref, keep_sem.at[1]),
    ]
    for move in keep:
        move.start()
    other_core = col + 1 - 2 * lax.rem(col, 2)

    def beside(owner, index):
        section = units_ref.at[pl.ds(owner * width, width)]
        source = units if index == 4 else section
        return remote(source, section, index, other_core)

    mine = beside(col, 4)
    mine.start()
    moves = []
    begin = 0
    for turn, target in enumerate((got_one, got_two, got_three)):
        fill(first.at[pl.ds(begin, caps[turn])], turn)
        moves.append(remote(first.at[pl.ds(begin, caps[turn])], target, turn, others[turn]))
        moves[-1].start()
        begin += caps[turn]

    def stores(a, side):
        rows = pl.ds(pl.multiple_of((a - 1) * blk, blk), blk)
        copies = [pltpu.make_async_copy(stage.at[side], panel_ref.at[:, rows, :], out_sem.at[side, 0])]
        for turn, target in enumerate((late_one, late_two, late_three)):
            copies.append(
                pltpu.make_async_copy(
                    stages[turn].at[side], target.at[:, rows, :], out_sem.at[side, 1 + turn]
                )
            )
        return copies

    def step(a, carry):
        side = lax.rem(a, 2)
        for load in loads(a, side):
            load.wait()

        @pl.when(a + 1 < part_rows)
        def _():
            for load in loads(a + 1, 1 - side):
                load.start()

        @pl.when(a > 2)
        def _():
            for store in stores(a - 2, side):
                store.wait()

        spread(side, stage.at[side])
        for turn in range(3):
            fill(stages[turn].at[side], turn)
        for store in stores(a, side):
            store.start()
        return carry

    keep[1].wait()
    lax.fori_loop(1, part_rows, step, 0)
    for a in range(max(1, part_rows - 2), part_rows):
        for store in stores(a, a % 2):
            store.wait()
    keep[0].wait()
    across.wait_send()
    remote(units, units_ref.at[pl.ds(others[1] * width, width)], 3, others[1]).wait_recv()
    passed = beside(others[1], 5)
    passed.start()
    for index, owner in enumerate((other_core, lax.rem(other_core + 2, 4))):
        beside(owner, 4 + index).wait_recv()
    for move in (mine, passed):
        move.wait_send()
    for move in moves:
        move.wait()


def send_head(table, front, updates, caps, most, identity):
    part_rows, blk, part_cols = front.shape[0], front.shape[2], front.shape[3]
    child_cols = updates.shape[4]
    anywhere = pl.BlockSpec(memory_space=pl.ANY)
    width = 4 + NP
    rest = (part_rows - 1) * blk
    shapes = [(4 * width, blk, blk), (2 * child_cols, blk, blk)] + [(cap, blk, blk) for cap in caps]
    shapes += [(width, rest, blk)] + [(cap, rest, blk) for cap in caps]
    outs = pl.pallas_call(
        functools.partial(send_kernel, blk, caps, most),
        in_specs=[pl.BlockSpec(memory_space=pltpu.SMEM), anywhere, anywhere],
        out_specs=[anywhere] * 9,
        out_shape=[jax.ShapeDtypeStruct(shape, jnp.float32) for shape in shapes],
        scratch_shapes=[
            pltpu.VMEM((2, blk * part_cols, blk), jnp.float32),
            pltpu.VMEM((2, 2, blk * child_cols, blk), jnp.float32),
            pltpu.VMEM((2 * child_cols, blk, blk), jnp.float32),
            pltpu.VMEM((width, blk, blk), jnp.float32),
            pltpu.VMEM((sum(caps), blk, blk), jnp.float32),
            pltpu.VMEM((2, width, blk, blk), jnp.float32),
        ]
        + [pltpu.VMEM((2, cap, blk, blk), jnp.float32) for cap in caps]
        + [
            pltpu.SemaphoreType.DMA((2, 3)),
            pltpu.SemaphoreType.DMA((2,)),
            pltpu.SemaphoreType.DMA((6,)),
            pltpu.SemaphoreType.DMA((6,)),
            pltpu.SemaphoreType.DMA((2, 4)),
        ],
        compiler_params=pltpu.CompilerParams(
            vmem_limit_bytes=VMEM_LIMIT, collective_id=identity, has_side_effects=True
        ),
        cost_estimate=pl.CostEstimate(flops=blk, bytes_accessed=blk, transcendentals=0),
        name="send",
    )(
        table,
        front.reshape(part_rows, blk * part_cols, blk),
        updates.reshape(2, part_rows, blk * child_cols, blk),
    )
    return outs[0], outs[1], outs[2:5], outs[5], outs[6:]


def square_kernel(
    blk, row_count, turn, bases, table, given_ref, sent_ref, front_ref, columns_ref,
    early_one, early_two, early_three, square_ref, got_ref, top_ref,
    work, units, front_part, columns, one, two, three, top, local, line_send, line_recv, core_send, core_recv, turn_send, turn_recv,
):
    row, col = lax.axis_index("row"), lax.axis_index("col")
    width = units.shape[0] // 4
    half = row_count // 2
    core = lax.rem(col, 2)
    other_core = col + 1 - 2 * core
    other_chip = lax.rem(col + 2, 4)
    diagonal = lax.rem(other_core + 2, 4)

    part_cols = front_part.shape[0] // blk
    early = ((1, one), (2, two), (3, three))
    loads = [
        pltpu.make_async_copy(source, target, local.at[index])
        for index, (source, target) in enumerate(
            (
                (given_ref, units), (front_ref.at[0], front_part), (columns_ref, columns),
                (early_one, one), (early_two, two), (early_three, three),
            )
        )
    ]
    for load in loads:
        load.start()

    def ring_row(position):
        position = lax.rem(position + row_count, row_count)
        return jnp.where(position < half, 2 * position, 2 * (row_count - position) - 1)

    place = jnp.where(lax.rem(row, 2) == 0, row // 2, row_count - 1 - row // 2)
    right, left = ring_row(place + 1), ring_row(place - 1)
    barrier = pltpu.get_barrier_semaphore()
    for device in (
        (row, other_core), (row, other_chip), (row, diagonal), (right, col), (left, col)
    ):
        pl.semaphore_signal(barrier, inc=1, device_id=device, device_id_type=MESH)
    for load in loads:
        load.wait()
    pl.semaphore_wait(barrier, 5)
    turned = pltpu.make_async_remote_copy(
        src_ref=sent_ref, dst_ref=got_ref, send_sem=turn_send, recv_sem=turn_recv,
        device_id=(row, lax.rem(col + turn, 4)), device_id_type=MESH,
    )
    turned.start()

    here = pl.multiple_of(row * blk, blk)
    for q in range(row_count):
        s, owner = q // 4, q % 4
        total = units[owner * width + 4 + s]
        for member in range(2):
            entry = bases[1] + 2 * (member * row_count + q)
            total = total + units[table[entry]] * table[entry + 1].astype(jnp.float32)
        work[pl.ds(here, blk), q * blk : (q + 1) * blk] = total

    cols = work.shape[1] // 2

    def part(position, side):
        begin = pl.multiple_of(ring_row(position) * blk, blk)
        return work.at[pl.ds(begin, blk), pl.ds(pl.multiple_of(side * cols, cols), cols)]

    def copy(ref, device, send, recv):
        return pltpu.make_async_remote_copy(
            src_ref=ref, dst_ref=ref, send_sem=send, recv_sem=recv,
            device_id=device, device_id_type=MESH,
        )

    pending = []
    for step in range(half):
        ways = range(2 if step < half - 1 else 1)
        for way in ways:
            position = place - step if way == 0 else place + step
            target = right if way == 0 else left
            move = copy(
                part(position, core), (target, col), line_send.at[way, step], line_recv.at[way, step]
            )
            move.start()
            pending.append(move)
        for slot in range(NP + step, part_cols, half):
            top[:, (slot - NP) * blk : (slot - NP + 1) * blk] = child_sum(
                front_part[pl.ds(slot, blk, stride=part_cols), :],
                table, bases[0], slot, part_cols, columns, early, units,
            )
        for way in ways:
            origin = place - step - 1 if way == 0 else place + step + 1
            landed = part(origin, core)
            copy(
                landed, (right, col), line_send.at[way, step], line_recv.at[way, step]
            ).wait_recv()
            forward = copy(
                landed, (row, other_core), core_send.at[way, step], core_recv.at[way, step]
            )
            forward.start()
            pending.append(forward)
    for way in range(2):
        for step in range(half - way):
            origin = place - step - 1 if way == 0 else place + step + 1
            copy(
                part(origin, 1 - core), (row, other_core),
                core_send.at[way, step], core_recv.at[way, step],
            ).wait_recv()
    stores = [
        pltpu.make_async_copy(work, square_ref, local.at[0]),
        pltpu.make_async_copy(top, top_ref, local.at[1]),
    ]
    for store in stores:
        store.start()
    for move in pending:
        move.wait_send()
    for store in stores:
        store.wait()
    turned.wait()


def gather_square(table, bases, given, sent, turn, front, columns, early, row_count, identity):
    part_rows, blk, part_cols = front.shape[0], front.shape[2], front.shape[3]
    size = row_count * blk
    half = row_count // 2
    anywhere = pl.BlockSpec(memory_space=pl.ANY)
    top = jax.ShapeDtypeStruct((blk, (part_cols - NP) * blk), jnp.float32)
    return pl.pallas_call(
        functools.partial(square_kernel, blk, row_count, turn, bases),
        in_specs=[pl.BlockSpec(memory_space=pltpu.SMEM)] + [anywhere] * 7,
        out_specs=[anywhere] * 3,
        out_shape=[
            jax.ShapeDtypeStruct((size, size), jnp.float32),
            jax.ShapeDtypeStruct(sent.shape, jnp.float32),
            top,
        ],
        scratch_shapes=[
            pltpu.VMEM((size, size), jnp.float32),
            pltpu.VMEM(given.shape, jnp.float32),
            pltpu.VMEM((blk * part_cols, blk), jnp.float32),
            pltpu.VMEM(columns.shape, jnp.float32),
        ]
        + [pltpu.VMEM(e.shape, jnp.float32) for e in early]
        + [
            pltpu.VMEM(top.shape, jnp.float32),
            pltpu.SemaphoreType.DMA((6,)),
            pltpu.SemaphoreType.DMA((2, half)),
            pltpu.SemaphoreType.DMA((2, half)),
            pltpu.SemaphoreType.DMA((2, half)),
            pltpu.SemaphoreType.DMA((2, half)),
            pltpu.SemaphoreType.DMA,
            pltpu.SemaphoreType.DMA,
        ],
        compiler_params=pltpu.CompilerParams(
            vmem_limit_bytes=VMEM_LIMIT, collective_id=identity, has_side_effects=True
        ),
        cost_estimate=pl.CostEstimate(flops=size, bytes_accessed=size, transcendentals=0),
        name="square",
    )(table, given, sent, front.reshape(part_rows, blk * part_cols, blk), columns, *early)


def pick(kind, index, wanted):
    hit = kind == wanted
    return jnp.where(hit, index, 0), hit.astype(jnp.float32)


def child_sum(total, table, base, slot, part_cols, columns, received, shared):
    for member in range(2):
        entry = base + (member * part_cols + slot) * 2
        kind, index = table[entry], table[entry + 1]
        if columns is not None:
            at, weight = pick(kind, index, 0)
            total = total + weight * columns[member * (columns.shape[0] // 2) + at]
        if shared is not None:
            at, weight = pick(kind, index, SHARED)
            total = total + weight * shared[at]
        for turn, ref in received:
            at, weight = pick(kind, index, turn)
            total = total + weight * ref[at]
    return total


def prepare_kernel(
    part_cols, child_cols, blk, row_count, col_count, bases, soon, table,
    front_ref, updates_ref, own, chip, core, both, arrived, inverse_ref,
    sum_ref, left_ref, inv_high, inv_low, units, panel_ref,
):
    place_base, square_base, where = bases
    size = inverse_ref.shape[0]

    @pl.when(pl.program_id(0) == 0)
    def _():
        inv_high[...], inv_low[...] = split(inverse_ref[...])

    width = own.shape[0]
    for order, ref in enumerate((own, chip, core, both)):
        owner = table[where + 1 + order]
        for i in range(width):
            units[owner * width + i] = ref[i]
    for q in range(row_count):
        total = units[(q % col_count) * width + 4 + q // col_count]
        for member in range(2):
            entry = square_base + 2 * (member * row_count + q)
            total = total + units[table[entry]] * table[entry + 1].astype(jnp.float32)
        panel_ref[:, q * blk : (q + 1) * blk] = total
    for slot in range(NP, part_cols):
        cols = slice((slot - NP) * blk, (slot - NP + 1) * blk)
        sum_ref[:, cols] = child_sum(
            front_ref[0, pl.ds(slot, blk, stride=part_cols), :],
            table, place_base, slot, part_cols, None, ((soon, arrived),), units,
        )
    for slot in range(NP, part_cols):
        cols = slice((slot - NP) * blk, (slot - NP + 1) * blk)
        for member in range(2):
            entry = place_base + (member * part_cols + slot) * 2

            @pl.when(table[entry] == 0)
            def _():
                sum_ref[:, cols] += updates_ref[
                    member, 0, pl.ds(table[entry + 1], blk, stride=child_cols), :
                ]

    panel_pair = split(panel_ref[...])
    for begin in range(0, size, 2 * blk):
        end = begin + 2 * blk
        left_ref[:, begin:end] = product3(
            tuple(p[:, :end] for p in panel_pair),
            (inv_high[begin:end, :end], inv_low[begin:end, :end]),
            True,
        )


def prepare(table, bases, front, updates, gathered, arrived, soon, inverse, row_count, col_count):
    part_rows, blk, part_cols = front.shape[0], front.shape[2], front.shape[3]
    child_cols = updates.shape[4]
    size = inverse.shape[0]
    rows, width = (part_rows - 1) * blk, (part_cols - NP) * blk
    return pl.pallas_call(
        functools.partial(
            prepare_kernel, part_cols, child_cols, blk, row_count, col_count, bases, soon
        ),
        grid_spec=pltpu.PrefetchScalarGridSpec(
            num_scalar_prefetch=1,
            grid=(part_rows - 1,),
            in_specs=[
                pl.BlockSpec((1, blk * part_cols, blk), lambda a, t: (a + 1, 0, 0)),
                pl.BlockSpec((2, 1, blk * child_cols, blk), lambda a, t: (0, a + 1, 0, 0)),
            ]
            + [pl.BlockSpec((g.shape[0], blk, blk), lambda a, t: (0, a, 0)) for g in (*gathered, arrived)]
            + [pl.BlockSpec((size, size), lambda a, t: (0, 0), pipeline_mode=pl.Buffered(1))],
            out_specs=[
                pl.BlockSpec((blk, width), lambda a, t: (a, 0)),
                pl.BlockSpec((blk, size), lambda a, t: (a, 0)),
            ],
            scratch_shapes=[
                pltpu.VMEM((size, size), jnp.bfloat16),
                pltpu.VMEM((size, size), jnp.bfloat16),
                pltpu.VMEM((4 * (4 + NP), blk, blk), jnp.float32),
                pltpu.VMEM((blk, size), jnp.float32),
            ],
        ),
        out_shape=[
            jax.ShapeDtypeStruct((rows, width), jnp.float32),
            jax.ShapeDtypeStruct((rows, size), jnp.float32),
        ],
        compiler_params=pltpu.CompilerParams(vmem_limit_bytes=VMEM_LIMIT),
        cost_estimate=pl.CostEstimate(flops=blk, bytes_accessed=blk, transcendentals=0),
        name="prepare",
    )(
        table,
        front.reshape(part_rows, blk * part_cols, blk),
        updates.reshape(2, part_rows, blk * child_cols, blk),
        *gathered, arrived, inverse,
    )


def trail_kernel(parts, inverse_ref, top_ref, given_ref, left_ref, out_ref, inv_high, inv_low, high, low):
    step = pl.program_id(0)
    size = inverse_ref.shape[0]
    width = top_ref.shape[1]

    @pl.when(step == 0)
    def _():
        inv_high[...], inv_low[...] = split(inverse_ref[...])

    @pl.when(step < parts)
    def _():
        here = pl.ds(pl.multiple_of(step * width, width), width)
        top_high, top_low = split(top_ref[...])
        for begin in range(0, size, 256):
            end = begin + 256
            result = product3(
                (inv_high[begin:end, :end], inv_low[begin:end, :end]),
                (top_high[:end], top_low[:end]),
            )
            high[begin:end, here], low[begin:end, here] = split(result)

    @pl.when(step >= parts)
    def _():
        left_pair = split(left_ref[...])
        for begin in range(0, given_ref.shape[1], 256):
            cols = slice(begin, begin + 256)
            trailing = product3(left_pair, (high[:, cols], low[:, cols]))
            out_ref[:, cols] = given_ref[:, cols] - trailing


def trail(inverse, top, given, left, blk):
    size, cols = top.shape
    width = 2 * blk
    parts = cols // width

    def late(a):
        return (jnp.maximum(a - parts, 0), 0)

    return pl.pallas_call(
        functools.partial(trail_kernel, parts),
        grid=(parts + given.shape[0] // blk,),
        in_specs=[
            pl.BlockSpec((size, size), lambda a: (0, 0), pipeline_mode=pl.Buffered(1)),
            pl.BlockSpec((size, width), lambda a: (0, jnp.minimum(a, parts - 1))),
            pl.BlockSpec((blk, cols), late),
            pl.BlockSpec((blk, size), late),
        ],
        out_specs=pl.BlockSpec((blk, cols), late),
        out_shape=jax.ShapeDtypeStruct(given.shape, given.dtype),
        scratch_shapes=[pltpu.VMEM((size, size), jnp.bfloat16)] * 2
        + [pltpu.VMEM((size, cols), jnp.bfloat16)] * 2,
        compiler_params=pltpu.CompilerParams(vmem_limit_bytes=VMEM_LIMIT),
        cost_estimate=pl.CostEstimate(flops=blk, bytes_accessed=blk, transcendentals=0),
        name="trail",
    )(inverse, top, given, left)


def add_last_kernel(part_cols, blk, base, turns, table, given_ref, *refs):
    lefts, lowers, out_ref = refs[:NP], refs[NP : 2 * NP], refs[-1]
    received = list(zip(turns, refs[2 * NP : -1]))
    step = pl.program_id(0)

    @pl.when(step == 0)
    def _():
        out_ref[...] = jnp.zeros_like(out_ref)
        for s in range(NP):
            out_ref[0, pl.ds(s, blk, stride=part_cols), :] = lowers[s][...]

    @pl.when(step > 0)
    def _():
        for s in range(NP):
            out_ref[0, pl.ds(s, blk, stride=part_cols), :] = lefts[s][...]
        for slot in range(NP, part_cols):
            total = given_ref[:, (slot - NP) * blk : (slot - NP + 1) * blk]
            out_ref[0, pl.ds(slot, blk, stride=part_cols), :] = child_sum(
                total, table, base, slot, part_cols, None, received, None
            )


def add_last(table, bases, given, left, lower, received, turns, part_rows, part_cols, blk):
    place_base, _, where = bases

    def late(a):
        return jnp.maximum(a - 1, 0)

    def left_spec(s):
        return pl.BlockSpec((blk, blk), lambda a, t: (late(a), s * 4 + t[where + 1]))

    def lower_spec(s):
        return pl.BlockSpec((blk, blk), lambda a, t: (t[where], s * 4 + t[where + 1]))

    return pl.pallas_call(
        functools.partial(add_last_kernel, part_cols, blk, place_base, turns),
        grid_spec=pltpu.PrefetchScalarGridSpec(
            num_scalar_prefetch=1,
            grid=(part_rows,),
            in_specs=[pl.BlockSpec((blk, given.shape[1]), lambda a, t: (late(a), 0))]
            + [left_spec(s) for s in range(NP)]
            + [lower_spec(s) for s in range(NP)]
            + [pl.BlockSpec((r.shape[0], blk, blk), lambda a, t: (0, late(a), 0)) for r in received],
            out_specs=pl.BlockSpec((1, blk * part_cols, blk), lambda a, t: (a, 0, 0)),
        ),
        out_shape=jax.ShapeDtypeStruct((part_rows, blk * part_cols, blk), given.dtype),
        compiler_params=pltpu.CompilerParams(vmem_limit_bytes=VMEM_LIMIT),
        cost_estimate=pl.CostEstimate(flops=blk, bytes_accessed=blk, transcendentals=0),
        name="add_last",
    )(table, given, *[left] * NP, *[lower] * NP, *received)


def table_layout(most, part_cols, panel_blocks):
    place = 3 * most
    square = place + 4 * part_cols
    where = square + 4 * panel_blocks
    return place, square, where, where + 8


def table_kernel(most, part_cols, panel_blocks, maps_ref, table, level_ref, ranks):
    place, square, where, size = table_layout(most, part_cols, panel_blocks)
    child_cols = maps_ref.shape[1] // 4
    row, col = lax.axis_index("row"), lax.axis_index("col")
    for i in range(size):
        table[i] = 0
    for i in range(2 * part_cols):
        table[place + 2 * i] = 4
    for i in range(4):
        ranks[i] = 0
    for g in range(child_cols):
        for member in range(2):
            turn = (maps_ref[member, 4 * g] - 4 * g) & 3
            slot = maps_ref[member, 4 * g + ((col - turn) & 3)] // 4
            entry = place + 2 * (member * part_cols + slot)
            if g < 2:
                unit = 2 * member + g
                table[entry] = jnp.where(turn == 0, 0, SHARED)
                table[entry + 1] = jnp.where(
                    turn == 0, g, ((col - turn) & 3) * (4 + NP) + unit
                )
                for j in range(4):
                    parent = maps_ref[member, 4 * g + j]

                    @pl.when(parent < panel_blocks)
                    def _():
                        table[square + 2 * (member * panel_blocks + parent)] = j * (4 + NP) + unit
                        table[square + 2 * (member * panel_blocks + parent) + 1] = 1

            else:
                rank = ranks[turn]
                ranks[turn] = rank + 1
                table[entry] = turn
                table[entry + 1] = jnp.where(turn == 0, g, rank)

                @pl.when(turn > 0)
                def _():
                    table[(turn - 1) * most + rank] = member * child_cols + g

    table[where] = row
    for i, mask in enumerate((0, 2, 1, 3)):
        table[where + 1 + i] = col ^ mask
    order = sorted(range(len(LEVELS)), key=lambda index: crossing(LEVELS[index]))
    level = jnp.int32(order[-1])
    for index in reversed(order[:-1]):
        one, two, three = LEVELS[index]
        fits = (ranks[1] <= one) & (ranks[2] <= two) & (ranks[3] <= three)
        level = jnp.where(fits, index, level)
    level_ref[0] = level


def make_table(maps, most, part_cols, panel_blocks):
    size = table_layout(most, part_cols, panel_blocks)[-1]
    scalars = pl.BlockSpec(memory_space=pltpu.SMEM)
    return pl.pallas_call(
        functools.partial(table_kernel, most, part_cols, panel_blocks),
        in_specs=[scalars],
        out_specs=[scalars] * 2,
        out_shape=[
            jax.ShapeDtypeStruct((size,), jnp.int32), jax.ShapeDtypeStruct((1,), jnp.int32)
        ],
        scratch_shapes=[pltpu.SMEM((4,), jnp.int32)],
        name="tables",
    )(maps)


def crossing(caps):
    return caps[0] + 2 * caps[1] + caps[2]


def first_turn(caps):
    loads = {1: caps[0], 2: 2 * caps[1], 3: caps[2]}
    light = [turn for turn in loads if loads[turn] <= 6]
    heavy = [turn for turn in loads if loads[turn] >= 6]
    if crossing(caps) <= 22 and light:
        return max(light, key=loads.get)
    return min(heavy, key=loads.get)


def main_branch(level, most, row_count, front, updates, table):
    part_rows, blk, part_cols = front.shape[0], front.shape[2], front.shape[3]
    col_count = 4
    cols = range(col_count)

    def swap(value, mask):
        return lax.ppermute(value, "col", [(c, c ^ mask) for c in cols])

    def turned(value, turn):
        return lax.ppermute(value, "col", [(c, (c + turn) % col_count) for c in cols])

    place, square_base, where, _ = table_layout(most, part_cols, row_count)
    given, columns, early, units, late = send_head(table, front, updates, LEVELS[level], most, level + 1)
    bases = (place, square_base, where)
    soon = first_turn(LEVELS[level])
    turns = [turn for turn in range(1, col_count) if turn != soon]
    square, arrived, top = gather_square(
        table, bases, given, late[soon - 1], soon, front, columns, early, row_count,
        len(LEVELS) + level + 1,
    )
    top, square = lax.optimization_barrier((top, square))
    top = lax.all_gather(top, "row", axis=0, tiled=True)
    units, late, square = lax.optimization_barrier((units, late, square))
    chip, core = swap(units, 2), swap(units, 1)
    lower, inverse = factorize(square, blk)
    chip, core, inverse = lax.optimization_barrier((chip, core, inverse))
    both = swap(chip, 1)
    late = [turned(late[turn - 1], turn) for turn in turns]
    result, left = prepare(
        table, bases, front, updates, (units, chip, core, both), arrived, soon, inverse,
        row_count, col_count,
    )
    result, top = lax.optimization_barrier((result, top))
    result = trail(inverse, top, result, left, blk)
    result, late = lax.optimization_barrier((result, late))
    return add_last(table, bases, result, left, lower, late, turns, part_rows, part_cols, blk)


def body(row_count, col_count, front, updates, maps):
    part_rows = front.shape[0]
    if part_rows < 3 or row_count != NP * col_count or col_count != 4:
        return simple_body(front, updates, maps)
    front = front.reshape(front.shape[0], 1, *front.shape[2:4], front.shape[5])
    blk, part_cols = front.shape[2], front.shape[3]
    most = updates.shape[4]
    table, level = make_table(maps, most, part_cols, row_count)
    branches = [
        functools.partial(main_branch, level, most, row_count) for level in range(len(LEVELS))
    ]
    result = lax.switch(level[0], branches, front, updates, table)
    return result.reshape(part_rows, 1, blk, part_cols, 1, blk)


def solution(mesh):
    return jax.shard_map(
        functools.partial(body, mesh.shape["row"], mesh.shape["col"]),
        mesh=mesh,
        in_specs=(
            P(None, "row", None, None, "col", None),
            P(None, None, "row", None, None, "col", None),
            P(),
        ),
        out_specs=P(None, "row", None, None, "col", None),
        check_vma=False,
    )
```

```python
import functools

import jax
import jax.numpy as jnp
from jax import lax
from jax.experimental import pallas as pl
from jax.experimental.pallas import tpu as pltpu
from jax.sharding import PartitionSpec as P

NP = 2
highest = lax.Precision.HIGHEST
VMEM_LIMIT = 56 * 1024 * 1024
MESH = pl.DeviceIdType.MESH
SHARED = 5
LEVELS = (
    (10, 10, 5), (6, 8, 8), (10, 4, 10), (8, 5, 6),
    (12, 12, 12),
)


def split(value):
    high = value.astype(jnp.bfloat16)
    low = (value - high.astype(jnp.float32)).astype(jnp.bfloat16)
    return high, low


def dims(transposed):
    return (((1,), (1 if transposed else 0,)), ((), ()))


def product3(left_pair, right_pair, transposed=False):
    def one(a, b):
        return lax.dot_general(a, b, dims(transposed), preferred_element_type=jnp.float32)

    return (
        one(left_pair[0], right_pair[0])
        + one(left_pair[0], right_pair[1])
        + one(left_pair[1], right_pair[0])
    )


def product(a, b, transposed=False):
    return lax.dot_general(
        a, b, dims(transposed), precision=highest, preferred_element_type=jnp.float32
    )


def pack_kernel(child_cols, cap, blk, table, updates_ref, one_ref, two_ref, three_ref):
    for turn, out_ref in enumerate((one_ref, two_ref, three_ref)):
        for member in range(2):
            for slot in range(cap):
                source = table[(turn + 1) * 2 * cap + member * cap + slot]
                out_ref[member * cap + slot] = updates_ref[
                    member, 0, pl.ds(source, blk, stride=child_cols), :
                ]


def pack(table, updates, cap, begin, count):
    part_rows, blk, child_cols = updates.shape[1], updates.shape[3], updates.shape[4]
    flat = updates.reshape(2, part_rows, blk * child_cols, blk)
    return pl.pallas_call(
        functools.partial(pack_kernel, child_cols, cap, blk),
        grid_spec=pltpu.PrefetchScalarGridSpec(
            num_scalar_prefetch=1,
            grid=(count,),
            in_specs=[
                pl.BlockSpec((2, 1, blk * child_cols, blk), lambda a, t: (0, a + begin, 0, 0))
            ],
            out_specs=[pl.BlockSpec((2 * cap, blk, blk), lambda a, t: (0, a, 0))] * 3,
        ),
        out_shape=[jax.ShapeDtypeStruct((2 * cap, count * blk, blk), jnp.float32)] * 3,
        compiler_params=pltpu.CompilerParams(vmem_limit_bytes=VMEM_LIMIT),
        name="pack",
    )(table, flat)


def add_children(out_ref, table, front_ref, updates_ref, received, slots, part_cols, child_cols, blk):
    for slot in slots:
        cols = slice(slot * blk, (slot + 1) * blk)
        out_ref[:, cols] = front_ref[0, pl.ds(slot, blk, stride=part_cols), :]
        for member in range(2):
            turn = table[(member * part_cols + slot) * 2]
            index = table[(member * part_cols + slot) * 2 + 1]

            @pl.when(turn == 0)
            def _():
                out_ref[:, cols] += updates_ref[member, 0, pl.ds(index, blk, stride=child_cols), :]

            for step in range(3):

                @pl.when(turn == step + 1)
                def _():
                    out_ref[:, cols] += received[step][index]


def assemble(table, front, updates, received, begin, count, width):
    part_rows, blk, part_cols = front.shape[0], front.shape[2], front.shape[3]
    child_cols = updates.shape[4]
    slots = received[0].shape[0]

    def kernel(table, front_ref, updates_ref, one, two, three, out_ref):
        add_children(
            out_ref, table, front_ref, updates_ref, (one, two, three),
            range(width), part_cols, child_cols, blk,
        )

    return pl.pallas_call(
        kernel,
        grid_spec=pltpu.PrefetchScalarGridSpec(
            num_scalar_prefetch=1,
            grid=(count,),
            in_specs=[
                pl.BlockSpec((1, blk * part_cols, blk), lambda a, t: (a + begin, 0, 0)),
                pl.BlockSpec((2, 1, blk * child_cols, blk), lambda a, t: (0, a + begin, 0, 0)),
            ]
            + [pl.BlockSpec((slots, blk, blk), lambda a, t: (0, a, 0))] * 3,
            out_specs=pl.BlockSpec((blk, width * blk), lambda a, t: (a, 0)),
        ),
        out_shape=jax.ShapeDtypeStruct((count * blk, width * blk), jnp.float32),
        compiler_params=pltpu.CompilerParams(vmem_limit_bytes=VMEM_LIMIT),
        name="assemble",
    )(
        table,
        front.reshape(part_rows, blk * part_cols, blk),
        updates.reshape(2, part_rows, blk * child_cols, blk),
        *received,
    )


def eliminate(block):
    size = block.shape[0]
    group = 8
    tiles = size // group
    shape = (group, size)
    row_ids = lax.broadcasted_iota(jnp.int32, (size, size), 0)
    col_ids = lax.broadcasted_iota(jnp.int32, (size, size), 1)
    local = lax.broadcasted_iota(jnp.int32, shape, 0)
    start = (row_ids == col_ids).astype(jnp.float32)
    upper = [block[group * t : group * (t + 1), :] for t in range(tiles)]
    solved = [start[group * t : group * (t + 1), :] for t in range(tiles)]
    for h in range(tiles):
        def column(t, j):
            return jnp.broadcast_to(upper[t][:, group * h + j : group * h + j + 1], shape)
        home = [column(h, j) for j in range(group)]
        pivot = {
            (i, j): jnp.broadcast_to(home[j][i : i + 1, :], shape)
            for j in range(group) for i in range(j, group)
        }
        scale, ratio = [], {}
        for j in range(group):
            scale.append(1.0 / pivot[j, j])
            for i in range(j + 1, group):
                ratio[i, j] = pivot[i, j] * scale[j]
            for k in range(j + 1, group):
                for i in range(k, group):
                    pivot[i, k] = pivot[i, k] - ratio[i, j] * pivot[k, j]
        upper_rows, solved_rows = [], []
        for j in range(group):
            u = jnp.broadcast_to(upper[h][j : j + 1, :], shape)
            s = jnp.broadcast_to(solved[h][j : j + 1, :], shape)
            for i in range(j):
                u = u - ratio[j, i] * upper_rows[i]
                s = s - ratio[j, i] * solved_rows[i]
            upper_rows.append(u)
            solved_rows.append(s)
        for t in range(h, tiles):
            if t == h:
                u, s = upper_rows[0], solved_rows[0]
                for j in range(1, group):
                    u = jnp.where(local == j, upper_rows[j], u)
                    s = jnp.where(local == j, solved_rows[j], s)
                upper[t], solved[t] = u, s
                continue
            factors = []
            for j in range(group):
                c = column(t, j)
                for i in range(j):
                    c = c - factors[i] * pivot[j, i]
                factors.append(c * scale[j])
            for j in range(group):
                upper[t] = upper[t] - factors[j] * upper_rows[j]
                solved[t] = solved[t] - factors[j] * solved_rows[j]
    upper = jnp.concatenate(upper, axis=0)
    solved = jnp.concatenate(solved, axis=0)
    diagonal = jnp.sum(jnp.where(row_ids == col_ids, upper, 0.0), axis=1, keepdims=True)
    scale = 1.0 / jnp.sqrt(diagonal)
    lower = jnp.where(col_ids >= row_ids, upper * scale, 0.0).T
    return lower, solved * scale

def factor_kernel(blk, square_ref, lower_ref, inverse_ref, work):
    size = square_ref.shape[0]
    count = size // blk
    work[...] = square_ref[...]
    lower_ref[...] = jnp.zeros_like(lower_ref)
    inverse_ref[...] = jnp.zeros_like(inverse_ref)

    def spread(k, diag_inverse):
        begin, end = k * blk, (k + 1) * blk
        here = slice(begin, end)
        inverse_pair = split(diag_inverse)
        if k:
            done = product3(inverse_pair, split(inverse_ref[here, :begin]))
            inverse_ref[here, :begin] = done
        inverse_ref[here, here] = diag_inverse
        if end == size:
            return
        row_high, row_low = split(inverse_ref[here, :end])
        left_high, left_low = [], []
        for q in range(end, size, 256):
            top = min(q + 256, size)
            left = product3(split(work[q:top, here]), inverse_pair, True)
            lower_ref[q:top, here] = left
            high, low = split(left)
            left_high.append(high)
            left_low.append(low)
        high = jnp.concatenate(left_high, axis=0)
        low = jnp.concatenate(left_low, axis=0)
        for q in range(end, size, 256):
            top = min(q + 256, size)
            pair = high[q - end : top - end], low[q - end : top - end]
            below = high[: top - end], low[: top - end]
            work[q:top, end:top] -= product3(pair, below, True)
            inverse_ref[q:top, :end] -= product3(pair, (row_high, row_low))

    def step(k, carry):
        begin = pl.multiple_of(k * blk, blk)
        here = pl.ds(begin, blk)
        diag_lower, diag_inverse = eliminate(work[here, here])
        lower_ref[here, here] = diag_lower
        for t in range(count):
            pl.when(k == t)(functools.partial(spread, t, diag_inverse))
        return carry

    lax.fori_loop(0, count, step, 0)


def factorize(square, blk):
    size = square.shape[0]
    shape = jax.ShapeDtypeStruct((size, size), jnp.float32)
    return pl.pallas_call(
        functools.partial(factor_kernel, blk),
        out_shape=[shape, shape],
        scratch_shapes=[pltpu.VMEM((size, size), jnp.float32)],
        compiler_params=pltpu.CompilerParams(vmem_limit_bytes=VMEM_LIMIT),
        cost_estimate=pl.CostEstimate(flops=size, bytes_accessed=size, transcendentals=0),
        name="factorize",
    )(square)


def right_kernel(inverse_ref, top_ref, high_ref, low_ref, inv_high, inv_low):
    @pl.when(pl.program_id(0) == 0)
    def _():
        inv_high[...], inv_low[...] = split(inverse_ref[...])

    result = product3((inv_high[...], inv_low[...]), split(top_ref[...]))
    high_ref[...], low_ref[...] = split(result)


def right_side(inverse, top, tile):
    size, cols = top.shape
    out = jax.ShapeDtypeStruct((size, cols), jnp.bfloat16)
    return pl.pallas_call(
        right_kernel,
        grid=(cols // tile,),
        in_specs=[
            pl.BlockSpec((size, size), lambda n: (0, 0)),
            pl.BlockSpec((size, tile), lambda n: (0, n)),
        ],
        out_specs=[pl.BlockSpec((size, tile), lambda n: (0, n))] * 2,
        out_shape=[out, out],
        scratch_shapes=[pltpu.VMEM((size, size), jnp.bfloat16)] * 2,
        compiler_params=pltpu.CompilerParams(vmem_limit_bytes=VMEM_LIMIT),
        cost_estimate=pl.CostEstimate(flops=size, bytes_accessed=size, transcendentals=0),
        name="right",
    )(inverse, top)


def finish_kernel(
    part_cols, child_cols, blk, row_count, col_count, first, table, place,
    panel_ref, front_ref, updates_ref, one, two, three, inverse_ref, lower_ref, high_ref, low_ref,
    out_ref, inv_high, inv_low, left_ref, sum_ref,
):
    step = pl.program_id(0)
    block_row = step * row_count + place[0]
    panel_blocks = NP * col_count
    inside = block_row < panel_blocks
    columns = [pl.multiple_of((s * col_count + place[1]) * blk, blk) for s in range(NP)]

    @pl.when(step == 0)
    def _():
        inv_high[...], inv_low[...] = split(inverse_ref[...])

    @pl.when(jnp.logical_not(inside))
    def _():
        add_children(
            sum_ref, table, front_ref, updates_ref, (one, two, three),
            range(NP, part_cols), part_cols, child_cols, blk,
        )
        panel = jnp.concatenate(
            [
                panel_ref[c, :, s * blk : (s + 1) * blk]
                for s in range(NP)
                for c in range(col_count)
            ],
            axis=1,
        )
        left_ref[...] = product3(split(panel), (inv_high[...], inv_low[...]), True)
        left_pair = split(left_ref[...])
        for pair in range(NP, part_cols, 2):
            cols = slice((pair - NP) * blk, (pair - NP + 2) * blk)
            trailing = product3(left_pair, (high_ref[:, cols], low_ref[:, cols]))
            updated = sum_ref[:, pair * blk : (pair + 2) * blk] - trailing
            for half in range(2):
                out_ref[0, pl.ds(pair + half, blk, stride=part_cols), :] = updated[
                    :, half * blk : (half + 1) * blk
                ]
        for s in range(NP):
            out_ref[0, pl.ds(s, blk, stride=part_cols), :] = left_ref[:, pl.ds(columns[s], blk)]

    @pl.when(inside)
    def _():
        out_ref[...] = jnp.zeros_like(out_ref)
        begin = pl.multiple_of(block_row * blk, blk)
        for s in range(NP):
            out_ref[0, pl.ds(s, blk, stride=part_cols), :] = lower_ref[
                pl.ds(begin, blk), pl.ds(columns[s], blk)
            ]


def finish(table, place, panel, front, updates, received, inverse, lower, high, low, row_count, first):
    part_rows, blk, part_cols = front.shape[0], front.shape[2], front.shape[3]
    child_cols = updates.shape[4]
    size = inverse.shape[0]
    slots = received[0].shape[0]
    col_count = panel.shape[0]

    def resident(shape):
        return pl.BlockSpec(shape, lambda a, t, p: (0, 0), pipeline_mode=pl.Buffered(1))

    def late(a, t, p):
        return (0, jnp.maximum(a - first, 0), 0)

    return pl.pallas_call(
        functools.partial(finish_kernel, part_cols, child_cols, blk, row_count, col_count, first),
        grid_spec=pltpu.PrefetchScalarGridSpec(
            num_scalar_prefetch=2,
            grid=(part_rows,),
            in_specs=[
                pl.BlockSpec((col_count, blk, NP * blk), late),
                pl.BlockSpec((1, blk * part_cols, blk), lambda a, t, p: (a, 0, 0)),
                pl.BlockSpec((2, 1, blk * child_cols, blk), lambda a, t, p: (0, a, 0, 0)),
            ]
            + [pl.BlockSpec((slots, blk, blk), late)] * 3
            + [
                resident((size, size)),
                resident((size, size)),
                resident(high.shape),
                resident(low.shape),
            ],
            out_specs=pl.BlockSpec((1, blk * part_cols, blk), lambda a, t, p: (a, 0, 0)),
            scratch_shapes=[
                pltpu.VMEM((size, size), jnp.bfloat16),
                pltpu.VMEM((size, size), jnp.bfloat16),
                pltpu.VMEM((blk, size), jnp.float32),
                pltpu.VMEM((blk, part_cols * blk), jnp.float32),
            ],
        ),
        out_shape=jax.ShapeDtypeStruct((part_rows, blk * part_cols, blk), jnp.float32),
        compiler_params=pltpu.CompilerParams(vmem_limit_bytes=VMEM_LIMIT),
        name="finish",
    )(
        table, place, panel,
        front.reshape(part_rows, blk * part_cols, blk),
        updates.reshape(2, part_rows, blk * child_cols, blk),
        *received, inverse, lower, high, low,
    )


def tables(maps, col_index, col_count, child_cols, part_cols, cap):
    offsets = maps[:, ::col_count] - col_count * jnp.arange(child_cols, dtype=jnp.int32)[None, :]
    turn = offsets % col_count
    groups = jnp.arange(child_cols, dtype=jnp.int32)
    same = (turn[:, :, None] == turn[:, None, :]) & (groups[None, None, :] < groups[None, :, None])
    rank = jnp.sum(same.astype(jnp.int32), axis=2)
    turns = jnp.arange(col_count, dtype=jnp.int32)
    slots = jnp.arange(cap, dtype=jnp.int32)
    hot = (turn[None, :, None, :] == turns[:, None, None, None]) & (
        rank[None, :, None, :] == slots[None, None, :, None]
    )
    send = jnp.sum(jnp.where(hot, groups[None, None, None, :], 0), axis=3).reshape(-1)
    parents = jnp.arange(part_cols, dtype=jnp.int32) * col_count + col_index
    match = maps[:, None, :] == parents[None, :, None]
    spread = jnp.repeat(groups, col_count)
    group = jnp.sum(jnp.where(match, spread[None, None, :], 0), axis=2)
    present = jnp.any(match, axis=2)
    pick = group[:, :, None] == groups[None, None, :]
    kind = jnp.sum(jnp.where(pick, turn[:, None, :], 0), axis=2)
    order = jnp.sum(jnp.where(pick, rank[:, None, :], 0), axis=2)
    order = jnp.where(kind == 0, group, order + cap * jnp.arange(2, dtype=jnp.int32)[:, None])
    kind = jnp.where(present, kind, col_count)
    place = jnp.stack([kind, order], axis=2).reshape(-1)
    return send, place


def gather_top(piece, row_count, row_index, panel_blocks):
    if row_count == panel_blocks:
        return lax.all_gather(piece, "row", axis=0, tiled=True)
    ids = jnp.arange(panel_blocks, dtype=jnp.int32)
    kept = jnp.where((ids == row_index)[:, None, None], piece[None], 0.0)
    return lax.psum(kept, "row").reshape(panel_blocks * piece.shape[0], piece.shape[1])


def simple_body(front, updates, maps):
    row_count = lax.axis_size("row")
    col_count = lax.axis_size("col")
    row_index = lax.axis_index("row")
    col_index = lax.axis_index("col")
    front = front.reshape(front.shape[0], 1, *front.shape[2:4], front.shape[5])
    blk, part_cols = front.shape[2], front.shape[3]
    child_cols = updates.shape[4]
    cap = child_cols // 2
    panel_blocks = NP * col_count
    send, place = tables(maps, col_index, col_count, child_cols, part_cols, cap)
    part_rows = front.shape[0]
    first = 1 if part_rows > 1 and row_count == panel_blocks else part_rows

    def exchange(outgoing):
        return [
            lax.ppermute(
                outgoing[turn - 1], "col", [(c, (c + turn) % col_count) for c in range(col_count)]
            )
            for turn in range(1, col_count)
        ]

    early = exchange(pack(send, updates, cap, 0, first))
    if first < part_rows:
        outgoing = pack(send, updates, cap, first, part_rows - first)
        early, outgoing = lax.optimization_barrier((early, outgoing))
        received = exchange(outgoing)
    else:
        received = early
    head = assemble(place, front, updates, early, 0, 1, part_cols)
    square = jnp.concatenate(
        [
            lax.all_gather(head[:, s * blk : (s + 1) * blk], "col", axis=1, tiled=True)
            for s in range(NP)
        ],
        axis=1,
    )
    square = gather_top(square, row_count, row_index, panel_blocks)
    rest, square = lax.optimization_barrier((head[:, NP * blk :], square))
    top = gather_top(rest, row_count, row_index, panel_blocks)
    lower, inverse = factorize(square, blk)
    high, low = right_side(inverse, top, 2 * blk)
    received, high, low = lax.optimization_barrier((received, high, low))
    late = first if first < part_rows else 0
    panel = assemble(place, front, updates, received, late, part_rows - late, NP)
    panel = lax.all_gather(panel, "col", axis=0)
    where = jnp.stack([row_index, col_index]).astype(jnp.int32)
    result = finish(
        place, where, panel, front, updates, received, inverse, lower, high, low, row_count, late
    )
    return result.reshape(front.shape[0], 1, blk, part_cols, 1, blk)


def send_kernel(
    blk, caps, most, table, front_ref, updates_ref, units_ref, columns_ref,
    got_one, got_two, got_three, panel_ref, late_one, late_two, late_three,
    front_part, updates_part, columns, units, first, stage, stage_one, stage_two, stage_three,
    local, keep_sem, send, recv, out_sem,
):
    row, col = lax.axis_index("row"), lax.axis_index("col")
    part_rows = front_ref.shape[0]
    part_cols = front_part.shape[1] // blk
    child_cols = updates_part.shape[2] // blk
    width = units.shape[0]
    stages = (stage_one, stage_two, stage_three)

    def loads(a, side):
        copies = [pltpu.make_async_copy(front_ref.at[a], front_part.at[side], local.at[side, 0])]
        for member in range(2):
            copies.append(
                pltpu.make_async_copy(
                    updates_ref.at[member, a], updates_part.at[side, member],
                    local.at[side, 1 + member],
                )
            )
        return copies

    for load in loads(0, 0):
        load.start()
    for load in loads(1, 1):
        load.start()
    others = [lax.rem(col + turn, 4) for turn in range(1, 4)]
    barrier = pltpu.get_barrier_semaphore()
    for other in others:
        pl.semaphore_signal(barrier, inc=1, device_id=(row, other), device_id_type=MESH)

    def spread(side, target):
        def unpack(g, carry):
            for member in range(2):
                columns[member * child_cols + g] = updates_part[
                    side, member, pl.ds(g, blk, stride=child_cols), :
                ]
            return carry

        lax.fori_loop(0, child_cols, unpack, 0)
        for member in range(2):
            for g in range(2):
                target[member * 2 + g] = columns[member * child_cols + g]
        for s in range(NP):
            target[4 + s] = front_part[side, pl.ds(s, blk, stride=part_cols), :]

    def fill(target, turn):
        def put(slot, carry):
            target[slot] = columns[table[turn * most + slot]]
            return carry

        lax.fori_loop(0, caps[turn], put, 0)

    for load in loads(0, 0):
        load.wait()
    spread(0, units)
    pl.semaphore_wait(barrier, 3)

    def remote(source, target, index, device):
        return pltpu.make_async_remote_copy(
            src_ref=source, dst_ref=target, send_sem=send.at[index], recv_sem=recv.at[index],
            device_id=(row, device), device_id_type=MESH,
        )

    across = remote(units, units_ref.at[pl.ds(col * width, width)], 3, others[1])
    across.start()
    keep = [
        pltpu.make_async_copy(units, units_ref.at[pl.ds(col * width, width)], keep_sem.at[0]),
        pltpu.make_async_copy(columns, columns_ref, keep_sem.at[1]),
    ]
    for move in keep:
        move.start()
    other_core = col + 1 - 2 * lax.rem(col, 2)

    def beside(owner, index):
        section = units_ref.at[pl.ds(owner * width, width)]
        source = units if index == 4 else section
        return remote(source, section, index, other_core)

    mine = beside(col, 4)
    mine.start()
    moves = []
    begin = 0
    for turn, target in enumerate((got_one, got_two, got_three)):
        fill(first.at[pl.ds(begin, caps[turn])], turn)
        moves.append(remote(first.at[pl.ds(begin, caps[turn])], target, turn, others[turn]))
        moves[-1].start()
        begin += caps[turn]

    def stores(a, side):
        rows = pl.ds(pl.multiple_of((a - 1) * blk, blk), blk)
        copies = [pltpu.make_async_copy(stage.at[side], panel_ref.at[:, rows, :], out_sem.at[side, 0])]
        for turn, target in enumerate((late_one, late_two, late_three)):
            copies.append(
                pltpu.make_async_copy(
                    stages[turn].at[side], target.at[:, rows, :], out_sem.at[side, 1 + turn]
                )
            )
        return copies

    def step(a, carry):
        side = lax.rem(a, 2)
        for load in loads(a, side):
            load.wait()

        @pl.when(a + 1 < part_rows)
        def _():
            for load in loads(a + 1, 1 - side):
                load.start()

        @pl.when(a > 2)
        def _():
            for store in stores(a - 2, side):
                store.wait()

        spread(side, stage.at[side])
        for turn in range(3):
            fill(stages[turn].at[side], turn)
        for store in stores(a, side):
            store.start()
        return carry

    keep[1].wait()
    lax.fori_loop(1, part_rows, step, 0)
    for a in range(max(1, part_rows - 2), part_rows):
        for store in stores(a, a % 2):
            store.wait()
    keep[0].wait()
    across.wait_send()
    remote(units, units_ref.at[pl.ds(others[1] * width, width)], 3, others[1]).wait_recv()
    passed = beside(others[1], 5)
    passed.start()
    for index, owner in enumerate((other_core, lax.rem(other_core + 2, 4))):
        beside(owner, 4 + index).wait_recv()
    for move in (mine, passed):
        move.wait_send()
    for move in moves:
        move.wait()


def send_head(table, front, updates, caps, most, identity):
    part_rows, blk, part_cols = front.shape[0], front.shape[2], front.shape[3]
    child_cols = updates.shape[4]
    anywhere = pl.BlockSpec(memory_space=pl.ANY)
    width = 4 + NP
    rest = (part_rows - 1) * blk
    shapes = [(4 * width, blk, blk), (2 * child_cols, blk, blk)] + [(cap, blk, blk) for cap in caps]
    shapes += [(width, rest, blk)] + [(cap, rest, blk) for cap in caps]
    outs = pl.pallas_call(
        functools.partial(send_kernel, blk, caps, most),
        in_specs=[pl.BlockSpec(memory_space=pltpu.SMEM), anywhere, anywhere],
        out_specs=[anywhere] * 9,
        out_shape=[jax.ShapeDtypeStruct(shape, jnp.float32) for shape in shapes],
        scratch_shapes=[
            pltpu.VMEM((2, blk * part_cols, blk), jnp.float32),
            pltpu.VMEM((2, 2, blk * child_cols, blk), jnp.float32),
            pltpu.VMEM((2 * child_cols, blk, blk), jnp.float32),
            pltpu.VMEM((width, blk, blk), jnp.float32),
            pltpu.VMEM((sum(caps), blk, blk), jnp.float32),
            pltpu.VMEM((2, width, blk, blk), jnp.float32),
        ]
        + [pltpu.VMEM((2, cap, blk, blk), jnp.float32) for cap in caps]
        + [
            pltpu.SemaphoreType.DMA((2, 3)),
            pltpu.SemaphoreType.DMA((2,)),
            pltpu.SemaphoreType.DMA((6,)),
            pltpu.SemaphoreType.DMA((6,)),
            pltpu.SemaphoreType.DMA((2, 4)),
        ],
        compiler_params=pltpu.CompilerParams(
            vmem_limit_bytes=VMEM_LIMIT, collective_id=identity, has_side_effects=True
        ),
        cost_estimate=pl.CostEstimate(flops=blk, bytes_accessed=blk, transcendentals=0),
        name="send",
    )(
        table,
        front.reshape(part_rows, blk * part_cols, blk),
        updates.reshape(2, part_rows, blk * child_cols, blk),
    )
    return outs[0], outs[1], outs[2:5], outs[5], outs[6:]


def square_kernel(
    blk, row_count, turn, bases, table, given_ref, sent_ref, front_ref, columns_ref,
    early_one, early_two, early_three, square_ref, got_ref, top_ref,
    work, units, front_part, columns, one, two, three, top, local, line_send, line_recv, core_send, core_recv, turn_send, turn_recv,
):
    row, col = lax.axis_index("row"), lax.axis_index("col")
    width = units.shape[0] // 4
    half = row_count // 2
    core = lax.rem(col, 2)
    other_core = col + 1 - 2 * core
    other_chip = lax.rem(col + 2, 4)
    diagonal = lax.rem(other_core + 2, 4)

    part_cols = front_part.shape[0] // blk
    early = ((1, one), (2, two), (3, three))
    loads = [
        pltpu.make_async_copy(source, target, local.at[index])
        for index, (source, target) in enumerate(
            (
                (given_ref, units), (front_ref.at[0], front_part), (columns_ref, columns),
                (early_one, one), (early_two, two), (early_three, three),
            )
        )
    ]
    for load in loads:
        load.start()

    def ring_row(position):
        position = lax.rem(position + row_count, row_count)
        return jnp.where(position < half, 2 * position, 2 * (row_count - position) - 1)

    place = jnp.where(lax.rem(row, 2) == 0, row // 2, row_count - 1 - row // 2)
    right, left = ring_row(place + 1), ring_row(place - 1)
    barrier = pltpu.get_barrier_semaphore()
    for device in (
        (row, other_core), (row, other_chip), (row, diagonal), (right, col), (left, col)
    ):
        pl.semaphore_signal(barrier, inc=1, device_id=device, device_id_type=MESH)
    for load in loads:
        load.wait()
    pl.semaphore_wait(barrier, 5)
    turned = pltpu.make_async_remote_copy(
        src_ref=sent_ref, dst_ref=got_ref, send_sem=turn_send, recv_sem=turn_recv,
        device_id=(row, lax.rem(col + turn, 4)), device_id_type=MESH,
    )
    turned.start()

    here = pl.multiple_of(row * blk, blk)
    for q in range(row_count):
        s, owner = q // 4, q % 4
        total = units[owner * width + 4 + s]
        for member in range(2):
            entry = bases[1] + 2 * (member * row_count + q)
            total = total + units[table[entry]] * table[entry + 1].astype(jnp.float32)
        work[pl.ds(here, blk), q * blk : (q + 1) * blk] = total

    cols = work.shape[1] // 2

    def part(position, side):
        begin = pl.multiple_of(ring_row(position) * blk, blk)
        return work.at[pl.ds(begin, blk), pl.ds(pl.multiple_of(side * cols, cols), cols)]

    def copy(ref, device, send, recv):
        return pltpu.make_async_remote_copy(
            src_ref=ref, dst_ref=ref, send_sem=send, recv_sem=recv,
            device_id=device, device_id_type=MESH,
        )

    pending = []
    for step in range(half):
        ways = range(2 if step < half - 1 else 1)
        for way in ways:
            position = place - step if way == 0 else place + step
            target = right if way == 0 else left
            move = copy(
                part(position, core), (target, col), line_send.at[way, step], line_recv.at[way, step]
            )
            move.start()
            pending.append(move)
        for slot in range(NP + step, part_cols, half):
            top[:, (slot - NP) * blk : (slot - NP + 1) * blk] = child_sum(
                front_part[pl.ds(slot, blk, stride=part_cols), :],
                table, bases[0], slot, part_cols, columns, early, units,
            )
        for way in ways:
            origin = place - step - 1 if way == 0 else place + step + 1
            landed = part(origin, core)
            copy(
                landed, (right, col), line_send.at[way, step], line_recv.at[way, step]
            ).wait_recv()
            forward = copy(
                landed, (row, other_core), core_send.at[way, step], core_recv.at[way, step]
            )
            forward.start()
            pending.append(forward)
    for way in range(2):
        for step in range(half - way):
            origin = place - step - 1 if way == 0 else place + step + 1
            copy(
                part(origin, 1 - core), (row, other_core),
                core_send.at[way, step], core_recv.at[way, step],
            ).wait_recv()
    stores = [
        pltpu.make_async_copy(work, square_ref, local.at[0]),
        pltpu.make_async_copy(top, top_ref, local.at[1]),
    ]
    for store in stores:
        store.start()
    for move in pending:
        move.wait_send()
    for store in stores:
        store.wait()
    turned.wait()


def gather_square(table, bases, given, sent, turn, front, columns, early, row_count, identity):
    part_rows, blk, part_cols = front.shape[0], front.shape[2], front.shape[3]
    size = row_count * blk
    half = row_count // 2
    anywhere = pl.BlockSpec(memory_space=pl.ANY)
    top = jax.ShapeDtypeStruct((blk, (part_cols - NP) * blk), jnp.float32)
    return pl.pallas_call(
        functools.partial(square_kernel, blk, row_count, turn, bases),
        in_specs=[pl.BlockSpec(memory_space=pltpu.SMEM)] + [anywhere] * 7,
        out_specs=[anywhere] * 3,
        out_shape=[
            jax.ShapeDtypeStruct((size, size), jnp.float32),
            jax.ShapeDtypeStruct(sent.shape, jnp.float32),
            top,
        ],
        scratch_shapes=[
            pltpu.VMEM((size, size), jnp.float32),
            pltpu.VMEM(given.shape, jnp.float32),
            pltpu.VMEM((blk * part_cols, blk), jnp.float32),
            pltpu.VMEM(columns.shape, jnp.float32),
        ]
        + [pltpu.VMEM(e.shape, jnp.float32) for e in early]
        + [
            pltpu.VMEM(top.shape, jnp.float32),
            pltpu.SemaphoreType.DMA((6,)),
            pltpu.SemaphoreType.DMA((2, half)),
            pltpu.SemaphoreType.DMA((2, half)),
            pltpu.SemaphoreType.DMA((2, half)),
            pltpu.SemaphoreType.DMA((2, half)),
            pltpu.SemaphoreType.DMA,
            pltpu.SemaphoreType.DMA,
        ],
        compiler_params=pltpu.CompilerParams(
            vmem_limit_bytes=VMEM_LIMIT, collective_id=identity, has_side_effects=True
        ),
        cost_estimate=pl.CostEstimate(flops=size, bytes_accessed=size, transcendentals=0),
        name="square",
    )(table, given, sent, front.reshape(part_rows, blk * part_cols, blk), columns, *early)


def pick(kind, index, wanted):
    hit = kind == wanted
    return jnp.where(hit, index, 0), hit.astype(jnp.float32)


def child_sum(total, table, base, slot, part_cols, columns, received, shared):
    for member in range(2):
        entry = base + (member * part_cols + slot) * 2
        kind, index = table[entry], table[entry + 1]
        if columns is not None:
            at, weight = pick(kind, index, 0)
            total = total + weight * columns[member * (columns.shape[0] // 2) + at]
        if shared is not None:
            at, weight = pick(kind, index, SHARED)
            total = total + weight * shared[at]
        for turn, ref in received:
            at, weight = pick(kind, index, turn)
            total = total + weight * ref[at]
    return total


def prepare_kernel(
    part_cols, child_cols, blk, row_count, col_count, bases, soon, table,
    front_ref, updates_ref, own, chip, core, both, arrived, inverse_ref,
    sum_ref, left_ref, inv_high, inv_low, units, panel_ref,
):
    place_base, square_base, where = bases
    size = inverse_ref.shape[0]

    @pl.when(pl.program_id(0) == 0)
    def _():
        inv_high[...], inv_low[...] = split(inverse_ref[...])

    width = own.shape[0]
    for order, ref in enumerate((own, chip, core, both)):
        owner = table[where + 1 + order]
        for i in range(width):
            units[owner * width + i] = ref[i]
    for q in range(row_count):
        total = units[(q % col_count) * width + 4 + q // col_count]
        for member in range(2):
            entry = square_base + 2 * (member * row_count + q)
            total = total + units[table[entry]] * table[entry + 1].astype(jnp.float32)
        panel_ref[:, q * blk : (q + 1) * blk] = total
    for slot in range(NP, part_cols):
        cols = slice((slot - NP) * blk, (slot - NP + 1) * blk)
        sum_ref[:, cols] = child_sum(
            front_ref[0, pl.ds(slot, blk, stride=part_cols), :],
            table, place_base, slot, part_cols, None, ((soon, arrived),), units,
        )
    for slot in range(NP, part_cols):
        cols = slice((slot - NP) * blk, (slot - NP + 1) * blk)
        for member in range(2):
            entry = place_base + (member * part_cols + slot) * 2

            @pl.when(table[entry] == 0)
            def _():
                sum_ref[:, cols] += updates_ref[
                    member, 0, pl.ds(table[entry + 1], blk, stride=child_cols), :
                ]

    panel_pair = split(panel_ref[...])
    for begin in range(0, size, 2 * blk):
        end = begin + 2 * blk
        left_ref[:, begin:end] = product3(
            tuple(p[:, :end] for p in panel_pair),
            (inv_high[begin:end, :end], inv_low[begin:end, :end]),
            True,
        )


def prepare(table, bases, front, updates, gathered, arrived, soon, inverse, row_count, col_count):
    part_rows, blk, part_cols = front.shape[0], front.shape[2], front.shape[3]
    child_cols = updates.shape[4]
    size = inverse.shape[0]
    rows, width = (part_rows - 1) * blk, (part_cols - NP) * blk
    return pl.pallas_call(
        functools.partial(
            prepare_kernel, part_cols, child_cols, blk, row_count, col_count, bases, soon
        ),
        grid_spec=pltpu.PrefetchScalarGridSpec(
            num_scalar_prefetch=1,
            grid=(part_rows - 1,),
            in_specs=[
                pl.BlockSpec((1, blk * part_cols, blk), lambda a, t: (a + 1, 0, 0)),
                pl.BlockSpec((2, 1, blk * child_cols, blk), lambda a, t: (0, a + 1, 0, 0)),
            ]
            + [pl.BlockSpec((g.shape[0], blk, blk), lambda a, t: (0, a, 0)) for g in (*gathered, arrived)]
            + [pl.BlockSpec((size, size), lambda a, t: (0, 0), pipeline_mode=pl.Buffered(1))],
            out_specs=[
                pl.BlockSpec((blk, width), lambda a, t: (a, 0)),
                pl.BlockSpec((blk, size), lambda a, t: (a, 0)),
            ],
            scratch_shapes=[
                pltpu.VMEM((size, size), jnp.bfloat16),
                pltpu.VMEM((size, size), jnp.bfloat16),
                pltpu.VMEM((4 * (4 + NP), blk, blk), jnp.float32),
                pltpu.VMEM((blk, size), jnp.float32),
            ],
        ),
        out_shape=[
            jax.ShapeDtypeStruct((rows, width), jnp.float32),
            jax.ShapeDtypeStruct((rows, size), jnp.float32),
        ],
        compiler_params=pltpu.CompilerParams(vmem_limit_bytes=VMEM_LIMIT),
        cost_estimate=pl.CostEstimate(flops=blk, bytes_accessed=blk, transcendentals=0),
        name="prepare",
    )(
        table,
        front.reshape(part_rows, blk * part_cols, blk),
        updates.reshape(2, part_rows, blk * child_cols, blk),
        *gathered, arrived, inverse,
    )


def trail_kernel(parts, inverse_ref, top_ref, given_ref, left_ref, out_ref, inv_high, inv_low, high, low):
    step = pl.program_id(0)
    size = inverse_ref.shape[0]
    width = top_ref.shape[1]

    @pl.when(step == 0)
    def _():
        inv_high[...], inv_low[...] = split(inverse_ref[...])

    @pl.when(step < parts)
    def _():
        here = pl.ds(pl.multiple_of(step * width, width), width)
        top_high, top_low = split(top_ref[...])
        for begin in range(0, size, 256):
            end = begin + 256
            result = product3(
                (inv_high[begin:end, :end], inv_low[begin:end, :end]),
                (top_high[:end], top_low[:end]),
            )
            high[begin:end, here], low[begin:end, here] = split(result)

    @pl.when(step >= parts)
    def _():
        left_pair = split(left_ref[...])
        for begin in range(0, given_ref.shape[1], 256):
            cols = slice(begin, begin + 256)
            trailing = product3(left_pair, (high[:, cols], low[:, cols]))
            out_ref[:, cols] = given_ref[:, cols] - trailing


def trail(inverse, top, given, left, blk):
    size, cols = top.shape
    width = 2 * blk
    parts = cols // width

    def late(a):
        return (jnp.maximum(a - parts, 0), 0)

    return pl.pallas_call(
        functools.partial(trail_kernel, parts),
        grid=(parts + given.shape[0] // blk,),
        in_specs=[
            pl.BlockSpec((size, size), lambda a: (0, 0), pipeline_mode=pl.Buffered(1)),
            pl.BlockSpec((size, width), lambda a: (0, jnp.minimum(a, parts - 1))),
            pl.BlockSpec((blk, cols), late),
            pl.BlockSpec((blk, size), late),
        ],
        out_specs=pl.BlockSpec((blk, cols), late),
        out_shape=jax.ShapeDtypeStruct(given.shape, given.dtype),
        scratch_shapes=[pltpu.VMEM((size, size), jnp.bfloat16)] * 2
        + [pltpu.VMEM((size, cols), jnp.bfloat16)] * 2,
        compiler_params=pltpu.CompilerParams(vmem_limit_bytes=VMEM_LIMIT),
        cost_estimate=pl.CostEstimate(flops=blk, bytes_accessed=blk, transcendentals=0),
        name="trail",
    )(inverse, top, given, left)


def add_last_kernel(part_cols, blk, base, turns, table, given_ref, *refs):
    lefts, lowers, out_ref = refs[:NP], refs[NP : 2 * NP], refs[-1]
    received = list(zip(turns, refs[2 * NP : -1]))
    step = pl.program_id(0)

    @pl.when(step == 0)
    def _():
        out_ref[...] = jnp.zeros_like(out_ref)
        for s in range(NP):
            out_ref[0, pl.ds(s, blk, stride=part_cols), :] = lowers[s][...]

    @pl.when(step > 0)
    def _():
        for s in range(NP):
            out_ref[0, pl.ds(s, blk, stride=part_cols), :] = lefts[s][...]
        for slot in range(NP, part_cols):
            total = given_ref[:, (slot - NP) * blk : (slot - NP + 1) * blk]
            out_ref[0, pl.ds(slot, blk, stride=part_cols), :] = child_sum(
                total, table, base, slot, part_cols, None, received, None
            )


def add_last(table, bases, given, left, lower, received, turns, part_rows, part_cols, blk):
    place_base, _, where = bases

    def late(a):
        return jnp.maximum(a - 1, 0)

    def left_spec(s):
        return pl.BlockSpec((blk, blk), lambda a, t: (late(a), s * 4 + t[where + 1]))

    def lower_spec(s):
        return pl.BlockSpec((blk, blk), lambda a, t: (t[where], s * 4 + t[where + 1]))

    return pl.pallas_call(
        functools.partial(add_last_kernel, part_cols, blk, place_base, turns),
        grid_spec=pltpu.PrefetchScalarGridSpec(
            num_scalar_prefetch=1,
            grid=(part_rows,),
            in_specs=[pl.BlockSpec((blk, given.shape[1]), lambda a, t: (late(a), 0))]
            + [left_spec(s) for s in range(NP)]
            + [lower_spec(s) for s in range(NP)]
            + [pl.BlockSpec((r.shape[0], blk, blk), lambda a, t: (0, late(a), 0)) for r in received],
            out_specs=pl.BlockSpec((1, blk * part_cols, blk), lambda a, t: (a, 0, 0)),
        ),
        out_shape=jax.ShapeDtypeStruct((part_rows, blk * part_cols, blk), given.dtype),
        compiler_params=pltpu.CompilerParams(vmem_limit_bytes=VMEM_LIMIT),
        cost_estimate=pl.CostEstimate(flops=blk, bytes_accessed=blk, transcendentals=0),
        name="add_last",
    )(table, given, *[left] * NP, *[lower] * NP, *received)


def table_layout(most, part_cols, panel_blocks):
    place = 3 * most
    square = place + 4 * part_cols
    where = square + 4 * panel_blocks
    return place, square, where, where + 8


def table_kernel(most, part_cols, panel_blocks, maps_ref, table, level_ref, ranks):
    place, square, where, size = table_layout(most, part_cols, panel_blocks)
    child_cols = maps_ref.shape[1] // 4
    row, col = lax.axis_index("row"), lax.axis_index("col")
    for i in range(size):
        table[i] = 0
    for i in range(2 * part_cols):
        table[place + 2 * i] = 4
    for i in range(4):
        ranks[i] = 0
    for g in range(child_cols):
        for member in range(2):
            turn = (maps_ref[member, 4 * g] - 4 * g) & 3
            slot = maps_ref[member, 4 * g + ((col - turn) & 3)] // 4
            entry = place + 2 * (member * part_cols + slot)
            if g < 2:
                unit = 2 * member + g
                table[entry] = jnp.where(turn == 0, 0, SHARED)
                table[entry + 1] = jnp.where(
                    turn == 0, g, ((col - turn) & 3) * (4 + NP) + unit
                )
                for j in range(4):
                    parent = maps_ref[member, 4 * g + j]

                    @pl.when(parent < panel_blocks)
                    def _():
                        table[square + 2 * (member * panel_blocks + parent)] = j * (4 + NP) + unit
                        table[square + 2 * (member * panel_blocks + parent) + 1] = 1

            else:
                rank = ranks[turn]
                ranks[turn] = rank + 1
                table[entry] = turn
                table[entry + 1] = jnp.where(turn == 0, g, rank)

                @pl.when(turn > 0)
                def _():
                    table[(turn - 1) * most + rank] = member * child_cols + g

    table[where] = row
    for i, mask in enumerate((0, 2, 1, 3)):
        table[where + 1 + i] = col ^ mask
    order = sorted(range(len(LEVELS)), key=lambda index: crossing(LEVELS[index]))
    level = jnp.int32(order[-1])
    for index in reversed(order[:-1]):
        one, two, three = LEVELS[index]
        fits = (ranks[1] <= one) & (ranks[2] <= two) & (ranks[3] <= three)
        level = jnp.where(fits, index, level)
    level_ref[0] = level


def make_table(maps, most, part_cols, panel_blocks):
    size = table_layout(most, part_cols, panel_blocks)[-1]
    scalars = pl.BlockSpec(memory_space=pltpu.SMEM)
    return pl.pallas_call(
        functools.partial(table_kernel, most, part_cols, panel_blocks),
        in_specs=[scalars],
        out_specs=[scalars] * 2,
        out_shape=[
            jax.ShapeDtypeStruct((size,), jnp.int32), jax.ShapeDtypeStruct((1,), jnp.int32)
        ],
        scratch_shapes=[pltpu.SMEM((4,), jnp.int32)],
        name="tables",
    )(maps)


def crossing(caps):
    return caps[0] + 2 * caps[1] + caps[2]


def first_turn(caps):
    loads = {1: caps[0], 2: 2 * caps[1], 3: caps[2]}
    light = [turn for turn in loads if loads[turn] <= 6]
    heavy = [turn for turn in loads if loads[turn] >= (8 if crossing(caps) > 24 else 6)]
    if crossing(caps) <= 22 and light:
        return max(light, key=loads.get)
    return min(heavy, key=loads.get)


def main_branch(level, most, row_count, front, updates, table):
    part_rows, blk, part_cols = front.shape[0], front.shape[2], front.shape[3]
    col_count = 4
    cols = range(col_count)

    def swap(value, mask):
        return lax.ppermute(value, "col", [(c, c ^ mask) for c in cols])

    def turned(value, turn):
        return lax.ppermute(value, "col", [(c, (c + turn) % col_count) for c in cols])

    place, square_base, where, _ = table_layout(most, part_cols, row_count)
    given, columns, early, units, late = send_head(table, front, updates, LEVELS[level], most, level + 1)
    bases = (place, square_base, where)
    soon = first_turn(LEVELS[level])
    turns = [turn for turn in range(1, col_count) if turn != soon]
    square, arrived, top = gather_square(
        table, bases, given, late[soon - 1], soon, front, columns, early, row_count,
        len(LEVELS) + level + 1,
    )
    top, square = lax.optimization_barrier((top, square))
    top = lax.all_gather(top, "row", axis=0, tiled=True)
    units, late, square = lax.optimization_barrier((units, late, square))
    chip, core = swap(units, 2), swap(units, 1)
    lower, inverse = factorize(square, blk)
    chip, core, inverse = lax.optimization_barrier((chip, core, inverse))
    both = swap(chip, 1)
    late = [turned(late[turn - 1], turn) for turn in turns]
    result, left = prepare(
        table, bases, front, updates, (units, chip, core, both), arrived, soon, inverse,
        row_count, col_count,
    )
    result, top = lax.optimization_barrier((result, top))
    result = trail(inverse, top, result, left, blk)
    result, late = lax.optimization_barrier((result, late))
    return add_last(table, bases, result, left, lower, late, turns, part_rows, part_cols, blk)


def body(row_count, col_count, front, updates, maps):
    part_rows = front.shape[0]
    if part_rows < 3 or row_count != NP * col_count or col_count != 4:
        return simple_body(front, updates, maps)
    front = front.reshape(front.shape[0], 1, *front.shape[2:4], front.shape[5])
    blk, part_cols = front.shape[2], front.shape[3]
    most = updates.shape[4]
    table, level = make_table(maps, most, part_cols, row_count)
    branches = [
        functools.partial(main_branch, level, most, row_count) for level in range(len(LEVELS))
    ]
    result = lax.switch(level[0], branches, front, updates, table)
    return result.reshape(part_rows, 1, blk, part_cols, 1, blk)


def solution(mesh):
    return jax.shard_map(
        functools.partial(body, mesh.shape["row"], mesh.shape["col"]),
        mesh=mesh,
        in_specs=(
            P(None, "row", None, None, "col", None),
            P(None, None, "row", None, None, "col", None),
            P(),
        ),
        out_specs=P(None, "row", None, None, "col", None),
        check_vma=False,
    )
```
